32 devices in a mesh: cols: 16 (over z, y, core), fsdp: 2 (over x).
Axes of the slice: x: 2, y: 2, z: 4, core: 2. Of those that a mesh axis runs over, the one named last changes fastest.
Arguments:
- alignment: bfloat16 [2, 2, 4, 1024, 768], P(None, 'fsdp', None, 'cols'), may hold values from -6 to 6
- cotangent: bfloat16 [2, 2, 4, 1024, 768], P(None, 'fsdp', None, 'cols'), may hold values from -6 to 6
- row_counts: int32 [2, 2], P(None, 'fsdp'), may hold values from 1 to 4, as said below
- band_reach: int32 [2, 2, 2, 1024], P(None, 'fsdp', None, 'cols'), may hold values from 0 to 32
- master_weights: float32 [12288, 768], P(('cols', 'fsdp'))
- weight_moment: float32 [12288, 768], P(('cols', 'fsdp'))
- weight_square: float32 [12288, 768], P(('cols', 'fsdp')), as said below
- norm_gains: float32 [2304], P(('cols', 'fsdp')), may hold values from 0.5 to 1.5
- gain_moment: float32 [2304], P(('cols', 'fsdp'))
- gain_square: float32 [2304], P(('cols', 'fsdp')), as said below
Outputs:
- block_output: bfloat16 [2, 2, 4, 1024, 768], P(None, 'fsdp', None, 'cols')
- input_grad: bfloat16 [2, 2, 4, 1024, 768], P(None, 'fsdp', None, 'cols')
- new_weights: float32 [12288, 768], P(('cols', 'fsdp'))
- new_moment: float32 [12288, 768], P(('cols', 'fsdp'))
- new_square: float32 [12288, 768], P(('cols', 'fsdp'))
- weight_copies: bfloat16 [12288, 768], P(('cols', 'fsdp'))
- new_gains: float32 [2304], P(('cols', 'fsdp'))
- new_gain_moment: float32 [2304], P(('cols', 'fsdp'))
- new_gain_square: float32 [2304], P(('cols', 'fsdp'))
The draws below stay inside these ranges and needn't reach their ends.
Inputs may be any that keep to these rules, and one draw needn't show every extreme that they name: `row_counts`: every alignment holds at least one live sequence. `weight_square`: positive. `gain_square`: positive.
All inputs are finite; a program needn't handle non-finite values.
Results may differ from the reference program's by a relative error of at most 0.017.
Values may be sent and summed in bfloat16 or wider, within the bound.
No kernel may reach another device: no remote copies, remote signals or barrier semaphores. Data moves between devices by JAX's collectives and lax.ppermute only.
A program may use at most 240 MiB of HBM per device.

```python
import math
import jax
import jax.numpy as jnp
from jax import lax

D = 768
H = 12
DH = 64
FF = 3072
NMAT = 16
ROWS = 4
CB = 64
HALO = 32
MB = 2
GROUPS = 2
COLS = 1024
TOKENS_ALL = 16384


def matrix_factors():
    fold_count = FF // D
    row_out = math.sqrt(HALO + 1.0)
    col_out = math.sqrt(max(1.0, ROWS / 2.0))
    down_out = 1.5 * math.sqrt(D / FF)
    return jnp.array([1.0, 1.0, 1.0, row_out, 1.0, 1.0, 1.0, col_out] + [1.0] * fold_count + [down_out] * fold_count, jnp.float32)


def grad_factors():
    fold_count = FF // D
    return jnp.array([0.5, 0.5, 1.0, 0.5, 0.5, 0.5, 1.0, 0.5] + [0.5] * fold_count + [0.6] * fold_count, jnp.float32)


def grad_scale():
    return math.sqrt(TOKENS_ALL / 2.0)


def draw_row_counts(key, part):
    key_shift = jax.random.fold_in(key, 11)
    key_spot = jax.random.fold_in(key, 12)
    shifts = jax.random.randint(key_shift, (MB * GROUPS,), 0, 3)
    counts = jnp.maximum(jnp.right_shift(jnp.full((MB * GROUPS,), ROWS, jnp.int32), shifts), 1)
    spot_index = jax.random.randint(key_spot, (), 0, MB * GROUPS)
    counts = counts.at[spot_index].set(ROWS)
    return counts.reshape(MB, GROUPS)


def draw_band_reach(key, part):
    key_reach = jax.random.fold_in(key, 21)
    key_spot = jax.random.fold_in(key, 22)
    cell_count = MB * GROUPS * 2 * COLS
    reaches = jax.random.randint(key_reach, (cell_count,), 0, HALO + 1)
    spot_index = jax.random.randint(key_spot, (), 0, cell_count)
    reaches = reaches.at[spot_index].set(HALO)
    return reaches.reshape(MB, GROUPS, 2, COLS)


def draw_master_weights(key, part):
    normal = jax.random.normal(key, (NMAT, D, D), jnp.float32)
    return (normal * matrix_factors()[:, None, None] * D ** (-0.5)).reshape(NMAT * D, D)


def draw_weight_moment(key, part):
    normal = jax.random.normal(key, (NMAT, D, D), jnp.float32)
    sizes_grad = grad_factors()[:, None, None] * grad_scale()
    return (normal * sizes_grad * (0.1 / 0.9)).reshape(NMAT * D, D)


def draw_weight_square(key, part):
    factor = jax.random.uniform(key, (NMAT, D, D), jnp.float32, 0.0, math.log(4.0))
    sizes_grad = grad_factors()[:, None, None] * grad_scale()
    return (jnp.exp(factor) * sizes_grad * sizes_grad * (0.001 / 0.999)).reshape(NMAT * D, D)


def draw_gain_moment(key, part):
    normal = jax.random.normal(key, (3 * D,), jnp.float32)
    return normal * 2.0 * grad_scale() * (0.1 / 0.9)


def draw_gain_square(key, part):
    factor = jax.random.uniform(key, (3 * D,), jnp.float32, 0.0, math.log(4.0))
    sizes_grad = 2.0 * grad_scale()
    return jnp.exp(factor) * sizes_grad * sizes_grad * (0.001 / 0.999)


def block_scale(key, shape, pieces, least, high):
    loudness, own = 1.0, jax.random.fold_in(key, 6)
    for position, blocks in pieces:
        steps = jnp.exp(jax.random.uniform(jax.random.fold_in(own, position), (blocks,), jnp.float32, least / len(pieces), high / len(pieces)))
        loudness = loudness * jnp.repeat(steps, shape[position] // blocks).reshape([-1 if axis == position else 1 for axis in range(len(shape))])
    return loudness


def bell_draw(rng, shape, deviation, limit, split=(), held_as=jnp.bfloat16):
    factor_of = block_scale(rng, shape, split, -0.22, 0.18) if split else 1.0
    values = jax.random.normal(rng, shape, jnp.float32) * deviation * factor_of
    return jnp.minimum(jnp.maximum(values, -limit), limit).astype(held_as)


def setup_inputs(seed: int = 0) -> dict:
    arg_keys = jax.random.split(jax.random.key(seed), 11)
    alignment = bell_draw(arg_keys[0], (MB, GROUPS, ROWS, COLS, D), 1.0, 6.0, ((1, 2), (3, 16)))
    cotangent = bell_draw(arg_keys[1], (MB, GROUPS, ROWS, COLS, D), 1.0, 6.0, ((1, 2), (3, 16)))
    row_counts = draw_row_counts(jax.random.fold_in(arg_keys[10], 71), 0)
    band_reach = draw_band_reach(jax.random.fold_in(arg_keys[10], 71), 0)
    master_weights = draw_master_weights(jax.random.fold_in(arg_keys[10], 71), 0)
    weight_moment = draw_weight_moment(jax.random.fold_in(arg_keys[10], 71), 0)
    weight_square = draw_weight_square(jax.random.fold_in(arg_keys[10], 71), 0)
    norm_gains = jnp.clip(1.0 + 0.1 * jax.random.normal(arg_keys[7], (3 * D,), jnp.float32), 0.5, 1.5)
    gain_moment = draw_gain_moment(jax.random.fold_in(arg_keys[10], 71), 0)
    gain_square = draw_gain_square(jax.random.fold_in(arg_keys[10], 71), 0)
    return {"alignment": alignment, "cotangent": cotangent, "row_counts": row_counts, "band_reach": band_reach, "master_weights": master_weights, "weight_moment": weight_moment, "weight_square": weight_square, "norm_gains": norm_gains, "gain_moment": gain_moment, "gain_square": gain_square}


EPS = 1e-05
BETA_ONE = 0.9
BETA_TWO = 0.999
ADAM_EPS = 1e-08
DECAY = 0.01
RATE_GAIN = 0.3
STEP_NUMBER = 10.0
MASKED = -1e+30
HIGHEST = lax.Precision.HIGHEST

@jax.custom_vjp
def low(v):
    return lax.optimization_barrier(v.astype(jnp.bfloat16)).astype(jnp.float32)

@jax.custom_vjp
def low_back(v):
    return v

def low_keep(v):
    return (low(v), None)

def low_pass(kept, grad):
    return (grad,)

def back_keep(v):
    return (v, None)

def back_low(kept, grad):
    return (low(grad),)
low.defvjp(low_keep, low_pass)
low_back.defvjp(back_keep, back_low)

def both_ways(values):
    return low_back(low(values))

def layer_norm(values, norm_gain):
    center = values - lax.optimization_barrier(jnp.mean(values, axis=-1, keepdims=True))
    return center * lax.rsqrt(lax.optimization_barrier(jnp.mean(center * center, axis=-1, keepdims=True)) + EPS) * norm_gain

def project(layer_activations, matrix):
    return jnp.einsum('rcd,de->rce', layer_activations, matrix, precision=HIGHEST)

def row_attention(queries, keys, values, present_count, lower_reach, upper_reach):
    row_scale = DH ** (-0.5) * lax.rsqrt(present_count)
    extent = CB + 2 * HALO
    padded_keys = jnp.pad(keys, ((0, 0), (HALO, HALO), (0, 0)))
    padded_values = jnp.pad(values, ((0, 0), (HALO, HALO), (0, 0)))

    def one_block(start):
        query_block = lax.dynamic_slice_in_dim(queries, start, CB, 1).reshape(ROWS, CB, H, DH)
        key_block = lax.dynamic_slice_in_dim(padded_keys, start, extent, 1).reshape(ROWS, extent, H, DH)
        value_block = lax.dynamic_slice_in_dim(padded_values, start, extent, 1).reshape(ROWS, extent, H, DH)
        scores = low_back(jnp.einsum('rchd,rkhd->hck', query_block, key_block, precision=HIGHEST) * row_scale)
        query_pos = start + jnp.arange(CB, dtype=jnp.int32)
        key_pos = start - HALO + jnp.arange(extent, dtype=jnp.int32)
        lowest = query_pos - lax.dynamic_slice_in_dim(lower_reach, start, CB, 0)
        highest = query_pos + lax.dynamic_slice_in_dim(upper_reach, start, CB, 0)
        allowed = (key_pos[None, :] >= lowest[:, None]) & (key_pos[None, :] <= highest[:, None])
        allowed = allowed & (key_pos[None, :] >= 0) & (key_pos[None, :] < COLS)
        scores = jnp.where(allowed[None], scores, MASKED)
        attention = low(jax.nn.softmax(scores, axis=-1))
        mixed = jnp.einsum('hck,rkhd->rchd', attention, value_block, precision=HIGHEST)
        return mixed.reshape(ROWS, CB, D)
    starts = jnp.arange(COLS // CB, dtype=jnp.int32) * CB
    blocks = lax.map(jax.checkpoint(one_block), starts)
    return jnp.transpose(blocks, (1, 0, 2, 3)).reshape(ROWS, COLS, D)

def column_attention(queries, keys, values, present_mask):
    query_heads = queries.reshape(ROWS, COLS, H, DH)
    key_heads = keys.reshape(ROWS, COLS, H, DH)
    value_heads = values.reshape(ROWS, COLS, H, DH)
    scores = low_back(jnp.einsum('rchd,schd->chrs', query_heads, key_heads, precision=HIGHEST) * DH ** (-0.5))
    scores = jnp.where(present_mask[None, None, None, :] > 0, scores, MASKED)
    attention = low(jax.nn.softmax(scores, axis=-1))
    mixed = jnp.einsum('chrs,schd->rchd', attention, value_heads, precision=HIGHEST)
    return mixed.reshape(ROWS, COLS, D)

def alignment_layer(block_input, weight_matrices, norm_gain_values, present_mask, present_count, lower_reach, upper_reach):
    rounded = low(weight_matrices).reshape(NMAT, D, D)
    gain_rows = low(norm_gain_values).reshape(3, D)
    live_rows = present_mask[:, None, None]
    normed = low(layer_norm(block_input, gain_rows[0]))
    queries = both_ways(project(normed, rounded[0])) * live_rows
    keys = both_ways(project(normed, rounded[1]))
    values = both_ways(project(normed, rounded[2]))
    mixed = both_ways(row_attention(queries, keys, values, present_count, lower_reach, upper_reach))
    after_rows = block_input + low_back(project(mixed, rounded[3]))
    normed = low(layer_norm(after_rows, gain_rows[1]))
    queries = both_ways(project(normed, rounded[4]))
    keys = both_ways(project(normed, rounded[5]))
    values = both_ways(project(normed, rounded[6]))
    mixed = both_ways(column_attention(queries, keys, values, present_mask))
    after_cols = after_rows + low_back(project(mixed, rounded[7]))
    normed = low(layer_norm(after_cols, gain_rows[2]))
    fold_count = FF // D
    hidden = low_back(jnp.concatenate([project(normed, rounded[8 + block_index]) for block_index in range(fold_count)], axis=-1))
    active = low(jax.nn.gelu(hidden, approximate=False))
    down_matrix = rounded[8 + fold_count:].reshape(FF, D)
    result = after_cols + low_back(jnp.einsum('rcf,fe->rce', active, down_matrix, precision=HIGHEST))
    return result * live_rows

def adamw(master, moment, square, grad_total, rate, decay, steps_done):
    moment_new = BETA_ONE * moment + (1.0 - BETA_ONE) * grad_total
    square_new = BETA_TWO * square + (1.0 - BETA_TWO) * grad_total * grad_total
    moment_fix = 1.0 - BETA_ONE ** steps_done
    square_fix = 1.0 - BETA_TWO ** steps_done
    update = moment_new / moment_fix / (jnp.sqrt(square_new / square_fix) + ADAM_EPS)
    return (master - rate * (update + decay * master), moment_new, square_new)

def reference(alignment, cotangent, row_counts, band_reach, master_weights, weight_moment, weight_square, norm_gains, gain_moment, gain_square):
    alignments = MB * GROUPS
    inputs_all = alignment.reshape(alignments, ROWS, COLS, D)
    cotangents = cotangent.reshape(alignments, ROWS, COLS, D)
    counts = row_counts.reshape(alignments)
    reaches = band_reach.reshape(alignments, 2, COLS)

    def accumulate(running, item_slice):
        weight_sum, gain_sum = running
        block_input, block_cot, present_count, reach_bounds = item_slice
        present_mask = (jnp.arange(ROWS, dtype=jnp.int32) < present_count).astype(jnp.float32)
        count_number = present_count.astype(jnp.float32)

        def forward(layer_activations, weight_matrices, norm_gain_values):
            return alignment_layer(layer_activations, weight_matrices, norm_gain_values, present_mask, count_number, reach_bounds[0], reach_bounds[1])
        result, pullback = jax.vjp(forward, block_input.astype(jnp.float32), master_weights, norm_gains)
        input_part, weight_part, gain_part = pullback(block_cot.astype(jnp.float32))
        return ((weight_sum + weight_part, gain_sum + gain_part), (result.astype(jnp.bfloat16), input_part.astype(jnp.bfloat16)))
    initial = (jnp.zeros_like(master_weights), jnp.zeros_like(norm_gains))
    totals, produced = lax.scan(accumulate, initial, (inputs_all, cotangents, counts, reaches))
    weight_total, gain_total = totals
    outputs, input_grads = produced
    rate_matrix = D ** (-0.5)
    new_weights, new_moment, new_square = adamw(master_weights, weight_moment, weight_square, weight_total, rate_matrix, DECAY, STEP_NUMBER)
    new_gains, new_gain_moment, new_gain_square = adamw(norm_gains, gain_moment, gain_square, gain_total, RATE_GAIN, 0.0, STEP_NUMBER)
    full_shape = (MB, GROUPS, ROWS, COLS, D)
    return (outputs.reshape(full_shape), input_grads.reshape(full_shape), new_weights, new_moment, new_square, new_weights.astype(jnp.bfloat16), new_gains, new_gain_moment, new_gain_square)
```

```python
from functools import partial

import jax
import jax.numpy as jnp
from jax import lax
from jax.experimental import pallas as pl
from jax.experimental.pallas import tpu as pltpu
from jax.sharding import PartitionSpec as P

D = 768
H = 12
DH = 64
FF = 3072
NMAT = 16
ROWS = 4
CB = 64
HALO = 32
MB = 2
EXT = CB + 2 * HALO
SEQ = MB * ROWS
TOK = SEQ * CB
PAIRS = H // 2
LANES = 128
FOLD = FF // D

EPS = 1e-05
BETA_ONE = 0.9
BETA_TWO = 0.999
ADAM_EPS = 1e-08
DECAY = 0.01
RATE_GAIN = 0.3
STEP_NUMBER = 10.0
MASKED = -1e30
F32 = jnp.float32
LOW = jnp.bfloat16


def dot_nn(a, b):
    return lax.dot_general(a, b, (((1,), (0,)), ((), ())), preferred_element_type=F32)


def dot_nt(a, b):
    return lax.dot_general(a, b, (((1,), (1,)), ((), ())), preferred_element_type=F32)


def dot_tn(a, b):
    return lax.dot_general(a, b, (((0,), (0,)), ((), ())), preferred_element_type=F32)


def standardize(values):
    center = values - jnp.mean(values, axis=-1, keepdims=True)
    spread = lax.rsqrt(jnp.mean(center * center, axis=-1, keepdims=True) + EPS)
    return center * spread, spread


def norm_pull(upward, values, gain):
    scaled, spread = standardize(values)
    weighted = upward * gain
    result = spread * (
        weighted
        - jnp.mean(weighted, axis=-1, keepdims=True)
        - scaled * jnp.mean(weighted * scaled, axis=-1, keepdims=True)
    )
    return result, jnp.sum(upward * scaled, axis=0, keepdims=True)


def lane_window(pair):
    return pl.ds(pl.multiple_of(pair * LANES, LANES), LANES)


def side_by_side(ref, micro, window):
    return jnp.concatenate([ref[micro * ROWS + r, :, window] for r in range(ROWS)], axis=1)


def head_stack(packed):
    lane = lax.broadcasted_iota(jnp.int32, packed.shape, 1)
    first = (lane % LANES) < DH
    zero = jnp.zeros_like(packed)
    return jnp.concatenate([jnp.where(first, packed, zero), jnp.where(first, zero, packed)], axis=0)


def head_merge(stacked, r):
    block = stacked[:, r * LANES : (r + 1) * LANES]
    lane = lax.broadcasted_iota(jnp.int32, (CB, LANES), 1)
    return jnp.where(lane < DH, block[:CB], block[CB:])


def head_sums():
    feature = lax.broadcasted_iota(jnp.int32, (D, LANES), 0)
    head = lax.broadcasted_iota(jnp.int32, (D, LANES), 1)
    return (feature // DH == head).astype(F32).astype(LOW)


def head_spread():
    head = lax.broadcasted_iota(jnp.int32, (LANES, D), 0)
    feature = lax.broadcasted_iota(jnp.int32, (LANES, D), 1)
    return (feature // DH == head).astype(F32).astype(LOW)


def row_forward(scal, xe, allowed, gain, w, a1e, q, ke, ve, p1, o1, x1, a2):
    def norm_step(i, _):
        scaled, _s = standardize(xe[i].astype(F32))
        a1e[i] = (scaled * gain[0:1]).astype(LOW)
        return 0

    lax.fori_loop(0, SEQ, norm_step, 0)
    wide = a1e[...].reshape(SEQ * EXT, D)
    ke[...] = dot_nn(wide, w[1]).astype(LOW).reshape(SEQ, EXT, D)
    ve[...] = dot_nn(wide, w[2]).astype(LOW).reshape(SEQ, EXT, D)
    own = a1e[:, HALO : HALO + CB, :].reshape(TOK, D)
    q[...] = dot_nn(own, w[0]).astype(LOW).reshape(SEQ, CB, D)
    for i in range(SEQ):
        q[i] = (q[i].astype(F32) * scal[i // ROWS, 1 + i % ROWS]).astype(LOW)

    def attend(pair, _):
        window = lane_window(pair)
        for m in range(MB):
            query = head_stack(side_by_side(q, m, window))
            scores = dot_nt(query, side_by_side(ke, m, window)) * scal[m, 0]
            mask = allowed[m]
            mask = jnp.concatenate([mask, mask], axis=0)
            scores = jnp.where(mask > 0, scores, MASKED)
            weight = jnp.exp(scores - jnp.max(scores, axis=-1, keepdims=True))
            prob = weight / jnp.sum(weight, axis=-1, keepdims=True)
            p1[m, pair] = prob
            mixed = dot_nn(prob.astype(LOW), side_by_side(ve, m, window))
            for r in range(ROWS):
                o1[m * ROWS + r, :, window] = head_merge(mixed, r).astype(LOW)
        return 0

    lax.fori_loop(0, PAIRS, attend, 0)
    x1[...] = xe[:, HALO : HALO + CB, :].astype(F32) + dot_nn(
        o1[...].reshape(TOK, D), w[3]
    ).reshape(SEQ, CB, D)

    def next_norm(i, _):
        scaled, _s = standardize(x1[i])
        a2[i] = (scaled * gain[1:2]).astype(LOW)
        return 0

    lax.fori_loop(0, SEQ, next_norm, 0)


def col_forward(scal, x1, a2, gain, w, q2, k2, v2, p2, o2, x2, a3):
    flat = a2[...].reshape(TOK, D)
    q2[...] = dot_nn(flat, w[0]).astype(LOW).reshape(SEQ, CB, D)
    k2[...] = dot_nn(flat, w[1]).astype(LOW).reshape(SEQ, CB, D)
    v2[...] = dot_nn(flat, w[2]).astype(LOW).reshape(SEQ, CB, D)
    sums = head_sums()
    spread = head_spread()

    def attend(i, _):
        micro = i // ROWS
        query = q2[i].astype(F32)
        products = jnp.concatenate(
            [(query * k2[micro * ROWS + s].astype(F32)).astype(LOW) for s in range(ROWS)], axis=0
        )
        scores = dot_nn(products, sums) * (DH ** (-0.5))
        parts = [
            jnp.where(scal[micro, 1 + s] > 0, scores[s * CB : (s + 1) * CB], MASKED)
            for s in range(ROWS)
        ]
        top = jnp.maximum(jnp.maximum(parts[0], parts[1]), jnp.maximum(parts[2], parts[3]))
        parts = [jnp.exp(part - top) for part in parts]
        scale = 1.0 / (parts[0] + parts[1] + parts[2] + parts[3])
        prob = jnp.concatenate([part * scale for part in parts], axis=0)
        p2[i] = prob
        wide = dot_nn(prob.astype(LOW), spread)
        total = wide[:CB] * v2[micro * ROWS].astype(F32)
        for s in range(1, ROWS):
            total = total + wide[s * CB : (s + 1) * CB] * v2[micro * ROWS + s].astype(F32)
        o2[i] = total.astype(LOW)
        return 0

    lax.fori_loop(0, SEQ, attend, 0)
    x2[...] = x1[...] + dot_nn(o2[...].reshape(TOK, D), w[3]).reshape(SEQ, CB, D)

    def next_norm(i, _):
        scaled, _s = standardize(x2[i])
        a3[i] = (scaled * gain[2:3]).astype(LOW)
        return 0

    lax.fori_loop(0, SEQ, next_norm, 0)


CHUNK = 128


def feed_forward(
    scal, x2, a3, cot, gain, win, wout, out, e2, dwin, dwout, dgain, up, down, live_cot, gl, dhd, dgl
):
    step = pl.program_id(0)

    @pl.when(step == 0)
    def _():
        for i in range(SEQ):
            live_cot[i * CB : (i + 1) * CB] = (
                cot[i].astype(F32) * scal[i // ROWS, 1 + i % ROWS]
            ).astype(LOW)

    normed = a3[...].reshape(TOK, D)
    grad = live_cot[...]
    for base in range(0, TOK, CHUNK):
        rows = slice(base, base + CHUNK)
        hidden = dot_nn(normed[rows], win[0])
        pulled = dot_nt(grad[rows], wout[0])
        half = 0.5 * lax.erf(hidden * (0.5**0.5)) + 0.5
        gl[rows] = (hidden * half).astype(LOW)
        slope = half + hidden * (jnp.exp(-0.5 * hidden * hidden) * ((2.0 * jnp.pi) ** -0.5))
        dhd[rows] = (pulled * slope).astype(LOW)
    dwout[0] = dot_tn(gl[...], grad).astype(LOW)
    dwin[0] = dot_tn(normed, dhd[...]).astype(LOW)
    forward = dot_nn(gl[...], wout[0])
    backward = dot_nt(dhd[...], win[0])

    @pl.when(step == 0)
    def _():
        up[...] = forward
        down[...] = backward

    @pl.when(step > 0)
    def _():
        up[...] += forward
        down[...] += backward

    @pl.when(step == FOLD - 1)
    def _():
        total = jnp.zeros((1, D), F32)
        for i in range(SEQ):
            rows = slice(i * CB, (i + 1) * CB)
            value = x2[i]
            out[i] = ((value + up[rows]) * scal[i // ROWS, 1 + i % ROWS]).astype(LOW)
            part, gain_part = norm_pull(down[rows], value, gain[2:3])
            e2[i] = live_cot[rows].astype(F32) + part
            total = total + gain_part
        dgain[...] = total


def col_backward(
    scal, e2, o2, q2, k2, v2, p2, a2, x1, gain, w, dw, e1, dgain, do2, dq2, dk2, dv2, dka, dva
):
    low = e2[...].reshape(TOK, D).astype(LOW)
    dw[3] = dot_tn(o2[...].reshape(TOK, D), low).astype(LOW)
    do2[...] = dot_nt(low, w[3]).astype(LOW).reshape(SEQ, CB, D)
    sums = head_sums()
    spread = head_spread()
    dka[...] = jnp.zeros_like(dka)
    dva[...] = jnp.zeros_like(dva)

    def pull(i, _):
        micro = i // ROWS
        upward = do2[i].astype(F32)
        products = jnp.concatenate(
            [(upward * v2[micro * ROWS + s].astype(F32)).astype(LOW) for s in range(ROWS)], axis=0
        )
        dprob = dot_nn(products, sums)
        prob = p2[i]
        mixed = prob * dprob
        inner = mixed[:CB] + mixed[CB : 2 * CB] + mixed[2 * CB : 3 * CB] + mixed[3 * CB :]
        dscore = prob * (dprob - jnp.concatenate([inner] * ROWS, axis=0))
        wide = dot_nn(prob.astype(LOW), spread)
        dwide = dot_nn(dscore.astype(LOW), spread)
        query = q2[i].astype(F32)
        total = jnp.zeros((CB, D), F32)
        for s in range(ROWS):
            rows = slice(s * CB, (s + 1) * CB)
            total = total + dwide[rows] * k2[micro * ROWS + s].astype(F32)
            dka[micro * ROWS + s] += dwide[rows] * query
            dva[micro * ROWS + s] += wide[rows] * upward
        dq2[i] = (total * (DH ** (-0.5))).astype(LOW)
        return 0

    lax.fori_loop(0, SEQ, pull, 0)
    dk2[...] = (dka[...] * (DH ** (-0.5))).astype(LOW)
    dv2[...] = dva[...].astype(LOW)
    flat = a2[...].reshape(TOK, D)
    total = None
    for j, ref in enumerate((dq2, dk2, dv2)):
        grads = ref[...].reshape(TOK, D)
        dw[j] = dot_tn(flat, grads).astype(LOW)
        part = dot_nt(grads, w[j]).reshape(SEQ, CB, D)
        if j == 0:
            dka[...] = part
        else:
            dka[...] += part
    gain_total = jnp.zeros((1, D), F32)
    for i in range(SEQ):
        part, gain_part = norm_pull(dka[i], x1[i], gain[1:2])
        e1[i] = e2[i] + part
        gain_total = gain_total + gain_part
    dgain[...] = gain_total


def row_backward(scal, e1, o1, q, ke, ve, p1, a1e, w, dw, dq, dke, dve, do1):
    low = e1[...].reshape(TOK, D).astype(LOW)
    dw[3] = dot_tn(o1[...].reshape(TOK, D), low).astype(LOW)
    do1[...] = dot_nt(low, w[3]).astype(LOW).reshape(SEQ, CB, D)

    def pull(pair, _):
        window = lane_window(pair)
        for m in range(MB):
            query = head_stack(side_by_side(q, m, window))
            upward = head_stack(side_by_side(do1, m, window))
            prob = p1[m, pair]
            dprob = dot_nt(upward, side_by_side(ve, m, window))
            dscore = prob * (dprob - jnp.sum(prob * dprob, axis=-1, keepdims=True))
            dscore = dscore.astype(LOW)
            dvalue = dot_tn(prob.astype(LOW), upward)
            dkey = dot_tn(dscore, query) * scal[m, 0]
            dquery = dot_nn(dscore, side_by_side(ke, m, window)) * scal[m, 0]
            for r in range(ROWS):
                lanes = slice(r * LANES, (r + 1) * LANES)
                dve[m * ROWS + r, :, window] = dvalue[:, lanes].astype(LOW)
                dke[m * ROWS + r, :, window] = dkey[:, lanes].astype(LOW)
                dq[m * ROWS + r, :, window] = (head_merge(dquery, r) * scal[m, 1 + r]).astype(LOW)
        return 0

    lax.fori_loop(0, PAIRS, pull, 0)
    wide = a1e[...].reshape(SEQ * EXT, D)
    dw[0] = dot_tn(
        a1e[:, HALO : HALO + CB, :].reshape(TOK, D), dq[...].reshape(TOK, D)
    ).astype(LOW)
    dw[1] = dot_tn(wide, dke[...].reshape(SEQ * EXT, D)).astype(LOW)
    dw[2] = dot_tn(wide, dve[...].reshape(SEQ * EXT, D)).astype(LOW)


def input_backward(dq, dke, dve, from_low, from_high, w, e1, xe, gain, grad, dgain, own, acc):
    for j, ref in enumerate((dke, dve)):
        own[j, :, :HALO] = (
            ref[:, HALO:CB, :].astype(F32) + from_low[j].astype(F32)
        ).astype(LOW)
        own[j, :, HALO:] = (
            ref[:, CB : CB + HALO, :].astype(F32) + from_high[j].astype(F32)
        ).astype(LOW)
    acc[...] = dot_nt(dq[...].reshape(TOK, D), w[0]).reshape(SEQ, CB, D)
    for j in range(2):
        acc[...] += dot_nt(own[j].reshape(TOK, D), w[1 + j]).reshape(SEQ, CB, D)
    gain_total = jnp.zeros((1, D), F32)
    for i in range(SEQ):
        value = xe[i, HALO : HALO + CB, :].astype(F32)
        part, gain_part = norm_pull(acc[i], value, gain[0:1])
        grad[i] = (e1[i] + part).astype(LOW)
        gain_total = gain_total + gain_part
    dgain[...] = gain_total


def in_vmem(count):
    return [pl.BlockSpec(memory_space=pltpu.VMEM)] * count


def like(*shapes):
    return tuple(jax.ShapeDtypeStruct(shape, dtype) for shape, dtype in shapes)


SEQ_CB = (SEQ, CB, D)
SEQ_EXT = (SEQ, EXT, D)
SQUARE = (4, D, D)


def run_kernel(body, scal, args, outs, scratch=(), flops=0, megabytes=56):
    moved = sum(a.size * a.dtype.itemsize for a in args)
    moved += sum(o.size * jnp.dtype(o.dtype).itemsize for o in outs)
    ins = in_vmem(len(args))
    if scal is not None:
        args = (scal, *args)
        ins = [pl.BlockSpec(memory_space=pltpu.SMEM), *ins]
    return pl.pallas_call(
        body,
        name=body.__name__,
        out_shape=outs,
        in_specs=ins,
        out_specs=tuple(in_vmem(len(outs))),
        scratch_shapes=scratch,
        compiler_params=pltpu.CompilerParams(vmem_limit_bytes=megabytes << 20),
        cost_estimate=pl.CostEstimate(flops=flops, bytes_accessed=moved, transcendentals=0),
    )(*args)


UNIT = 2 * TOK * D * D


def call_row_forward(scal, xe, allowed, gain, w):
    outs = like(
        (SEQ_EXT, LOW),
        (SEQ_CB, LOW),
        (SEQ_EXT, LOW),
        (SEQ_EXT, LOW),
        ((MB, PAIRS, 2 * CB, EXT), F32),
        (SEQ_CB, LOW),
        (SEQ_CB, F32),
        (SEQ_CB, LOW),
    )
    return run_kernel(row_forward, scal, (xe, allowed, gain, w), outs, flops=8 * UNIT)


def call_col_forward(scal, x1, a2, gain, w):
    outs = like(
        (SEQ_CB, LOW),
        (SEQ_CB, LOW),
        (SEQ_CB, LOW),
        ((SEQ, ROWS * CB, LANES), F32),
        (SEQ_CB, LOW),
        (SEQ_CB, F32),
        (SEQ_CB, LOW),
    )
    return run_kernel(col_forward, scal, (x1, a2, gain, w), outs, flops=8 * UNIT)


def call_feed_forward(scal, x2, a3, cot, gain, win, wout):
    whole = lambda shape: pl.BlockSpec(shape, lambda f: (0,) * len(shape))
    block = pl.BlockSpec((1, D, D), lambda f: (f, 0, 0))
    outs = like((SEQ_CB, LOW), (SEQ_CB, F32), (SQUARE, LOW), (SQUARE, LOW), ((1, D), F32))
    return pl.pallas_call(
        feed_forward,
        name="feed_forward",
        grid=(FOLD,),
        out_shape=outs,
        in_specs=[
            pl.BlockSpec(memory_space=pltpu.SMEM),
            whole(SEQ_CB),
            whole(SEQ_CB),
            whole(SEQ_CB),
            whole((3, D)),
            block,
            block,
        ],
        out_specs=(whole(SEQ_CB), whole(SEQ_CB), block, block, whole((1, D))),
        scratch_shapes=[
            pltpu.VMEM((TOK, D), F32),
            pltpu.VMEM((TOK, D), F32),
            pltpu.VMEM((TOK, D), LOW),
            pltpu.VMEM((TOK, D), LOW),
            pltpu.VMEM((TOK, D), LOW),
            pltpu.VMEM((TOK, D), LOW),
        ],
        compiler_params=pltpu.CompilerParams(vmem_limit_bytes=56 << 20),
        cost_estimate=pl.CostEstimate(
            flops=24 * UNIT, bytes_accessed=2 * 8 * 2 * D * D + 12 * TOK * D, transcendentals=0
        ),
    )(scal, x2, a3, cot, gain, win, wout)


def call_col_backward(scal, e2, o2, q2, k2, v2, p2, a2, x1, gain, w):
    outs = like((SQUARE, LOW), (SEQ_CB, F32), ((1, D), F32))
    scratch = [pltpu.VMEM(SEQ_CB, LOW)] * 4 + [pltpu.VMEM(SEQ_CB, F32)] * 2
    return run_kernel(
        col_backward, scal, (e2, o2, q2, k2, v2, p2, a2, x1, gain, w), outs, scratch, 16 * UNIT
    )


def call_row_backward(scal, e1, o1, q, ke, ve, p1, a1e, w):
    outs = like((SQUARE, LOW), (SEQ_CB, LOW), (SEQ_EXT, LOW), (SEQ_EXT, LOW))
    scratch = [pltpu.VMEM(SEQ_CB, LOW)]
    return run_kernel(
        row_backward, scal, (e1, o1, q, ke, ve, p1, a1e, w), outs, scratch, 16 * UNIT
    )


def call_input_backward(dq, dke, dve, from_low, from_high, w, e1, xe, gain):
    outs = like((SEQ_CB, LOW), ((1, D), F32))
    scratch = [pltpu.VMEM((2, *SEQ_CB), LOW), pltpu.VMEM(SEQ_CB, F32)]
    return run_kernel(
        input_backward,
        None,
        (dq, dke, dve, from_low, from_high, w, e1, xe, gain),
        outs,
        scratch,
        4 * UNIT,
    )


def shifted(block, dim, width):
    count = lax.axis_size("cols")
    forward = [(i, i + 1) for i in range(count - 1)]
    backward = [(target, source) for source, target in forward]
    from_low = lax.ppermute(
        lax.slice_in_dim(block, block.shape[dim] - width, None, axis=dim), "cols", forward
    )
    from_high = lax.ppermute(lax.slice_in_dim(block, 0, width, axis=dim), "cols", backward)
    return from_low, from_high


def adamw(master, moment, square, grad_total, rate, decay, steps_done):
    moment_new = BETA_ONE * moment + (1.0 - BETA_ONE) * grad_total
    square_new = BETA_TWO * square + (1.0 - BETA_TWO) * grad_total * grad_total
    moment_fix = 1.0 - BETA_ONE**steps_done
    square_fix = 1.0 - BETA_TWO**steps_done
    update = moment_new / moment_fix / (jnp.sqrt(square_new / square_fix) + ADAM_EPS)
    return (master - rate * (update + decay * master), moment_new, square_new)


def band_mask(band_reach):
    first_col = lax.axis_index("cols") * CB
    col_total = CB * lax.axis_size("cols")
    query_pos = first_col + jnp.arange(CB, dtype=jnp.int32)
    key_pos = first_col - HALO + jnp.arange(EXT, dtype=jnp.int32)
    lowest = query_pos[None] - band_reach[:, 0]
    highest = query_pos[None] + band_reach[:, 1]
    key = key_pos[None, None]
    allowed = (key >= lowest[..., None]) & (key <= highest[..., None])
    allowed = allowed & (key >= 0) & (key < col_total)
    return allowed.astype(F32)


def layer(tokens, cot, counts, reach, weights, gain):
    present = (jnp.arange(ROWS, dtype=jnp.int32)[None] < counts[:, None]).astype(F32)
    row_scale = DH ** (-0.5) * lax.rsqrt(counts.astype(F32))
    scal = jnp.concatenate([row_scale[:, None], present], axis=1)
    allowed = band_mask(reach)
    from_low, from_high = shifted(tokens, 1, HALO)
    xe = jnp.concatenate([from_low, tokens, from_high], axis=1)
    a1e, q, ke, ve, p1, o1, x1, a2 = call_row_forward(scal, xe, allowed, gain, weights[0:4])
    q2, k2, v2, p2, o2, x2, a3 = call_col_forward(scal, x1, a2, gain, weights[4:8])
    out, e2, dwin, dwout, dg3 = call_feed_forward(
        scal, x2, a3, cot, gain, weights[8:12], weights[12:16]
    )
    dw_col, e1, dg2 = call_col_backward(scal, e2, o2, q2, k2, v2, p2, a2, x1, gain, weights[4:8])
    dw_row, dq, dke, dve = call_row_backward(scal, e1, o1, q, ke, ve, p1, a1e, weights[0:4])
    rims = jnp.stack([dke, dve])
    count = lax.axis_size("cols")
    forward = [(i, i + 1) for i in range(count - 1)]
    backward = [(target, source) for source, target in forward]
    to_high = lax.ppermute(rims[:, :, HALO + CB :], "cols", forward)
    to_low = lax.ppermute(rims[:, :, :HALO], "cols", backward)
    grad, dg1 = call_input_backward(dq, dke, dve, to_high, to_low, weights[0:3], e1, xe, gain)
    weight_grad = jnp.concatenate([dw_row, dw_col, dwin, dwout], axis=0)
    gain_grad = jnp.concatenate([dg1, dg2, dg3], axis=0)
    return out, grad, weight_grad, gain_grad


def per_device(
    alignment,
    cotangent,
    row_counts,
    band_reach,
    master_weights,
    weight_moment,
    weight_square,
    norm_gains,
    gain_moment,
    gain_square,
):
    axes = ("cols", "fsdp")
    weights = lax.all_gather(master_weights.astype(LOW), axes, axis=0, tiled=True)
    gain = lax.all_gather(norm_gains.astype(LOW), axes, axis=0, tiled=True)
    out, grad, weight_grad, gain_grad = layer(
        alignment.reshape(SEQ, CB, D),
        cotangent.reshape(SEQ, CB, D),
        row_counts[:, 0],
        band_reach[:, 0],
        weights.reshape(NMAT, D, D),
        gain.astype(F32).reshape(3, D),
    )
    weight_total = lax.psum_scatter(
        weight_grad.reshape(NMAT * D, D), axes, scatter_dimension=0, tiled=True
    ).astype(F32)
    gain_total = lax.psum_scatter(gain_grad.reshape(3 * D), axes, scatter_dimension=0, tiled=True)
    new_weights, new_moment, new_square = adamw(
        master_weights, weight_moment, weight_square, weight_total, D ** (-0.5), DECAY, STEP_NUMBER
    )
    new_gains, new_gain_moment, new_gain_square = adamw(
        norm_gains, gain_moment, gain_square, gain_total, RATE_GAIN, 0.0, STEP_NUMBER
    )
    shape = (MB, 1, ROWS, CB, D)
    return (
        out.reshape(shape),
        grad.reshape(shape),
        new_weights,
        new_moment,
        new_square,
        new_weights.astype(LOW),
        new_gains,
        new_gain_moment,
        new_gain_square,
    )


def solution(mesh):
    tokens = P(None, "fsdp", None, "cols", None)
    rows = P(("cols", "fsdp"), None)
    flat = P(("cols", "fsdp"))
    in_specs = (
        tokens,
        tokens,
        P(None, "fsdp"),
        P(None, "fsdp", None, "cols"),
        rows,
        rows,
        rows,
        flat,
        flat,
        flat,
    )
    out_specs = (tokens, tokens, rows, rows, rows, rows, flat, flat, flat)
    return jax.shard_map(
        per_device, mesh=mesh, in_specs=in_specs, out_specs=out_specs, check_vma=False
    )
```

```python
from functools import partial

import jax
import jax.numpy as jnp
from jax import lax
from jax.experimental import pallas as pl
from jax.experimental.pallas import tpu as pltpu
from jax.sharding import PartitionSpec as P

D = 768
H = 12
DH = 64
FF = 3072
NMAT = 16
ROWS = 4
CB = 64
HALO = 32
MB = 2
EXT = CB + 2 * HALO
SEQ = MB * ROWS
TOK = SEQ * CB
PAIRS = H // 2
LANES = 128
FOLD = FF // D
PART = 192
SPAN = 2 * PART

EPS = 1e-05
BETA_ONE = 0.9
BETA_TWO = 0.999
ADAM_EPS = 1e-08
DECAY = 0.01
RATE_GAIN = 0.3
STEP_NUMBER = 10.0
MASKED = -1e30
F32 = jnp.float32
LOW = jnp.bfloat16


def dot_nn(a, b):
    return lax.dot_general(a, b, (((1,), (0,)), ((), ())), preferred_element_type=F32)


def dot_nt(a, b):
    return lax.dot_general(a, b, (((1,), (1,)), ((), ())), preferred_element_type=F32)


def dot_tn(a, b):
    return lax.dot_general(a, b, (((0,), (0,)), ((), ())), preferred_element_type=F32)


def standardize(values):
    center = values - jnp.mean(values, axis=-1, keepdims=True)
    spread = lax.rsqrt(jnp.mean(center * center, axis=-1, keepdims=True) + EPS)
    return center * spread, spread


def norm_pull(upward, values, gain):
    scaled, spread = standardize(values)
    weighted = upward * gain
    result = spread * (
        weighted
        - jnp.mean(weighted, axis=-1, keepdims=True)
        - scaled * jnp.mean(weighted * scaled, axis=-1, keepdims=True)
    )
    return result, jnp.sum(upward * scaled, axis=0, keepdims=True)


def lane_window(pair):
    return pl.ds(pl.multiple_of(pair * LANES, LANES), LANES)


def side_by_side(ref, micro, window):
    return jnp.concatenate([ref[micro * ROWS + r, :, window] for r in range(ROWS)], axis=1)


def head_stack(packed):
    lane = lax.broadcasted_iota(jnp.int32, packed.shape, 1)
    first = (lane % LANES) < DH
    zero = jnp.zeros_like(packed)
    return jnp.concatenate([jnp.where(first, packed, zero), jnp.where(first, zero, packed)], axis=0)


def head_merge(stacked, r):
    block = stacked[:, r * LANES : (r + 1) * LANES]
    lane = lax.broadcasted_iota(jnp.int32, (CB, LANES), 1)
    return jnp.where(lane < DH, block[:CB], block[CB:])


def head_sums():
    feature = lax.broadcasted_iota(jnp.int32, (D, LANES), 0)
    head = lax.broadcasted_iota(jnp.int32, (D, LANES), 1)
    return (feature // DH == head).astype(F32).astype(LOW)


def head_spread():
    head = lax.broadcasted_iota(jnp.int32, (LANES, D), 0)
    feature = lax.broadcasted_iota(jnp.int32, (LANES, D), 1)
    return (feature // DH == head).astype(F32).astype(LOW)


def flip(index, relative):
    return index if relative == 0 else 1 - index


def fetch_copies(place, own, other, w, sems):
    copies = []
    count = own.shape[3]
    for n in range(count):
        for core_rel, source in enumerate((own, other)):
            for part in range(2):
                for i in range(2):
                    for j in range(2):
                        y_rel, x_rel = (i, j) if part == 0 else (j, i)
                        matrix = 2 * flip(place[1], y_rel) + flip(place[2], core_rel) + 4 * n
                        row = pl.multiple_of(flip(place[0], x_rel) * SPAN + part * PART, PART)
                        copies.append(
                            pltpu.make_async_copy(
                                source.at[part, i, j, n],
                                w.at[matrix, pl.ds(row, PART)],
                                sems.at[len(copies)],
                            )
                        )
    return copies


def emit_matrix(place, source, matrix, n, keep, send, sems, base):
    core_same = place[2] == matrix % 2
    y_rel = jnp.where(place[1] == matrix // 2, 0, 1)
    waits = []
    for x in range(2):
        x_rel = jnp.where(place[0] == x, 0, 1)
        for part in range(2):
            i, j = (x_rel, y_rel) if part == 0 else (y_rel, x_rel)
            block = source.at[pl.ds(x * SPAN + part * PART, PART)]
            sem = sems.at[base + 2 * x + part]
            kept = pltpu.make_async_copy(block, keep.at[part, i, j, n], sem)
            sent = pltpu.make_async_copy(block, send.at[part, i, j, n], sem)
            pl.when(core_same)(kept.start)
            pl.when(jnp.logical_not(core_same))(sent.start)
            waits.append(kept)
    return waits


def row_forward(
    scal,
    place,
    tokens,
    from_low,
    from_high,
    allowed,
    gain,
    own,
    other,
    a1e,
    q,
    ke,
    ve,
    p1,
    o1,
    x1,
    a2,
    w,
    sems,
):
    copies = fetch_copies(place, own, other, w, sems)
    for copy in copies:
        copy.start()
    def norm_step(i, _):
        for source, start, size in (
            (from_low, 0, HALO),
            (tokens, HALO, CB),
            (from_high, HALO + CB, HALO),
        ):
            scaled, _s = standardize(source[i].astype(F32))
            a1e[i, start : start + size] = (scaled * gain[0:1]).astype(LOW)
        return 0

    lax.fori_loop(0, SEQ, norm_step, 0)
    for copy in copies:
        copy.wait()
    wide = a1e[...].reshape(SEQ * EXT, D)
    ke[...] = dot_nn(wide, w[1]).astype(LOW).reshape(SEQ, EXT, D)
    ve[...] = dot_nn(wide, w[2]).astype(LOW).reshape(SEQ, EXT, D)
    inner = a1e[:, HALO : HALO + CB, :].reshape(TOK, D)
    q[...] = dot_nn(inner, w[0]).astype(LOW).reshape(SEQ, CB, D)
    for i in range(SEQ):
        q[i] = (q[i].astype(F32) * scal[i // ROWS, 1 + i % ROWS]).astype(LOW)

    def attend(pair, _):
        window = lane_window(pair)
        for m in range(MB):
            query = head_stack(side_by_side(q, m, window))
            scores = dot_nt(query, side_by_side(ke, m, window)) * scal[m, 0]
            mask = allowed[m]
            mask = jnp.concatenate([mask, mask], axis=0)
            scores = jnp.where(mask > 0, scores, MASKED)
            weight = jnp.exp(scores - jnp.max(scores, axis=-1, keepdims=True))
            prob = weight / jnp.sum(weight, axis=-1, keepdims=True)
            p1[m, pair] = prob
            mixed = dot_nn(prob.astype(LOW), side_by_side(ve, m, window))
            for r in range(ROWS):
                o1[m * ROWS + r, :, window] = head_merge(mixed, r).astype(LOW)
        return 0

    lax.fori_loop(0, PAIRS, attend, 0)
    x1[...] = tokens[...].astype(F32) + dot_nn(
        o1[...].reshape(TOK, D), w[3]
    ).reshape(SEQ, CB, D)

    def next_norm(i, _):
        scaled, _s = standardize(x1[i])
        a2[i] = (scaled * gain[1:2]).astype(LOW)
        return 0

    lax.fori_loop(0, SEQ, next_norm, 0)


def col_forward(
    scal, place, x1, a2, gain, own, other, q2, k2, v2, p2, o2, x2, a3, w, sems
):
    copies = fetch_copies(place, own, other, w, sems)
    for copy in copies:
        copy.start()
    for copy in copies:
        copy.wait()
    flat = a2[...].reshape(TOK, D)
    q2[...] = dot_nn(flat, w[0]).astype(LOW).reshape(SEQ, CB, D)
    k2[...] = dot_nn(flat, w[1]).astype(LOW).reshape(SEQ, CB, D)
    v2[...] = dot_nn(flat, w[2]).astype(LOW).reshape(SEQ, CB, D)
    sums = head_sums()
    spread = head_spread()

    def attend(i, _):
        micro = i // ROWS
        query = q2[i].astype(F32)
        products = jnp.concatenate(
            [(query * k2[micro * ROWS + s].astype(F32)).astype(LOW) for s in range(ROWS)], axis=0
        )
        scores = dot_nn(products, sums) * (DH ** (-0.5))
        parts = [
            jnp.where(scal[micro, 1 + s] > 0, scores[s * CB : (s + 1) * CB], MASKED)
            for s in range(ROWS)
        ]
        top = jnp.maximum(jnp.maximum(parts[0], parts[1]), jnp.maximum(parts[2], parts[3]))
        parts = [jnp.exp(part - top) for part in parts]
        scale = 1.0 / (parts[0] + parts[1] + parts[2] + parts[3])
        prob = jnp.concatenate([part * scale for part in parts], axis=0)
        p2[i] = prob
        wide = dot_nn(prob.astype(LOW), spread)
        total = wide[:CB] * v2[micro * ROWS].astype(F32)
        for s in range(1, ROWS):
            total = total + wide[s * CB : (s + 1) * CB] * v2[micro * ROWS + s].astype(F32)
        o2[i] = total.astype(LOW)
        return 0

    lax.fori_loop(0, SEQ, attend, 0)
    x2[...] = x1[...] + dot_nn(o2[...].reshape(TOK, D), w[3]).reshape(SEQ, CB, D)

    def next_norm(i, _):
        scaled, _s = standardize(x2[i])
        a3[i] = (scaled * gain[2:3]).astype(LOW)
        return 0

    lax.fori_loop(0, SEQ, next_norm, 0)


CHUNK = 128


def feed_forward(
    scal,
    place,
    x2,
    a3,
    cot,
    gain,
    own,
    other,
    out,
    e2,
    dgain,
    keep,
    send,
    up,
    down,
    live_cot,
    gl,
    dhd,
    w,
    dw,
    in_sems,
    out_sems,
):
    copies = fetch_copies(place, own, other, w, in_sems)
    for copy in copies:
        copy.start()
    for i in range(SEQ):
        live_cot[i * CB : (i + 1) * CB] = (
            cot[i].astype(F32) * scal[i // ROWS, 1 + i % ROWS]
        ).astype(LOW)
    normed = a3[...].reshape(TOK, D)
    grad = live_cot[...]
    for copy in copies:
        copy.wait()
    waits = []
    for step in range(FOLD):
        win = w[step]
        wout = w[FOLD + step]
        for base in range(0, TOK, CHUNK):
            rows = slice(base, base + CHUNK)
            hidden = dot_nn(normed[rows], win)
            pulled = dot_nt(grad[rows], wout)
            half = 0.5 * lax.erf(hidden * (0.5**0.5)) + 0.5
            gl[rows] = (hidden * half).astype(LOW)
            slope = half + hidden * (jnp.exp(-0.5 * hidden * hidden) * ((2.0 * jnp.pi) ** -0.5))
            dhd[rows] = (pulled * slope).astype(LOW)
        for n, value in enumerate((dot_tn(normed, dhd[...]), dot_tn(gl[...], grad))):
            slot = 4 * n + step
            dw[slot] = value.astype(LOW)
            waits += emit_matrix(place, dw.at[slot], step, n, keep, send, out_sems, 4 * slot)
        forward = dot_nn(gl[...], wout)
        backward = dot_nt(dhd[...], win)
        if step == 0:
            up[...] = forward
            down[...] = backward
        else:
            up[...] += forward
            down[...] += backward
    total = jnp.zeros((1, D), F32)
    for i in range(SEQ):
        rows = slice(i * CB, (i + 1) * CB)
        value = x2[i]
        out[i] = ((value + up[rows]) * scal[i // ROWS, 1 + i % ROWS]).astype(LOW)
        part, gain_part = norm_pull(down[rows], value, gain[2:3])
        e2[i] = live_cot[rows].astype(F32) + part
        total = total + gain_part
    dgain[...] = total
    for copy in waits:
        copy.wait()


def col_backward(
    scal,
    place,
    e2,
    o2,
    q2,
    k2,
    v2,
    p2,
    a2,
    x1,
    gain,
    own,
    other,
    e1,
    dgain,
    keep,
    send,
    do2,
    dq2,
    dk2,
    dv2,
    dka,
    dva,
    w,
    dw,
    in_sems,
    out_sems,
):
    copies = fetch_copies(place, own, other, w, in_sems)
    for copy in copies:
        copy.start()
    for copy in copies:
        copy.wait()
    low = e2[...].reshape(TOK, D).astype(LOW)
    dw[3] = dot_tn(o2[...].reshape(TOK, D), low).astype(LOW)
    waits = emit_matrix(place, dw.at[3], 3, 0, keep, send, out_sems, 12)
    do2[...] = dot_nt(low, w[3]).astype(LOW).reshape(SEQ, CB, D)
    sums = head_sums()
    spread = head_spread()
    dka[...] = jnp.zeros_like(dka)
    dva[...] = jnp.zeros_like(dva)

    def pull(i, _):
        micro = i // ROWS
        upward = do2[i].astype(F32)
        products = jnp.concatenate(
            [(upward * v2[micro * ROWS + s].astype(F32)).astype(LOW) for s in range(ROWS)], axis=0
        )
        dprob = dot_nn(products, sums)
        prob = p2[i]
        mixed = prob * dprob
        inner = mixed[:CB] + mixed[CB : 2 * CB] + mixed[2 * CB : 3 * CB] + mixed[3 * CB :]
        dscore = prob * (dprob - jnp.concatenate([inner] * ROWS, axis=0))
        wide = dot_nn(prob.astype(LOW), spread)
        dwide = dot_nn(dscore.astype(LOW), spread)
        query = q2[i].astype(F32)
        total = jnp.zeros((CB, D), F32)
        for s in range(ROWS):
            rows = slice(s * CB, (s + 1) * CB)
            total = total + dwide[rows] * k2[micro * ROWS + s].astype(F32)
            dka[micro * ROWS + s] += dwide[rows] * query
            dva[micro * ROWS + s] += wide[rows] * upward
        dq2[i] = (total * (DH ** (-0.5))).astype(LOW)
        return 0

    lax.fori_loop(0, SEQ, pull, 0)
    dk2[...] = (dka[...] * (DH ** (-0.5))).astype(LOW)
    dv2[...] = dva[...].astype(LOW)
    flat = a2[...].reshape(TOK, D)
    total = None
    for j, ref in enumerate((dq2, dk2, dv2)):
        grads = ref[...].reshape(TOK, D)
        dw[j] = dot_tn(flat, grads).astype(LOW)
        waits += emit_matrix(place, dw.at[j], j, 0, keep, send, out_sems, 4 * j)
        part = dot_nt(grads, w[j]).reshape(SEQ, CB, D)
        if j == 0:
            dka[...] = part
        else:
            dka[...] += part
    gain_total = jnp.zeros((1, D), F32)
    for i in range(SEQ):
        part, gain_part = norm_pull(dka[i], x1[i], gain[1:2])
        e1[i] = e2[i] + part
        gain_total = gain_total + gain_part
    dgain[...] = gain_total
    for copy in waits:
        copy.wait()


def row_backward(
    scal,
    place,
    e1,
    o1,
    q,
    ke,
    ve,
    p1,
    a1e,
    own,
    other,
    dq,
    inner,
    to_low,
    to_high,
    keep,
    send,
    do1,
    dke,
    dve,
    w,
    dw,
    in_sems,
    out_sems,
):
    copies = fetch_copies(place, own, other, w, in_sems)
    for copy in copies:
        copy.start()
    for copy in copies:
        copy.wait()
    low = e1[...].reshape(TOK, D).astype(LOW)
    dw[3] = dot_tn(o1[...].reshape(TOK, D), low).astype(LOW)
    waits = emit_matrix(place, dw.at[3], 3, 0, keep, send, out_sems, 12)
    do1[...] = dot_nt(low, w[3]).astype(LOW).reshape(SEQ, CB, D)

    def pull(pair, _):
        window = lane_window(pair)
        for m in range(MB):
            query = head_stack(side_by_side(q, m, window))
            upward = head_stack(side_by_side(do1, m, window))
            prob = p1[m, pair]
            dprob = dot_nt(upward, side_by_side(ve, m, window))
            dscore = prob * (dprob - jnp.sum(prob * dprob, axis=-1, keepdims=True))
            dscore = dscore.astype(LOW)
            dvalue = dot_tn(prob.astype(LOW), upward)
            dkey = dot_tn(dscore, query) * scal[m, 0]
            dquery = dot_nn(dscore, side_by_side(ke, m, window)) * scal[m, 0]
            for r in range(ROWS):
                lanes = slice(r * LANES, (r + 1) * LANES)
                dve[m * ROWS + r, :, window] = dvalue[:, lanes].astype(LOW)
                dke[m * ROWS + r, :, window] = dkey[:, lanes].astype(LOW)
                dq[m * ROWS + r, :, window] = (head_merge(dquery, r) * scal[m, 1 + r]).astype(LOW)
        return 0

    lax.fori_loop(0, PAIRS, pull, 0)
    for j, ref in enumerate((dke, dve)):
        inner[j] = ref[:, HALO : HALO + CB, :]
        to_low[j] = ref[:, :HALO, :]
        to_high[j] = ref[:, HALO + CB :, :]
    wide = a1e[...].reshape(SEQ * EXT, D)
    dw[0] = dot_tn(
        a1e[:, HALO : HALO + CB, :].reshape(TOK, D), dq[...].reshape(TOK, D)
    ).astype(LOW)
    waits += emit_matrix(place, dw.at[0], 0, 0, keep, send, out_sems, 0)
    dw[1] = dot_tn(wide, dke[...].reshape(SEQ * EXT, D)).astype(LOW)
    waits += emit_matrix(place, dw.at[1], 1, 0, keep, send, out_sems, 4)
    dw[2] = dot_tn(wide, dve[...].reshape(SEQ * EXT, D)).astype(LOW)
    waits += emit_matrix(place, dw.at[2], 2, 0, keep, send, out_sems, 8)
    for copy in waits:
        copy.wait()


def input_backward(
    place, dq, inner, from_low, from_high, own, other, e1, tokens, gain, grad, dgain, full, acc, w, sems
):
    copies = fetch_copies(place, own, other, w, sems)
    for copy in copies:
        copy.start()
    for j in range(2):
        full[j, :, :HALO] = (
            inner[j, :, :HALO].astype(F32) + from_low[j].astype(F32)
        ).astype(LOW)
        full[j, :, HALO:] = (
            inner[j, :, HALO:].astype(F32) + from_high[j].astype(F32)
        ).astype(LOW)
    for copy in copies:
        copy.wait()
    acc[...] = dot_nt(dq[...].reshape(TOK, D), w[0]).reshape(SEQ, CB, D)
    for j in range(2):
        acc[...] += dot_nt(full[j].reshape(TOK, D), w[1 + j]).reshape(SEQ, CB, D)
    gain_total = jnp.zeros((1, D), F32)
    for i in range(SEQ):
        part, gain_part = norm_pull(acc[i], tokens[i].astype(F32), gain[0:1])
        grad[i] = (e1[i] + part).astype(LOW)
        gain_total = gain_total + gain_part
    dgain[...] = gain_total


def in_vmem(count):
    return [pl.BlockSpec(memory_space=pltpu.VMEM)] * count


def like(*shapes):
    return tuple(jax.ShapeDtypeStruct(shape, dtype) for shape, dtype in shapes)


SEQ_CB = (SEQ, CB, D)
SEQ_EXT = (SEQ, EXT, D)
RIM = (2, SEQ, HALO, D)
UNIT = 2 * TOK * D * D
VM = pltpu.VMEM
DMA = pltpu.SemaphoreType.DMA


def pieces(count):
    return (2, 2, 2, count, PART, D)


def run_kernel(body, scalars, args, outs, scratch, flops, raw_in=(), raw_out=()):
    vmem = pl.BlockSpec(memory_space=pltpu.VMEM)
    raw = pl.BlockSpec(memory_space=pl.ANY)
    moved = sum(a.size * a.dtype.itemsize for a in args)
    moved += sum(o.size * jnp.dtype(o.dtype).itemsize for o in outs)
    return pl.pallas_call(
        body,
        name=body.__name__,
        out_shape=outs,
        in_specs=[pl.BlockSpec(memory_space=pltpu.SMEM)] * len(scalars)
        + [raw if i in raw_in else vmem for i in range(len(args))],
        out_specs=tuple(raw if i in raw_out else vmem for i in range(len(outs))),
        scratch_shapes=scratch,
        compiler_params=pltpu.CompilerParams(vmem_limit_bytes=60 << 20),
        cost_estimate=pl.CostEstimate(flops=flops, bytes_accessed=moved, transcendentals=0),
    )(*scalars, *args)


def call_row_forward(scalars, tokens, from_low, from_high, allowed, gain, weights):
    outs = like(
        (SEQ_EXT, LOW),
        (SEQ_CB, LOW),
        (SEQ_EXT, LOW),
        (SEQ_EXT, LOW),
        ((MB, PAIRS, 2 * CB, EXT), F32),
        (SEQ_CB, LOW),
        (SEQ_CB, F32),
        (SEQ_CB, LOW),
    )
    args = (tokens, from_low, from_high, allowed, gain, *weights)
    scratch = [VM((4, D, D), LOW), DMA((16,))]
    return run_kernel(row_forward, scalars, args, outs, scratch, 8 * UNIT, (5, 6))


def call_col_forward(scalars, x1, a2, gain, weights):
    outs = like(
        (SEQ_CB, LOW),
        (SEQ_CB, LOW),
        (SEQ_CB, LOW),
        ((SEQ, ROWS * CB, LANES), F32),
        (SEQ_CB, LOW),
        (SEQ_CB, F32),
        (SEQ_CB, LOW),
    )
    scratch = [VM((4, D, D), LOW), DMA((16,))]
    return run_kernel(
        col_forward, scalars, (x1, a2, gain, *weights), outs, scratch, 8 * UNIT, (3, 4)
    )


def call_feed_forward(scalars, x2, a3, cot, gain, weights):
    outs = like(
        (SEQ_CB, LOW), (SEQ_CB, F32), ((1, D), F32), (pieces(2), LOW), (pieces(2), LOW)
    )
    scratch = [
        VM((TOK, D), F32),
        VM((TOK, D), F32),
        VM((TOK, D), LOW),
        VM((TOK, D), LOW),
        VM((TOK, D), LOW),
        VM((8, D, D), LOW),
        VM((8, D, D), LOW),
        DMA((32,)),
        DMA((32,)),
    ]
    args = (x2, a3, cot, gain, *weights)
    return run_kernel(feed_forward, scalars, args, outs, scratch, 24 * UNIT, (4, 5), (3, 4))


def call_col_backward(scalars, e2, o2, q2, k2, v2, p2, a2, x1, gain, weights):
    outs = like((SEQ_CB, F32), ((1, D), F32), (pieces(1), LOW), (pieces(1), LOW))
    scratch = [VM(SEQ_CB, LOW)] * 4 + [VM(SEQ_CB, F32)] * 2
    scratch += [VM((4, D, D), LOW)] * 2 + [DMA((16,))] * 2
    args = (e2, o2, q2, k2, v2, p2, a2, x1, gain, *weights)
    return run_kernel(col_backward, scalars, args, outs, scratch, 16 * UNIT, (9, 10), (2, 3))


def call_row_backward(scalars, e1, o1, q, ke, ve, p1, a1e, weights):
    outs = like(
        (SEQ_CB, LOW),
        ((2, *SEQ_CB), LOW),
        (RIM, LOW),
        (RIM, LOW),
        (pieces(1), LOW),
        (pieces(1), LOW),
    )
    scratch = [VM(SEQ_CB, LOW)] + [VM(SEQ_EXT, LOW)] * 2
    scratch += [VM((4, D, D), LOW)] * 2 + [DMA((16,))] * 2
    args = (e1, o1, q, ke, ve, p1, a1e, *weights)
    return run_kernel(row_backward, scalars, args, outs, scratch, 16 * UNIT, (7, 8), (4, 5))


def call_input_backward(place, dq, inner, from_low, from_high, weights, e1, tokens, gain):
    outs = like((SEQ_CB, LOW), ((1, D), F32))
    scratch = [VM((2, *SEQ_CB), LOW), VM(SEQ_CB, F32), VM((4, D, D), LOW), DMA((16,))]
    args = (dq, inner, from_low, from_high, *weights, e1, tokens, gain)
    return run_kernel(input_backward, (place,), args, outs, scratch, 4 * UNIT, (4, 5))


def swap_pairs(count, bit):
    return [(i, i ^ bit) for i in range(count)]


class Staged:
    planes = 4

    def __init__(self):
        count = NMAT
        step = count // self.planes
        self.step = step
        self.count = count
        cols = lax.axis_index("cols")
        self.z = cols // step
        self.place = jnp.stack([lax.axis_index("fsdp"), (cols // 2) % 2, cols % 2])

    def over_x(self, value):
        return lax.ppermute(value, "fsdp", [(0, 1), (1, 0)])

    def over_y(self, value):
        return lax.ppermute(value, "cols", swap_pairs(self.count, 2))

    def over_core(self, value):
        return lax.ppermute(value, "cols", swap_pairs(self.count, 1))

    def over_z(self, value, pairs):
        step = self.step
        full = [(a * step + i, b * step + i) for a, b in pairs for i in range(step)]
        return lax.ppermute(value, "cols", full)

    def by_plane(self, options):
        result = options[-1]
        for index in range(len(options) - 2, -1, -1):
            result = jnp.where(self.z == index, options[index], result)
        return result

    def spread_planes(self, shard):
        last = self.planes - 1
        up, down = [shard], [shard]
        for k in range(last):
            up.append(self.over_z(up[-1], [(i, i + 1) for i in range(k, last)]))
            down.append(self.over_z(down[-1], [(i + 1, i) for i in range(last - k)]))
        return [
            self.by_plane([up[z - b] if z >= b else down[b - z] for z in range(self.planes)])
            for b in range(self.planes)
        ]

    def gather_group(self, shards):
        both = jnp.stack(shards)
        first, second = both[:, :PART], both[:, PART:]
        first = jnp.stack([first, self.over_x(first)])
        second = jnp.stack([second, self.over_y(second)])
        own = jnp.stack(
            [
                jnp.stack([first, self.over_y(first)]),
                jnp.stack([second, self.over_x(second)]),
            ]
        )
        return own, self.over_core(own)

    def gather(self, shard):
        planes = self.spread_planes(shard)
        col = self.gather_group(planes[1:2])
        row = self.gather_group(planes[0:1])
        return row, col, self.gather_group(planes[2:4])

    def reduce_group(self, keep, send, planes):
        got = self.over_core(send)

        def mine(*index):
            return keep[index].astype(F32) + got[index].astype(F32)

        from_x = self.over_x(mine(0, 1).astype(LOW)).astype(F32)
        from_y = self.over_y(mine(1, 1).astype(LOW)).astype(F32)
        first = mine(0, 0, 0) + from_x[0]
        second = mine(1, 0, 0) + from_y[0]
        first = first + self.over_y((mine(0, 0, 1) + from_x[1]).astype(LOW)).astype(F32)
        second = second + self.over_x((mine(1, 0, 1) + from_y[1]).astype(LOW)).astype(F32)
        partial_sum = jnp.concatenate([first, second], axis=1)
        return [self.reduce_plane(partial_sum[i], b) for i, b in enumerate(planes)]

    def reduce_plane(self, value, b):
        hub = 2 if b < 2 else 1
        near = self.over_z(value.astype(LOW), [(b ^ 1, b), (3 if hub == 2 else 0, hub)])
        value = value + near.astype(F32)
        return value + self.over_z(value.astype(LOW), [(hub, b)]).astype(F32)

    def reduce(self, row, col, forward):
        row = self.reduce_group(*row, (0,))
        col = self.reduce_group(*col, (1,))
        forward = self.reduce_group(*forward, (2, 3))
        return self.by_plane(row + col + forward)


class Native:
    axes = ("cols", "fsdp")

    def __init__(self):
        self.place = jnp.zeros((3,), jnp.int32)

    def gather(self, shard):
        full = lax.all_gather(shard, self.axes, axis=0, tiled=True)
        blocks = full.reshape(4, 2, 2, 2, 2, PART, D)
        first = blocks[:, :, :, :, 0].transpose(2, 1, 3, 0, 4, 5)
        second = blocks[:, :, :, :, 1].transpose(2, 3, 1, 0, 4, 5)
        cores = jnp.stack([first, second], axis=1)
        return [
            (cores[0][:, :, :, a:b], cores[1][:, :, :, a:b]) for a, b in ((0, 1), (1, 2), (2, 4))
        ]

    def reduce(self, row, col, forward):
        cores = jnp.stack(
            [jnp.concatenate([g[c] for g in (row, col, forward)], axis=3) for c in range(2)]
        )
        first = cores[:, 0].transpose(3, 2, 0, 1, 4, 5)
        second = cores[:, 1].transpose(3, 1, 0, 2, 4, 5)
        full = jnp.stack([first, second], axis=4).reshape(NMAT * D, D)
        return lax.psum_scatter(full, self.axes, scatter_dimension=0, tiled=True).astype(F32)


def neighbours(upward, downward):
    count = lax.axis_size("cols")
    forward = [(i, i + 1) for i in range(count - 1)]
    backward = [(target, source) for source, target in forward]
    return lax.ppermute(upward, "cols", forward), lax.ppermute(downward, "cols", backward)


def adamw(master, moment, square, grad_total, rate, decay, steps_done):
    moment_new = BETA_ONE * moment + (1.0 - BETA_ONE) * grad_total
    square_new = BETA_TWO * square + (1.0 - BETA_TWO) * grad_total * grad_total
    moment_fix = 1.0 - BETA_ONE**steps_done
    square_fix = 1.0 - BETA_TWO**steps_done
    update = moment_new / moment_fix / (jnp.sqrt(square_new / square_fix) + ADAM_EPS)
    return (master - rate * (update + decay * master), moment_new, square_new)


def band_mask(band_reach):
    first_col = lax.axis_index("cols") * CB
    col_total = CB * lax.axis_size("cols")
    query_pos = first_col + jnp.arange(CB, dtype=jnp.int32)
    key_pos = first_col - HALO + jnp.arange(EXT, dtype=jnp.int32)
    lowest = query_pos[None] - band_reach[:, 0]
    highest = query_pos[None] + band_reach[:, 1]
    key = key_pos[None, None]
    allowed = (key >= lowest[..., None]) & (key <= highest[..., None])
    allowed = allowed & (key >= 0) & (key < col_total)
    return allowed.astype(F32)


def layer(tokens, cot, counts, reach, place, weights, gain):
    row_w, col_w, forward_w = weights
    present = (jnp.arange(ROWS, dtype=jnp.int32)[None] < counts[:, None]).astype(F32)
    row_scale = DH ** (-0.5) * lax.rsqrt(counts.astype(F32))
    scalars = (jnp.concatenate([row_scale[:, None], present], axis=1), place)
    from_low, from_high = neighbours(tokens[:, CB - HALO :], tokens[:, :HALO])
    a1e, q, ke, ve, p1, o1, x1, a2 = call_row_forward(
        scalars, tokens, from_low, from_high, band_mask(reach), gain, row_w
    )
    q2, k2, v2, p2, o2, x2, a3 = call_col_forward(scalars, x1, a2, gain, col_w)
    out, e2, dg3, *forward_g = call_feed_forward(scalars, x2, a3, cot, gain, forward_w)
    e1, dg2, *col_g = call_col_backward(
        scalars, e2, o2, q2, k2, v2, p2, a2, x1, gain, col_w
    )
    dq, inner, to_low, to_high, *row_g = call_row_backward(
        scalars, e1, o1, q, ke, ve, p1, a1e, row_w
    )
    from_low, from_high = neighbours(to_high, to_low)
    grad, dg1 = call_input_backward(
        place, dq, inner, from_low, from_high, row_w, e1, tokens, gain
    )
    return out, grad, (row_g, col_g, forward_g), jnp.concatenate([dg1, dg2, dg3], axis=0)


def per_device(
    alignment,
    cotangent,
    row_counts,
    band_reach,
    master_weights,
    weight_moment,
    weight_square,
    norm_gains,
    gain_moment,
    gain_square,
):
    axes = ("cols", "fsdp")
    staged = lax.axis_size("cols") == NMAT and lax.axis_size("fsdp") == 2
    mover = Staged() if staged else Native()
    weights = mover.gather(master_weights.astype(LOW))
    gain = lax.all_gather(norm_gains.astype(LOW), axes, axis=0, tiled=True)
    out, grad, weight_grads, gain_grad = layer(
        alignment.reshape(SEQ, CB, D),
        cotangent.reshape(SEQ, CB, D),
        row_counts[:, 0],
        band_reach[:, 0],
        mover.place,
        weights,
        gain.astype(F32).reshape(3, D),
    )
    weight_total = mover.reduce(*weight_grads)
    gain_total = lax.psum_scatter(gain_grad.reshape(3 * D), axes, scatter_dimension=0, tiled=True)
    new_weights, new_moment, new_square = adamw(
        master_weights,
        weight_moment,
        weight_square,
        weight_total.reshape(master_weights.shape),
        D ** (-0.5),
        DECAY,
        STEP_NUMBER,
    )
    new_gains, new_gain_moment, new_gain_square = adamw(
        norm_gains, gain_moment, gain_square, gain_total, RATE_GAIN, 0.0, STEP_NUMBER
    )
    shape = (MB, 1, ROWS, CB, D)
    return (
        out.reshape(shape),
        grad.reshape(shape),
        new_weights,
        new_moment,
        new_square,
        new_weights.astype(LOW),
        new_gains,
        new_gain_moment,
        new_gain_square,
    )


def solution(mesh):
    tokens = P(None, "fsdp", None, "cols", None)
    rows = P(("cols", "fsdp"), None)
    flat = P(("cols", "fsdp"))
    in_specs = (
        tokens,
        tokens,
        P(None, "fsdp"),
        P(None, "fsdp", None, "cols"),
        rows,
        rows,
        rows,
        flat,
        flat,
        flat,
    )
    out_specs = (tokens, tokens, rows, rows, rows, rows, flat, flat, flat)
    return jax.shard_map(
        per_device, mesh=mesh, in_specs=in_specs, out_specs=out_specs, check_vma=False
    )
```

```python
from functools import partial

import jax
import jax.numpy as jnp
from jax import lax
from jax.experimental import pallas as pl
from jax.experimental.pallas import tpu as pltpu
from jax.sharding import PartitionSpec as P

D = 768
H = 12
DH = 64
FF = 3072
NMAT = 16
ROWS = 4
CB = 64
HALO = 32
MB = 2
EXT = CB + 2 * HALO
SEQ = MB * ROWS
TOK = SEQ * CB
PAIRS = H // 2
LANES = 128
FOLD = FF // D
SPAN = D // 2
PART = SPAN // 2

EPS = 1e-05
BETA_ONE = 0.9
BETA_TWO = 0.999
ADAM_EPS = 1e-08
DECAY = 0.01
RATE_GAIN = 0.3
STEP_NUMBER = 10.0
MASKED = -1e30
F32 = jnp.float32
LOW = jnp.bfloat16


def dot_nn(a, b):
    return lax.dot_general(a, b, (((1,), (0,)), ((), ())), preferred_element_type=F32)


def dot_nt(a, b):
    return lax.dot_general(a, b, (((1,), (1,)), ((), ())), preferred_element_type=F32)


def dot_tn(a, b):
    return lax.dot_general(a, b, (((0,), (0,)), ((), ())), preferred_element_type=F32)


def standardize(values):
    center = values - jnp.mean(values, axis=-1, keepdims=True)
    spread = lax.rsqrt(jnp.mean(center * center, axis=-1, keepdims=True) + EPS)
    return center * spread, spread


def norm_pull(upward, values, gain):
    scaled, spread = standardize(values)
    weighted = upward * gain
    result = spread * (
        weighted
        - jnp.mean(weighted, axis=-1, keepdims=True)
        - scaled * jnp.mean(weighted * scaled, axis=-1, keepdims=True)
    )
    return result, jnp.sum(upward * scaled, axis=0, keepdims=True)


def lane_window(pair):
    return pl.ds(pl.multiple_of(pair * LANES, LANES), LANES)


def side_by_side(ref, micro, window):
    return jnp.concatenate([ref[micro * ROWS + r, :, window] for r in range(ROWS)], axis=1)


def head_stack(packed):
    lane = lax.broadcasted_iota(jnp.int32, packed.shape, 1)
    first = (lane % LANES) < DH
    zero = jnp.zeros_like(packed)
    return jnp.concatenate([jnp.where(first, packed, zero), jnp.where(first, zero, packed)], axis=0)


def head_merge(stacked, r):
    block = stacked[:, r * LANES : (r + 1) * LANES]
    lane = lax.broadcasted_iota(jnp.int32, (CB, LANES), 1)
    return jnp.where(lane < DH, block[:CB], block[CB:])


def head_sums():
    feature = lax.broadcasted_iota(jnp.int32, (D, LANES), 0)
    head = lax.broadcasted_iota(jnp.int32, (D, LANES), 1)
    return (feature // DH == head).astype(F32).astype(LOW)


def head_spread():
    head = lax.broadcasted_iota(jnp.int32, (LANES, D), 0)
    feature = lax.broadcasted_iota(jnp.int32, (LANES, D), 1)
    return (feature // DH == head).astype(F32).astype(LOW)


def fetch_matrix(place, sources, table, matrix, target, sems, base):
    y_rel = jnp.where(place[1] == matrix // 2, 0, 1)
    waits = []
    for x in range(2):
        x_rel = jnp.where(place[0] == x, 0, 1)
        block = 2 * y_rel + x_rel
        rows = target.at[pl.ds(x * SPAN, SPAN)]
        for index in sorted(set(table)):
            here = None
            for plane, chosen in enumerate(table):
                if chosen == index:
                    hit = place[3] == plane
                    here = hit if here is None else jnp.logical_or(here, hit)
            for core_rel in range(2):
                held = jnp.logical_and(here, place[2] == (matrix % 2) ^ core_rel)
                sides, corner = sources[4 * index + 2 * core_rel : 4 * index + 2 * core_rel + 2]
                side = jnp.minimum(block, 2)
                near = pltpu.make_async_copy(sides.at[side], rows, sems.at[base + x])
                far = pltpu.make_async_copy(corner, rows, sems.at[base + x])
                pl.when(jnp.logical_and(held, block < 3))(near.start)
                pl.when(jnp.logical_and(held, block == 3))(far.start)
        waits.append(far)
    return waits


def fetch(place, sources, table, matrices, w, sems, first=0):
    waits = []
    for slot, matrix in enumerate(matrices):
        slot += first
        waits.append(
            fetch_matrix(place, sources, table, matrix, w.at[slot], sems, 2 * slot)
        )
    return waits


def settle(waits):
    for copy in waits:
        copy.wait()


def emit_matrix(place, source, matrix, n, keep, send, sems, base):
    core_same = place[2] == matrix % 2
    y_rel = jnp.where(place[1] == matrix // 2, 0, 1)
    waits = []
    for x in range(2):
        x_rel = jnp.where(place[0] == x, 0, 1)
        block = source.at[pl.ds(x * SPAN, SPAN)]
        kept = pltpu.make_async_copy(block, keep.at[y_rel, x_rel, n], sems.at[base + x])
        sent = pltpu.make_async_copy(block, send.at[y_rel, x_rel, n], sems.at[base + x])
        pl.when(core_same)(kept.start)
        pl.when(jnp.logical_not(core_same))(sent.start)
        waits.append(kept)
    return waits


def row_project(
    table, count, scal, place, tokens, from_low, from_high, gain, *refs
):
    sources, (a1e, q, ke, ve, w, sems) = refs[:count], refs[count:]
    copies = fetch(place, sources, table, range(3), w, sems)

    def norm_step(i, _):
        for source, start, size in (
            (from_low, 0, HALO),
            (tokens, HALO, CB),
            (from_high, HALO + CB, HALO),
        ):
            scaled, _s = standardize(source[i].astype(F32))
            a1e[i, start : start + size] = (scaled * gain[0:1]).astype(LOW)
        return 0

    lax.fori_loop(0, SEQ, norm_step, 0)
    wide = a1e[...].reshape(SEQ * EXT, D)
    settle(copies[1])
    ke[...] = dot_nn(wide, w[1]).astype(LOW).reshape(SEQ, EXT, D)
    settle(copies[2])
    ve[...] = dot_nn(wide, w[2]).astype(LOW).reshape(SEQ, EXT, D)
    inner = a1e[:, HALO : HALO + CB, :].reshape(TOK, D)
    settle(copies[0])
    q[...] = dot_nn(inner, w[0]).astype(LOW).reshape(SEQ, CB, D)
    for i in range(SEQ):
        q[i] = (q[i].astype(F32) * scal[i // ROWS, 1 + i % ROWS]).astype(LOW)


def row_attend(
    table, count, scal, place, tokens, q, ke, ve, allowed, gain, *refs
):
    sources, (p1, o1, x1, a2, w, sems) = refs[:count], refs[count:]
    copies = fetch(place, sources, table, (3,), w, sems)

    def attend(pair, _):
        window = lane_window(pair)
        for m in range(MB):
            query = head_stack(side_by_side(q, m, window))
            scores = dot_nt(query, side_by_side(ke, m, window)) * scal[m, 0]
            mask = allowed[m]
            mask = jnp.concatenate([mask, mask], axis=0)
            scores = jnp.where(mask > 0, scores, MASKED)
            weight = jnp.exp(scores - jnp.max(scores, axis=-1, keepdims=True))
            prob = weight / jnp.sum(weight, axis=-1, keepdims=True)
            p1[m, pair] = prob
            mixed = dot_nn(prob.astype(LOW), side_by_side(ve, m, window))
            for r in range(ROWS):
                o1[m * ROWS + r, :, window] = head_merge(mixed, r).astype(LOW)
        return 0

    lax.fori_loop(0, PAIRS, attend, 0)
    settle(copies[0])
    x1[...] = tokens[...].astype(F32) + dot_nn(o1[...].reshape(TOK, D), w[0]).reshape(SEQ, CB, D)

    def next_norm(i, _):
        scaled, _s = standardize(x1[i])
        a2[i] = (scaled * gain[1:2]).astype(LOW)
        return 0

    lax.fori_loop(0, SEQ, next_norm, 0)


def col_forward(table, count, scal, place, x1, a2, gain, *refs):
    sources, (q2, k2, v2, p2, o2, x2, a3, w, sems) = refs[:count], refs[count:]
    copies = fetch(place, sources, table, range(4), w, sems)
    for j in range(3):
        settle(copies[j])
    flat = a2[...].reshape(TOK, D)
    q2[...] = dot_nn(flat, w[0]).astype(LOW).reshape(SEQ, CB, D)
    k2[...] = dot_nn(flat, w[1]).astype(LOW).reshape(SEQ, CB, D)
    v2[...] = dot_nn(flat, w[2]).astype(LOW).reshape(SEQ, CB, D)
    sums = head_sums()
    spread = head_spread()

    def attend(i, _):
        micro = i // ROWS
        query = q2[i].astype(F32)
        products = jnp.concatenate(
            [(query * k2[micro * ROWS + s].astype(F32)).astype(LOW) for s in range(ROWS)], axis=0
        )
        scores = dot_nn(products, sums) * (DH ** (-0.5))
        parts = [
            jnp.where(scal[micro, 1 + s] > 0, scores[s * CB : (s + 1) * CB], MASKED)
            for s in range(ROWS)
        ]
        top = jnp.maximum(jnp.maximum(parts[0], parts[1]), jnp.maximum(parts[2], parts[3]))
        parts = [jnp.exp(part - top) for part in parts]
        scale = 1.0 / (parts[0] + parts[1] + parts[2] + parts[3])
        prob = jnp.concatenate([part * scale for part in parts], axis=0)
        p2[i] = prob
        wide = dot_nn(prob.astype(LOW), spread)
        total = wide[:CB] * v2[micro * ROWS].astype(F32)
        for s in range(1, ROWS):
            total = total + wide[s * CB : (s + 1) * CB] * v2[micro * ROWS + s].astype(F32)
        o2[i] = total.astype(LOW)
        return 0

    lax.fori_loop(0, SEQ, attend, 0)
    settle(copies[3])
    x2[...] = x1[...] + dot_nn(o2[...].reshape(TOK, D), w[3]).reshape(SEQ, CB, D)

    def next_norm(i, _):
        scaled, _s = standardize(x2[i])
        a3[i] = (scaled * gain[2:3]).astype(LOW)
        return 0

    lax.fori_loop(0, SEQ, next_norm, 0)


CHUNK = 128


def feed_forward(tables, count, scal, place, x2, a3, cot, gain, *refs):
    sources, refs = refs[:count], refs[count:]
    out, e2, dgain, keep, send, up, down, live_cot, gl, dhd, w, dw, in_sems, out_sems = refs
    copies = []
    for n in range(2):
        copies += fetch(place, sources, tables[n], range(4), w, in_sems, 4 * n)
    for i in range(SEQ):
        live_cot[i * CB : (i + 1) * CB] = (
            cot[i].astype(F32) * scal[i // ROWS, 1 + i % ROWS]
        ).astype(LOW)
    normed = a3[...].reshape(TOK, D)
    grad = live_cot[...]
    waits = []
    for step in range(FOLD):
        settle(copies[step])
        settle(copies[FOLD + step])
        win = w[step]
        wout = w[FOLD + step]
        for base in range(0, TOK, CHUNK):
            rows = slice(base, base + CHUNK)
            hidden = dot_nn(normed[rows], win)
            pulled = dot_nt(grad[rows], wout)
            half = 0.5 * lax.erf(hidden * (0.5**0.5)) + 0.5
            gl[rows] = (hidden * half).astype(LOW)
            slope = half + hidden * (jnp.exp(-0.5 * hidden * hidden) * ((2.0 * jnp.pi) ** -0.5))
            dhd[rows] = (pulled * slope).astype(LOW)
        for n, value in enumerate((dot_tn(normed, dhd[...]), dot_tn(gl[...], grad))):
            slot = 4 * n + step
            dw[slot] = value.astype(LOW)
            waits += emit_matrix(place, dw.at[slot], step, n, keep, send, out_sems, 2 * slot)
        forward = dot_nn(gl[...], wout)
        backward = dot_nt(dhd[...], win)
        if step == 0:
            up[...] = forward
            down[...] = backward
        else:
            up[...] += forward
            down[...] += backward
    total = jnp.zeros((1, D), F32)
    for i in range(SEQ):
        rows = slice(i * CB, (i + 1) * CB)
        value = x2[i]
        out[i] = ((value + up[rows]) * scal[i // ROWS, 1 + i % ROWS]).astype(LOW)
        part, gain_part = norm_pull(down[rows], value, gain[2:3])
        e2[i] = live_cot[rows].astype(F32) + part
        total = total + gain_part
    dgain[...] = total
    settle(waits)


def col_attend_back(table, count, scal, place, e2, q2, k2, v2, p2, *refs):
    sources, refs = refs[:count], refs[count:]
    dq2, dk2, dv2, do2, dka, dva, w, in_sems = refs
    copies = fetch(place, sources, table, (3,), w, in_sems)
    low = e2[...].reshape(TOK, D).astype(LOW)
    settle(copies[0])
    do2[...] = dot_nt(low, w[0]).astype(LOW).reshape(SEQ, CB, D)
    sums = head_sums()
    spread = head_spread()
    dka[...] = jnp.zeros_like(dka)
    dva[...] = jnp.zeros_like(dva)

    def pull(i, _):
        micro = i // ROWS
        upward = do2[i].astype(F32)
        products = jnp.concatenate(
            [(upward * v2[micro * ROWS + s].astype(F32)).astype(LOW) for s in range(ROWS)], axis=0
        )
        dprob = dot_nn(products, sums)
        prob = p2[i]
        mixed = prob * dprob
        inner = mixed[:CB] + mixed[CB : 2 * CB] + mixed[2 * CB : 3 * CB] + mixed[3 * CB :]
        dscore = prob * (dprob - jnp.concatenate([inner] * ROWS, axis=0))
        wide = dot_nn(prob.astype(LOW), spread)
        dwide = dot_nn(dscore.astype(LOW), spread)
        query = q2[i].astype(F32)
        total = jnp.zeros((CB, D), F32)
        for s in range(ROWS):
            rows = slice(s * CB, (s + 1) * CB)
            total = total + dwide[rows] * k2[micro * ROWS + s].astype(F32)
            dka[micro * ROWS + s] += dwide[rows] * query
            dva[micro * ROWS + s] += wide[rows] * upward
        dq2[i] = (total * (DH ** (-0.5))).astype(LOW)
        return 0

    lax.fori_loop(0, SEQ, pull, 0)
    dk2[...] = (dka[...] * (DH ** (-0.5))).astype(LOW)
    dv2[...] = dva[...].astype(LOW)


def col_project_back(table, count, scal, place, e2, o2, dq2, dk2, dv2, a2, x1, gain, *refs):
    sources, refs = refs[:count], refs[count:]
    e1, dgain, keep, send, acc, w, dw, in_sems, out_sems = refs
    copies = fetch(place, sources, table, range(3), w, in_sems)
    flat = a2[...].reshape(TOK, D)
    low = e2[...].reshape(TOK, D).astype(LOW)
    dw[3] = dot_tn(o2[...].reshape(TOK, D), low).astype(LOW)
    waits = emit_matrix(place, dw.at[3], 3, 0, keep, send, out_sems, 6)
    for j, ref in enumerate((dq2, dk2, dv2)):
        grads = ref[...].reshape(TOK, D)
        dw[j] = dot_tn(flat, grads).astype(LOW)
        waits += emit_matrix(place, dw.at[j], j, 0, keep, send, out_sems, 2 * j)
        settle(copies[j])
        part = dot_nt(grads, w[j]).reshape(SEQ, CB, D)
        if j == 0:
            acc[...] = part
        else:
            acc[...] += part
    gain_total = jnp.zeros((1, D), F32)
    for i in range(SEQ):
        part, gain_part = norm_pull(acc[i], x1[i], gain[1:2])
        e1[i] = e2[i] + part
        gain_total = gain_total + gain_part
    dgain[...] = gain_total
    settle(waits)


def row_backward(table, count, scal, place, e1, o1, q, ke, ve, p1, a1e, *refs):
    sources, refs = refs[:count], refs[count:]
    dq, inner, to_low, to_high, keep, send, do1, dke, dve, w, dw, in_sems, out_sems = refs
    copies = fetch(place, sources, table, (3,), w, in_sems)
    low = e1[...].reshape(TOK, D).astype(LOW)
    settle(copies[0])
    do1[...] = dot_nt(low, w[0]).astype(LOW).reshape(SEQ, CB, D)

    def pull(pair, _):
        window = lane_window(pair)
        for m in range(MB):
            query = head_stack(side_by_side(q, m, window))
            upward = head_stack(side_by_side(do1, m, window))
            prob = p1[m, pair]
            dprob = dot_nt(upward, side_by_side(ve, m, window))
            dscore = prob * (dprob - jnp.sum(prob * dprob, axis=-1, keepdims=True))
            dscore = dscore.astype(LOW)
            dvalue = dot_tn(prob.astype(LOW), upward)
            dkey = dot_tn(dscore, query) * scal[m, 0]
            dquery = dot_nn(dscore, side_by_side(ke, m, window)) * scal[m, 0]
            for r in range(ROWS):
                lanes = slice(r * LANES, (r + 1) * LANES)
                dve[m * ROWS + r, :, window] = dvalue[:, lanes].astype(LOW)
                dke[m * ROWS + r, :, window] = dkey[:, lanes].astype(LOW)
                dq[m * ROWS + r, :, window] = (head_merge(dquery, r) * scal[m, 1 + r]).astype(LOW)
        return 0

    lax.fori_loop(0, PAIRS, pull, 0)
    for j, ref in enumerate((dke, dve)):
        inner[j] = ref[:, HALO : HALO + CB, :]
        to_low[j] = ref[:, :HALO, :]
        to_high[j] = ref[:, HALO + CB :, :]
    wide = a1e[...].reshape(SEQ * EXT, D)
    own = a1e[:, HALO : HALO + CB, :].reshape(TOK, D)
    waits = []
    for j, (left, right) in enumerate(
        (
            (own, dq[...].reshape(TOK, D)),
            (wide, dke[...].reshape(SEQ * EXT, D)),
            (wide, dve[...].reshape(SEQ * EXT, D)),
            (o1[...].reshape(TOK, D), low),
        )
    ):
        dw[j] = dot_tn(left, right).astype(LOW)
        waits += emit_matrix(place, dw.at[j], j, 0, keep, send, out_sems, 2 * j)
    settle(waits)


def input_backward(
    table, count, scal, place, dq, inner, from_low, from_high, e1, tokens, gain, *refs
):
    sources, (grad, dgain, full, acc, w, sems) = refs[:count], refs[count:]
    copies = fetch(place, sources, table, range(3), w, sems)
    for j in range(2):
        full[j, :, :HALO] = (
            inner[j, :, :HALO].astype(F32) + from_low[j].astype(F32)
        ).astype(LOW)
        full[j, :, HALO:] = (
            inner[j, :, HALO:].astype(F32) + from_high[j].astype(F32)
        ).astype(LOW)
    for j in range(3):
        settle(copies[j])
    acc[...] = dot_nt(dq[...].reshape(TOK, D), w[0]).reshape(SEQ, CB, D)
    for j in range(2):
        acc[...] += dot_nt(full[j].reshape(TOK, D), w[1 + j]).reshape(SEQ, CB, D)
    gain_total = jnp.zeros((1, D), F32)
    for i in range(SEQ):
        part, gain_part = norm_pull(acc[i], tokens[i].astype(F32), gain[0:1])
        grad[i] = (e1[i] + part).astype(LOW)
        gain_total = gain_total + gain_part
    dgain[...] = gain_total


def in_vmem(count):
    return [pl.BlockSpec(memory_space=pltpu.VMEM)] * count


def like(*shapes):
    return tuple(jax.ShapeDtypeStruct(shape, dtype) for shape, dtype in shapes)


SEQ_CB = (SEQ, CB, D)
SEQ_EXT = (SEQ, EXT, D)
RIM = (2, SEQ, HALO, D)
PER_MICRO = 1.15e9
VM = pltpu.VMEM
DMA = pltpu.SemaphoreType.DMA


def pieces(count):
    return (2, 2, count, SPAN, D)


def run_kernel(body, scalars, args, weights, outs, raw_out, scratch, micros):
    vmem = pl.BlockSpec(memory_space=pltpu.VMEM)
    raw = pl.BlockSpec(memory_space=pltpu.HBM)
    moved = sum(a.size * a.dtype.itemsize for a in args)
    moved += sum(o.size * jnp.dtype(o.dtype).itemsize for o in outs)
    call = body
    sources = ()
    if weights is not None:
        table, sources = weights
        call = partial(body, table, len(sources))
    return pl.pallas_call(
        call,
        name=body.__name__,
        out_shape=outs,
        in_specs=[pl.BlockSpec(memory_space=pltpu.SMEM)] * len(scalars)
        + [vmem] * len(args)
        + [raw] * len(sources),
        out_specs=tuple(raw if i in raw_out else vmem for i in range(len(outs))),
        scratch_shapes=scratch,
        compiler_params=pltpu.CompilerParams(vmem_limit_bytes=60 << 20),
        cost_estimate=pl.CostEstimate(
            flops=int(micros * PER_MICRO), bytes_accessed=moved, transcendentals=0
        ),
    )(*scalars, *args, *sources)


def held(count):
    return [VM((count, D, D), LOW), DMA((2 * count,))]


def terms(count):
    return [VM((count, D, D), LOW), DMA((2 * count,))]


def swap_pairs(count, bit):
    return [(i, i ^ bit) for i in range(count)]


def after(value, *before):
    return lax.optimization_barrier((value, *before))[0]


def add(*parts):
    total = parts[0].astype(F32)
    for part in parts[1:]:
        total = total + part.astype(F32)
    return total


def add_half(block, half, arrived):
    first, second = block[:, :PART], block[:, PART:]
    if half == 0:
        first = first + arrived.astype(F32)
    else:
        second = second + arrived.astype(F32)
    return jnp.concatenate([first, second], axis=1)


def together(*values):
    return lax.optimization_barrier(values)


def held_by(side, corner):
    return (side[0], corner[0], side[1], corner[1])


class Staged:
    planes = 4
    tables = ((0, 1, 2, 2), (1, 0, 1, 3), (2, 2, 0, 1), (3, 3, 3, 0))

    def __init__(self):
        self.count = NMAT
        self.step = NMAT // self.planes
        cols = lax.axis_index("cols")
        self.z = cols // self.step
        self.place = jnp.stack(
            [lax.axis_index("fsdp"), (cols // 2) % 2, cols % 2, self.z]
        ).astype(jnp.int32)

    def over_x(self, value):
        return lax.ppermute(value, "fsdp", [(0, 1), (1, 0)])

    def over_y(self, value):
        return lax.ppermute(value, "cols", swap_pairs(self.count, 2))

    def over_core(self, value):
        return lax.ppermute(value, "cols", swap_pairs(self.count, 1))

    def over_z(self, value, pairs):
        step = self.step
        full = [(a * step + i, b * step + i) for a, b in pairs for i in range(step)]
        return lax.ppermute(value, "cols", full)

    def by_plane(self, options):
        result = options[-1]
        for index in range(len(options) - 2, -1, -1):
            result = jnp.where(self.z == index, options[index], result)
        return result

    def own_place(self, gains):
        index = lax.axis_index("cols") * 2 + lax.axis_index("fsdp")
        spread = jnp.zeros((3 * D,), F32)
        spread = lax.dynamic_update_slice(spread, gains, (index * gains.shape[0],))
        return spread.reshape(18, LANES)

    def sum_step(self, value, index):
        swaps = (
            self.over_core,
            self.over_x,
            self.over_y,
            lambda v: self.over_z(v, [(0, 1), (1, 0), (2, 3), (3, 2)]),
            lambda v: self.over_z(v, [(0, 2), (2, 0), (1, 3), (3, 1)]),
        )
        return value + swaps[index](value)

    def sum_gains(self, value):
        value = value.reshape(18, LANES)
        for index in range(5):
            value = self.sum_step(value, index)
        return value.reshape(3 * D)

    def own_gains(self, value, size):
        index = lax.axis_index("cols") * 2 + lax.axis_index("fsdp")
        return lax.dynamic_slice(self.sum_gains(value), (index * size,), (size,))

    def collect(self, *blocks):
        own = jnp.stack(blocks)
        return own, self.over_core(own)

    def corner(self, corner_a, corner_b):
        own = jnp.concatenate([corner_a, corner_b], axis=0)
        return own, self.over_core(own)

    def gather(self, shard, gains, tokens):
        z = self.z
        gains = self.own_place(gains)
        up1 = self.over_z(shard, [(0, 1), (1, 2), (2, 3)])
        down1 = self.over_z(shard, [(3, 2), (2, 1), (1, 0)])
        x1, y1 = self.over_x(shard), self.over_y(shard)
        gains = self.sum_step(gains, 0)
        up1, down1, x1, y1, gains = together(up1, down1, x1, y1, gains)
        second = jnp.where(z == 0, down1, up1)
        x2, y2 = self.over_x(second), self.over_y(second)
        a1, b1 = self.over_y(x1[:PART]), self.over_x(y1[PART:])
        up2 = self.over_z(up1, [(1, 2), (2, 3)])
        down2 = self.over_z(down1, [(2, 1), (1, 0)])
        gains = self.sum_step(gains, 1)
        up2, down2, a1, b1, x2, y2, gains = together(up2, down2, a1, b1, x2, y2, gains)
        side1 = self.collect(shard, x1, y1)
        up3 = self.over_z(up2, [(2, 3)])
        down3 = self.over_z(down2, [(1, 0)])
        a2, b2 = self.over_y(x2[:PART]), self.over_x(y2[PART:])
        rims = neighbours(*after((tokens[:, CB - HALO :], tokens[:, :HALO]), x2))
        gains = self.sum_step(gains, 2)
        up3, down3, a2, b2, gains, *rims = together(up3, down3, a2, b2, gains, *rims)
        third = self.by_plane([down2, down1, up2, up3])
        x3, y3 = self.over_x(third), self.over_y(third)
        gains = self.sum_step(gains, 3)
        corner1 = self.corner(a1, b1)
        side2 = self.collect(second, x2, y2)
        x3, y3, gains = together(x3, y3, gains)
        a3, b3 = self.over_y(x3[:PART]), self.over_x(y3[PART:])
        gains = self.sum_step(gains, 4)
        corner2 = self.corner(a2, b2)
        side3 = self.collect(third, x3, y3)
        fourth = self.by_plane([down3, down2, down1, up2])
        a3, b3, fourth, gains = together(a3, b3, fourth, gains)
        x4, y4 = self.over_x(fourth), self.over_y(fourth)
        corner3 = self.corner(a3, b3)
        self.row_gate = (fourth,)
        self.fourth = fourth, x4, y4
        first3 = (
            *held_by(side1, corner1),
            *held_by(side2, corner2),
            *held_by(side3, corner3),
        )
        self.first3 = first3
        return (self.tables[0], first3), gains.reshape(3 * D), rims

    def gather_last(self, seen):
        fourth, x4, y4 = self.fourth
        x4, y4, seen = together(x4, y4, seen)
        xa, yb = x4[:PART], y4[PART:]
        self.attend_gate = (xa, yb)
        a4, b4 = self.over_y(xa), self.over_x(yb)
        side4 = self.collect(fourth, x4, y4)
        corner4 = self.corner(a4, b4)
        every = (*self.first3, *held_by(side4, corner4))
        return (self.tables[1], every), (self.tables[2:], every)

    def corner_swap(self, keep, got):
        mixed = add(keep[1, 1], got[1, 1]).astype(LOW)
        return mixed[:, :PART], mixed[:, PART:]

    def side_blocks(self, keep, got, corner_a, corner_b):
        over_x = add_half(add(keep[0, 1], got[0, 1]), 0, corner_a).astype(LOW)
        over_y = add_half(add(keep[1, 0], got[1, 0]), 1, corner_b).astype(LOW)
        return over_x, over_y

    def plane_sum(self, value, b):
        hub = 2 if b < 2 else 1
        near = self.over_z(value.astype(LOW), [(b ^ 1, b), (3 if hub == 2 else 0, hub)])
        value = add(value, near)
        return add(value, self.over_z(value.astype(LOW), [(hub, b)]))

    def reduce_forward(self, keep, send):
        self.fwd_keep = keep
        self.fwd_got = self.over_core(send)
        self.fwd_corner = self.corner_swap(keep, self.fwd_got)
        return self.fwd_corner

    def reduce_forward_sides(self):
        a, b = self.fwd_corner
        self.fwd_sides = self.side_blocks(
            self.fwd_keep, self.fwd_got, self.over_y(a), self.over_x(b)
        )
        return self.fwd_sides

    def reduce_col(self, keep, send):
        self.col_keep = keep
        self.col_got = self.over_core(send)

    def reduce_col_corner(self, *before):
        got = after(self.col_got, *before)
        self.col_corner = self.corner_swap(self.col_keep, got)
        return self.col_corner

    def reduce_rest(self, keep, send):
        fx, fy = self.fwd_sides
        fx, fy = self.over_x(fx), self.over_y(fy)
        got = self.over_core(send)
        a, b = self.col_corner
        cx, cy = self.side_blocks(self.col_keep, self.col_got, self.over_y(a), self.over_x(b))
        cx, cy = self.over_x(cx), self.over_y(cy)
        a, b = self.corner_swap(keep, got)
        self.rim_gate = (a, b)
        rx, ry = self.side_blocks(keep, got, self.over_y(a), self.over_x(b))
        forward = add(self.fwd_keep[0, 0], self.fwd_got[0, 0], fx, fy)
        col = add(self.col_keep[0, 0], self.col_got[0, 0], cx, cy)
        rx, ry = self.over_x(rx), self.over_y(ry)
        row = add(keep[0, 0], got[0, 0], rx, ry)
        return self.by_plane(
            [
                self.plane_sum(row[0], 0),
                self.plane_sum(col[0], 1),
                self.plane_sum(forward[0], 2),
                self.plane_sum(forward[1], 3),
            ]
        )


class Native:
    axes = ("cols", "fsdp")
    row_gate = ()
    attend_gate = ()
    rim_gate = ()
    last_gate = ()

    def __init__(self):
        self.place = jnp.zeros((4,), jnp.int32)
        self.parts = []

    def own_gains(self, value, size):
        return lax.psum_scatter(value, self.axes, scatter_dimension=0, tiled=True)

    def gather(self, shard, gains, tokens):
        full = lax.all_gather(shard, self.axes, axis=0, tiled=True)
        gains = lax.all_gather(gains, self.axes, axis=0, tiled=True)
        rims = neighbours(tokens[:, CB - HALO :], tokens[:, :HALO])
        row, *self.rest = self.arranged(full)
        return row, gains, rims

    def gather_last(self, seen):
        return self.rest

    def arranged(self, full):
        blocks = full.reshape(4, 2, 2, 2 * SPAN, D).transpose(0, 2, 1, 3, 4)
        blocks = blocks.reshape(4, 2, 4, SPAN, D)
        row, col, low, high = [
            (blocks[b, 0, :3], blocks[b, 0, 3], blocks[b, 1, :3], blocks[b, 1, 3])
            for b in range(4)
        ]
        flat = (0, 0, 0, 0)
        return (flat, row), (flat, col), ((flat, (1, 1, 1, 1)), (*low, *high))

    def reduce_forward(self, keep, send):
        self.parts = [jnp.stack([keep, send], axis=1).transpose(3, 0, 1, 2, 4, 5)]
        return ()

    def reduce_forward_sides(self):
        return ()

    def reduce_col(self, keep, send):
        self.parts.insert(0, jnp.stack([keep, send], axis=1).transpose(3, 0, 1, 2, 4, 5))

    def reduce_col_corner(self, *before):
        return ()

    def reduce_rest(self, keep, send):
        self.parts.insert(0, jnp.stack([keep, send], axis=1).transpose(3, 0, 1, 2, 4, 5))
        full = jnp.concatenate(self.parts, axis=0).reshape(NMAT * D, D)
        return lax.psum_scatter(full, self.axes, scatter_dimension=0, tiled=True).astype(F32)


def neighbours(upward, downward):
    count = lax.axis_size("cols")
    forward = [(i, i + 1) for i in range(count - 1)]
    backward = [(target, source) for source, target in forward]
    return lax.ppermute(upward, "cols", forward), lax.ppermute(downward, "cols", backward)


def adamw(master, moment, square, grad_total, rate, decay, steps_done):
    moment_new = BETA_ONE * moment + (1.0 - BETA_ONE) * grad_total
    square_new = BETA_TWO * square + (1.0 - BETA_TWO) * grad_total * grad_total
    moment_fix = 1.0 - BETA_ONE**steps_done
    square_fix = 1.0 - BETA_TWO**steps_done
    update = moment_new / moment_fix / (jnp.sqrt(square_new / square_fix) + ADAM_EPS)
    return (master - rate * (update + decay * master), moment_new, square_new)


def band_mask(band_reach):
    first_col = lax.axis_index("cols") * CB
    col_total = CB * lax.axis_size("cols")
    query_pos = first_col + jnp.arange(CB, dtype=jnp.int32)
    key_pos = first_col - HALO + jnp.arange(EXT, dtype=jnp.int32)
    lowest = query_pos[None] - band_reach[:, 0]
    highest = query_pos[None] + band_reach[:, 1]
    key = key_pos[None, None]
    allowed = (key >= lowest[..., None]) & (key <= highest[..., None])
    allowed = allowed & (key >= 0) & (key < col_total)
    return allowed.astype(F32)


def layer(tokens, cot, counts, reach, mover, shard, gains):
    row_w, gain, rims = mover.gather(shard, gains, tokens)
    gain = gain.reshape(3, D)
    from_low, from_high = rims
    present = (jnp.arange(ROWS, dtype=jnp.int32)[None] < counts[:, None]).astype(F32)
    row_scale = DH ** (-0.5) * lax.rsqrt(counts.astype(F32))
    scalars = (jnp.concatenate([row_scale[:, None], present], axis=1), mover.place)
    run = partial(run_kernel, scalars=scalars)
    low, wide = (SEQ_CB, LOW), (SEQ_EXT, LOW)
    term = (pieces(1), LOW)
    row_gain = ((1, D), F32)
    probs = ((MB, PAIRS, 2 * CB, EXT), F32)
    col_probs = ((SEQ, ROWS * CB, LANES), F32)

    a1e, q, ke, ve = run(
        row_project,
        args=(after(tokens, *mover.row_gate), from_low, from_high, gain),
        weights=row_w,
        outs=like(wide, low, wide, wide),
        raw_out=(),
        scratch=held(3),
        micros=9.5,
    )
    col_w, forward_w = mover.gather_last(q)
    p1, o1, x1, a2 = run(
        row_attend,
        args=(tokens, after(q, *mover.attend_gate), ke, ve, band_mask(reach), gain),
        weights=row_w,
        outs=like(probs, low, (SEQ_CB, F32), low),
        raw_out=(),
        scratch=held(1),
        micros=12.5,
    )
    q2, k2, v2, p2, o2, x2, a3 = run(
        col_forward,
        args=(x1, a2, gain),
        weights=col_w,
        outs=like(low, low, low, col_probs, low, (SEQ_CB, F32), low),
        raw_out=(),
        scratch=held(4),
        micros=15.5,
    )
    token = (TOK, D)
    out, e2, dg3, *forward_g = run(
        feed_forward,
        args=(x2, a3, cot, gain),
        weights=forward_w,
        outs=like(low, (SEQ_CB, F32), row_gain, (pieces(2), LOW), (pieces(2), LOW)),
        raw_out=(3, 4),
        scratch=[VM(token, F32)] * 2 + [VM(token, LOW)] * 3 + [held(8)[0], terms(8)[0]]
        + [DMA((16,))] * 2,
        micros=26,
    )
    gate = mover.reduce_forward(*forward_g)
    dq2, dk2, dv2 = run(
        col_attend_back,
        args=(e2, q2, k2, v2, p2),
        weights=col_w,
        outs=like(low, low, low),
        raw_out=(),
        scratch=[VM(SEQ_CB, LOW)] + [VM(SEQ_CB, F32)] * 2 + held(1),
        micros=10.5,
    )
    dq2 = after(dq2, *gate)
    e1, dg2, *col_g = run(
        col_project_back,
        args=(e2, o2, dq2, dk2, dv2, a2, x1, gain),
        weights=col_w,
        outs=like((SEQ_CB, F32), row_gain, term, term),
        raw_out=(2, 3),
        scratch=[VM(SEQ_CB, F32), held(3)[0], terms(4)[0], DMA((6,)), DMA((8,))],
        micros=11.5,
    )
    mover.reduce_col(*col_g)
    gate = mover.reduce_forward_sides()
    gate = (*gate, *mover.reduce_col_corner())
    dq, inner, to_low, to_high, *row_g = run(
        row_backward,
        args=(after(e1, *gate), o1, q, ke, ve, p1, a1e),
        weights=row_w,
        outs=like(low, ((2, *SEQ_CB), LOW), (RIM, LOW), (RIM, LOW), term, term),
        raw_out=(4, 5),
        scratch=[VM(SEQ_CB, LOW)] + [VM(SEQ_EXT, LOW)] * 2
        + [held(1)[0], terms(4)[0], DMA((2,)), DMA((8,))],
        micros=20,
    )
    weight_grad = mover.reduce_rest(*row_g)
    to_high = after(to_high, *mover.rim_gate)
    to_low = after(to_low, *mover.rim_gate)
    from_low, from_high = neighbours(to_high, to_low)
    grad, dg1 = run(
        input_backward,
        args=(dq, inner, from_low, from_high, e1, tokens, gain),
        weights=row_w,
        outs=like(low, row_gain),
        raw_out=(),
        scratch=[VM((2, *SEQ_CB), LOW), VM(SEQ_CB, F32)] + held(3),
        micros=8.5,
    )
    return out, grad, weight_grad, jnp.concatenate([dg1, dg2, dg3], axis=0)


def per_device(
    alignment,
    cotangent,
    row_counts,
    band_reach,
    master_weights,
    weight_moment,
    weight_square,
    norm_gains,
    gain_moment,
    gain_square,
):
    staged = lax.axis_size("cols") == NMAT and lax.axis_size("fsdp") == 2
    mover = Staged() if staged else Native()
    out, grad, weight_total, gain_grad = layer(
        alignment.reshape(SEQ, CB, D),
        cotangent.reshape(SEQ, CB, D),
        row_counts[:, 0],
        band_reach[:, 0],
        mover,
        master_weights.astype(LOW),
        norm_gains.astype(LOW).astype(F32),
    )
    gain_total = mover.own_gains(gain_grad.reshape(3 * D), norm_gains.shape[0])
    new_weights, new_moment, new_square = adamw(
        master_weights,
        weight_moment,
        weight_square,
        weight_total.reshape(master_weights.shape),
        D ** (-0.5),
        DECAY,
        STEP_NUMBER,
    )
    new_gains, new_gain_moment, new_gain_square = adamw(
        norm_gains, gain_moment, gain_square, gain_total, RATE_GAIN, 0.0, STEP_NUMBER
    )
    shape = (MB, 1, ROWS, CB, D)
    return (
        out.reshape(shape),
        grad.reshape(shape),
        new_weights,
        new_moment,
        new_square,
        new_weights.astype(LOW),
        new_gains,
        new_gain_moment,
        new_gain_square,
    )


def solution(mesh):
    tokens = P(None, "fsdp", None, "cols", None)
    rows = P(("cols", "fsdp"), None)
    flat = P(("cols", "fsdp"))
    in_specs = (
        tokens,
        tokens,
        P(None, "fsdp"),
        P(None, "fsdp", None, "cols"),
        rows,
        rows,
        rows,
        flat,
        flat,
        flat,
    )
    out_specs = (tokens, tokens, rows, rows, rows, rows, flat, flat, flat)
    return jax.shard_map(
        per_device, mesh=mesh, in_specs=in_specs, out_specs=out_specs, check_vma=False
    )
```

```python
from functools import partial

import jax
import jax.numpy as jnp
from jax import lax
from jax.experimental import pallas as pl
from jax.experimental.pallas import tpu as pltpu
from jax.sharding import PartitionSpec as P

D = 768
H = 12
DH = 64
FF = 3072
NMAT = 16
ROWS = 4
CB = 64
HALO = 32
MB = 2
EXT = CB + 2 * HALO
SEQ = MB * ROWS
TOK = SEQ * CB
PAIRS = H // 2
LANES = 128
FOLD = FF // D
SPAN = D // 2
PART = SPAN // 2
EXTRA = 16
PER_GROUP = 10

EPS = 1e-05
BETA_ONE = 0.9
BETA_TWO = 0.999
ADAM_EPS = 1e-08
DECAY = 0.01
RATE_GAIN = 0.3
STEP_NUMBER = 10.0
MASKED = -1e30
F32 = jnp.float32
LOW = jnp.bfloat16


def dot_nn(a, b):
    return lax.dot_general(a, b, (((1,), (0,)), ((), ())), preferred_element_type=F32)


def dot_nt(a, b):
    return lax.dot_general(a, b, (((1,), (1,)), ((), ())), preferred_element_type=F32)


def dot_tn(a, b):
    return lax.dot_general(a, b, (((0,), (0,)), ((), ())), preferred_element_type=F32)


def standardize(values):
    center = values - jnp.mean(values, axis=-1, keepdims=True)
    spread = lax.rsqrt(jnp.mean(center * center, axis=-1, keepdims=True) + EPS)
    return center * spread, spread


def norm_pull(upward, values, gain):
    scaled, spread = standardize(values)
    weighted = upward * gain
    result = spread * (
        weighted
        - jnp.mean(weighted, axis=-1, keepdims=True)
        - scaled * jnp.mean(weighted * scaled, axis=-1, keepdims=True)
    )
    return result, jnp.sum(upward * scaled, axis=0, keepdims=True)


def lane_window(pair):
    return pl.ds(pl.multiple_of(pair * LANES, LANES), LANES)


def side_by_side(ref, micro, window):
    return jnp.concatenate([ref[micro * ROWS + r, :, window] for r in range(ROWS)], axis=1)


def head_stack(packed):
    lane = lax.broadcasted_iota(jnp.int32, packed.shape, 1)
    first = (lane % LANES) < DH
    zero = jnp.zeros_like(packed)
    return jnp.concatenate([jnp.where(first, packed, zero), jnp.where(first, zero, packed)], axis=0)


def head_merge(stacked, r):
    block = stacked[:, r * LANES : (r + 1) * LANES]
    lane = lax.broadcasted_iota(jnp.int32, (CB, LANES), 1)
    return jnp.where(lane < DH, block[:CB], block[CB:])


def head_sums():
    feature = lax.broadcasted_iota(jnp.int32, (D, LANES), 0)
    head = lax.broadcasted_iota(jnp.int32, (D, LANES), 1)
    return (feature // DH == head).astype(F32).astype(LOW)


def head_spread():
    head = lax.broadcasted_iota(jnp.int32, (LANES, D), 0)
    feature = lax.broadcasted_iota(jnp.int32, (LANES, D), 1)
    return (feature // DH == head).astype(F32).astype(LOW)


FULL = SPAN + EXTRA
STARTS = (0, FULL, 2 * FULL, 3 * FULL, 3 * FULL + PART)


def spot(buffers, number, row):
    if len(buffers) == 5:
        return buffers[number], row
    start = STARTS[number]
    if len(buffers) == 2 and number >= 3:
        return buffers[1], start - 3 * FULL + row
    return buffers[0], start + row


def regroup(sizes, refs):
    groups, start = [], 0
    for size in sizes:
        groups.append(refs[start : start + size])
        start += size
    return groups


def fetch_matrix(place, sources, table, matrix, target, sems, base):
    y_rel = jnp.where(place[1] == matrix // 2, 0, 1)
    waits = []
    for x in range(2):
        x_rel = jnp.where(place[0] == x, 0, 1)
        block = 2 * y_rel + x_rel
        sem = sems.at[base + x]
        for index in sorted(set(table)):
            here = None
            for plane, chosen in enumerate(table):
                if chosen == index:
                    hit = place[3] == plane
                    here = hit if here is None else jnp.logical_or(here, hit)
            for core_rel in range(2):
                held = jnp.logical_and(here, place[2] == (matrix % 2) ^ core_rel)
                buffers = sources[2 * index + core_rel]
                for number in range(5):
                    source, row = spot(buffers, number, 0)
                    size = SPAN if number < 3 else PART
                    to = x * SPAN + (PART if number == 4 else 0)
                    part = pltpu.make_async_copy(
                        source.at[pl.ds(row, size)], target.at[pl.ds(to, size)], sem
                    )
                    pl.when(jnp.logical_and(held, block == min(number, 3)))(part.start)
                    if number == 0:
                        copy = part
        waits.append(copy)
    return waits


def fetch(place, sources, table, matrices, w, sems, first=0):
    waits = []
    for slot, matrix in enumerate(matrices):
        slot += first
        waits.append(
            fetch_matrix(place, sources, table, matrix, w.at[slot], sems, 2 * slot)
        )
    return waits


def settle(waits):
    for copy in waits:
        copy.wait()


def emit_matrix(place, source, matrix, n, out, sems, base):
    *keep, rest, corner = out
    core_same = place[2] == matrix % 2
    y_rel = jnp.where(place[1] == matrix // 2, 0, 1)
    waits = []
    for x in range(2):
        x_rel = jnp.where(place[0] == x, 0, 1)
        spot_rel = 2 * y_rel + x_rel
        block = source.at[pl.ds(x * SPAN, SPAN)]
        sem = sems.at[base + x]
        sent = jnp.logical_not(core_same)
        for number, target in enumerate(keep):
            kept = pltpu.make_async_copy(block, target.at[n], sem)
            pl.when(jnp.logical_and(core_same, spot_rel == number))(kept.start)
        near = pltpu.make_async_copy(block, rest.at[jnp.minimum(spot_rel, 2), n], sem)
        far = pltpu.make_async_copy(block, corner.at[n], sem)
        pl.when(jnp.logical_and(sent, spot_rel < 3))(near.start)
        pl.when(jnp.logical_and(sent, spot_rel == 3))(far.start)
        waits.append(far)
    return waits


def gain_copies(sources, group, target, sem):
    copies = []
    for core_rel in range(2):
        buffers = sources[2 * group + core_rel]
        for number, row in ((0, SPAN), (1, SPAN), (2, SPAN), (4, PART)):
            source, row = spot(buffers, number, row)
            copy = pltpu.make_async_copy(
                source.at[pl.ds(row, EXTRA)], target.at[len(copies)], sem.at[len(copies)]
            )
            copies.append(copy)
    return copies


def row_project(
    spec, count, scal, place, tokens, from_low, from_high, *refs
):
    table, group = spec
    sources, (a1e, q, ke, ve, gain, w, held, sems, gain_sems) = regroup(count, refs), refs[sum(count) :]
    parts = gain_copies(sources, group, held, gain_sems)
    for copy in parts:
        copy.start()
    copies = fetch(place, sources, table, range(3), w, sems)
    settle(parts)
    total = held[0].astype(F32)
    for k in range(1, 8):
        total = total + held[k].astype(F32)
    gain[...] = total[:3]

    def norm_step(i, _):
        for source, start, size in (
            (from_low, 0, HALO),
            (tokens, HALO, CB),
            (from_high, HALO + CB, HALO),
        ):
            scaled, _s = standardize(source[i].astype(F32))
            a1e[i, start : start + size] = (scaled * gain[0:1]).astype(LOW)
        return 0

    lax.fori_loop(0, SEQ, norm_step, 0, unroll=True)
    wide = a1e[...].reshape(SEQ * EXT, D)
    settle(copies[1])
    ke[...] = dot_nn(wide, w[1]).astype(LOW).reshape(SEQ, EXT, D)
    settle(copies[2])
    ve[...] = dot_nn(wide, w[2]).astype(LOW).reshape(SEQ, EXT, D)
    inner = a1e[:, HALO : HALO + CB, :].reshape(TOK, D)
    settle(copies[0])
    q[...] = dot_nn(inner, w[0]).astype(LOW).reshape(SEQ, CB, D)
    for i in range(SEQ):
        q[i] = (q[i].astype(F32) * scal[i // ROWS, 1 + i % ROWS]).astype(LOW)


def row_attend(
    table, count, scal, place, tokens, q, ke, ve, allowed, gain, *refs
):
    sources, (p1, o1, x1, a2, w, sems) = regroup(count, refs), refs[sum(count) :]
    copies = fetch(place, sources, table, (3,), w, sems)

    def attend(pair, _):
        window = lane_window(pair)
        for m in range(MB):
            query = head_stack(side_by_side(q, m, window))
            scores = dot_nt(query, side_by_side(ke, m, window)) * scal[m, 0]
            mask = allowed[m]
            mask = jnp.concatenate([mask, mask], axis=0)
            scores = jnp.where(mask > 0, scores, MASKED)
            weight = jnp.exp(scores - jnp.max(scores, axis=-1, keepdims=True))
            prob = weight / jnp.sum(weight, axis=-1, keepdims=True)
            p1[m, pair] = prob
            mixed = dot_nn(prob.astype(LOW), side_by_side(ve, m, window))
            for r in range(ROWS):
                o1[m * ROWS + r, :, window] = head_merge(mixed, r).astype(LOW)
        return 0

    lax.fori_loop(0, PAIRS, attend, 0, unroll=True)
    settle(copies[0])
    x1[...] = tokens[...].astype(F32) + dot_nn(o1[...].reshape(TOK, D), w[0]).reshape(SEQ, CB, D)

    def next_norm(i, _):
        scaled, _s = standardize(x1[i])
        a2[i] = (scaled * gain[1:2]).astype(LOW)
        return 0

    lax.fori_loop(0, SEQ, next_norm, 0, unroll=True)


def col_forward(table, count, scal, place, x1, a2, gain, *refs):
    sources, (q2, k2, v2, p2, o2, x2, a3, w, sems) = regroup(count, refs), refs[sum(count) :]
    copies = fetch(place, sources, table, range(4), w, sems)
    for j in range(3):
        settle(copies[j])
    flat = a2[...].reshape(TOK, D)
    q2[...] = dot_nn(flat, w[0]).astype(LOW).reshape(SEQ, CB, D)
    k2[...] = dot_nn(flat, w[1]).astype(LOW).reshape(SEQ, CB, D)
    v2[...] = dot_nn(flat, w[2]).astype(LOW).reshape(SEQ, CB, D)
    sums = head_sums()
    spread = head_spread()

    def attend(i, _):
        micro = i // ROWS
        query = q2[i].astype(F32)
        products = jnp.concatenate(
            [(query * k2[micro * ROWS + s].astype(F32)).astype(LOW) for s in range(ROWS)], axis=0
        )
        scores = dot_nn(products, sums) * (DH ** (-0.5))
        parts = [
            jnp.where(scal[micro, 1 + s] > 0, scores[s * CB : (s + 1) * CB], MASKED)
            for s in range(ROWS)
        ]
        top = jnp.maximum(jnp.maximum(parts[0], parts[1]), jnp.maximum(parts[2], parts[3]))
        parts = [jnp.exp(part - top) for part in parts]
        scale = 1.0 / (parts[0] + parts[1] + parts[2] + parts[3])
        prob = jnp.concatenate([part * scale for part in parts], axis=0)
        p2[i] = prob
        wide = dot_nn(prob.astype(LOW), spread)
        total = wide[:CB] * v2[micro * ROWS].astype(F32)
        for s in range(1, ROWS):
            total = total + wide[s * CB : (s + 1) * CB] * v2[micro * ROWS + s].astype(F32)
        o2[i] = total.astype(LOW)
        return 0

    lax.fori_loop(0, SEQ, attend, 0, unroll=True)
    settle(copies[3])
    x2[...] = x1[...] + dot_nn(o2[...].reshape(TOK, D), w[3]).reshape(SEQ, CB, D)

    def next_norm(i, _):
        scaled, _s = standardize(x2[i])
        a3[i] = (scaled * gain[2:3]).astype(LOW)
        return 0

    lax.fori_loop(0, SEQ, next_norm, 0, unroll=True)


CHUNK = 256


def feed_forward(tables, count, scal, place, x2, a3, cot, gain, *refs):
    sources, refs = regroup(count, refs), refs[sum(count) :]
    out, e2, dgain, *terms_out, up, down, live_cot, gl, dhd, w, dw, in_sems, out_sems = refs
    copies = []
    for n in range(2):
        copies += fetch(place, sources, tables[n], range(4), w, in_sems, 4 * n)
    for i in range(SEQ):
        live_cot[i * CB : (i + 1) * CB] = (
            cot[i].astype(F32) * scal[i // ROWS, 1 + i % ROWS]
        ).astype(LOW)
    normed = a3[...].reshape(TOK, D)
    grad = live_cot[...]
    waits = []
    for step in range(FOLD):
        settle(copies[step])
        settle(copies[FOLD + step])
        win = w[step]
        wout = w[FOLD + step]
        for base in range(0, TOK, CHUNK):
            rows = slice(base, base + CHUNK)
            hidden = dot_nn(normed[rows], win)
            pulled = dot_nt(grad[rows], wout)
            half = 0.5 * lax.erf(hidden * (0.5**0.5)) + 0.5
            gl[rows] = (hidden * half).astype(LOW)
            slope = half + hidden * (jnp.exp(-0.5 * hidden * hidden) * ((2.0 * jnp.pi) ** -0.5))
            dhd[rows] = (pulled * slope).astype(LOW)
        for n, value in enumerate((dot_tn(normed, dhd[...]), dot_tn(gl[...], grad))):
            slot = 4 * n + step
            dw[slot] = value.astype(LOW)
            waits += emit_matrix(place, dw.at[slot], step, n, terms_out, out_sems, 2 * slot)
        forward = dot_nn(gl[...], wout)
        backward = dot_nt(dhd[...], win)
        if step == 0:
            up[...] = forward
            down[...] = backward
        else:
            up[...] += forward
            down[...] += backward
    total = jnp.zeros((1, D), F32)
    for i in range(SEQ):
        rows = slice(i * CB, (i + 1) * CB)
        value = x2[i]
        out[i] = ((value + up[rows]) * scal[i // ROWS, 1 + i % ROWS]).astype(LOW)
        part, gain_part = norm_pull(down[rows], value, gain[2:3])
        e2[i] = live_cot[rows].astype(F32) + part
        total = total + gain_part
    dgain[...] = total
    settle(waits)


def col_attend_back(table, count, scal, place, e2, q2, k2, v2, p2, *refs):
    sources, refs = regroup(count, refs), refs[sum(count) :]
    dq2, dk2, dv2, do2, dka, dva, w, in_sems = refs
    copies = fetch(place, sources, table, (3,), w, in_sems)
    low = e2[...].reshape(TOK, D).astype(LOW)
    settle(copies[0])
    do2[...] = dot_nt(low, w[0]).astype(LOW).reshape(SEQ, CB, D)
    sums = head_sums()
    spread = head_spread()
    dka[...] = jnp.zeros_like(dka)
    dva[...] = jnp.zeros_like(dva)

    def pull(i, _):
        micro = i // ROWS
        upward = do2[i].astype(F32)
        products = jnp.concatenate(
            [(upward * v2[micro * ROWS + s].astype(F32)).astype(LOW) for s in range(ROWS)], axis=0
        )
        dprob = dot_nn(products, sums)
        prob = p2[i]
        mixed = prob * dprob
        inner = mixed[:CB] + mixed[CB : 2 * CB] + mixed[2 * CB : 3 * CB] + mixed[3 * CB :]
        dscore = prob * (dprob - jnp.concatenate([inner] * ROWS, axis=0))
        wide = dot_nn(prob.astype(LOW), spread)
        dwide = dot_nn(dscore.astype(LOW), spread)
        query = q2[i].astype(F32)
        total = jnp.zeros((CB, D), F32)
        for s in range(ROWS):
            rows = slice(s * CB, (s + 1) * CB)
            total = total + dwide[rows] * k2[micro * ROWS + s].astype(F32)
            dka[micro * ROWS + s] += dwide[rows] * query
            dva[micro * ROWS + s] += wide[rows] * upward
        dq2[i] = (total * (DH ** (-0.5))).astype(LOW)
        return 0

    lax.fori_loop(0, SEQ, pull, 0, unroll=True)
    dk2[...] = (dka[...] * (DH ** (-0.5))).astype(LOW)
    dv2[...] = dva[...].astype(LOW)


def col_project_back(table, count, scal, place, e2, o2, dq2, dk2, dv2, a2, x1, gain, *refs):
    sources, refs = regroup(count, refs), refs[sum(count) :]
    e1, dgain, *terms_out, acc, w, dw, in_sems, out_sems = refs
    copies = fetch(place, sources, table, range(3), w, in_sems)
    flat = a2[...].reshape(TOK, D)
    low = e2[...].reshape(TOK, D).astype(LOW)
    dw[3] = dot_tn(o2[...].reshape(TOK, D), low).astype(LOW)
    waits = emit_matrix(place, dw.at[3], 3, 0, terms_out, out_sems, 6)
    for j, ref in enumerate((dq2, dk2, dv2)):
        grads = ref[...].reshape(TOK, D)
        dw[j] = dot_tn(flat, grads).astype(LOW)
        waits += emit_matrix(place, dw.at[j], j, 0, terms_out, out_sems, 2 * j)
        settle(copies[j])
        part = dot_nt(grads, w[j]).reshape(SEQ, CB, D)
        if j == 0:
            acc[...] = part
        else:
            acc[...] += part
    gain_total = jnp.zeros((1, D), F32)
    for i in range(SEQ):
        part, gain_part = norm_pull(acc[i], x1[i], gain[1:2])
        e1[i] = e2[i] + part
        gain_total = gain_total + gain_part
    dgain[...] = gain_total
    settle(waits)


def row_backward(table, count, scal, place, e1, o1, q, ke, ve, p1, a1e, *refs):
    sources, refs = regroup(count, refs), refs[sum(count) :]
    dq, dke, dve, *terms_out, do1, w, dw, in_sems, out_sems = refs
    copies = fetch(place, sources, table, (3,), w, in_sems)
    low = e1[...].reshape(TOK, D).astype(LOW)
    settle(copies[0])
    do1[...] = dot_nt(low, w[0]).astype(LOW).reshape(SEQ, CB, D)

    def pull(pair, _):
        window = lane_window(pair)
        for m in range(MB):
            query = head_stack(side_by_side(q, m, window))
            upward = head_stack(side_by_side(do1, m, window))
            prob = p1[m, pair]
            dprob = dot_nt(upward, side_by_side(ve, m, window))
            dscore = prob * (dprob - jnp.sum(prob * dprob, axis=-1, keepdims=True))
            dscore = dscore.astype(LOW)
            dvalue = dot_tn(prob.astype(LOW), upward)
            dkey = dot_tn(dscore, query) * scal[m, 0]
            dquery = dot_nn(dscore, side_by_side(ke, m, window)) * scal[m, 0]
            for r in range(ROWS):
                lanes = slice(r * LANES, (r + 1) * LANES)
                dve[m * ROWS + r, :, window] = dvalue[:, lanes].astype(LOW)
                dke[m * ROWS + r, :, window] = dkey[:, lanes].astype(LOW)
                dq[m * ROWS + r, :, window] = (head_merge(dquery, r) * scal[m, 1 + r]).astype(LOW)
        return 0

    lax.fori_loop(0, PAIRS, pull, 0, unroll=True)
    wide = a1e[...].reshape(SEQ * EXT, D)
    own = a1e[:, HALO : HALO + CB, :].reshape(TOK, D)
    waits = []
    for j, (left, right) in enumerate(
        (
            (own, dq[...].reshape(TOK, D)),
            (wide, dke[...].reshape(SEQ * EXT, D)),
            (wide, dve[...].reshape(SEQ * EXT, D)),
            (o1[...].reshape(TOK, D), low),
        )
    ):
        dw[j] = dot_tn(left, right).astype(LOW)
        waits += emit_matrix(place, dw.at[j], j, 0, terms_out, out_sems, 2 * j)
    settle(waits)


def input_project(
    table, count, scal, place, dq, dke, dve, tokens, from_low, from_high, *refs
):
    sources, (inner, to_low, to_high, dgain, acc, w, sems) = regroup(count, refs), refs[sum(count) :]
    copies = fetch(place, sources, table, range(3), w, sems)
    settle(copies[1])
    acc[...] = dot_nt(dke[...].reshape(SEQ * EXT, D), w[1]).reshape(SEQ, EXT, D)
    settle(copies[2])
    acc[...] += dot_nt(dve[...].reshape(SEQ * EXT, D), w[2]).reshape(SEQ, EXT, D)
    settle(copies[0])
    acc[:, HALO : HALO + CB, :] += dot_nt(dq[...].reshape(TOK, D), w[0]).reshape(SEQ, CB, D)
    total = jnp.zeros((1, D), F32)
    for i in range(SEQ):
        for source, start, size in (
            (from_low, 0, HALO),
            (tokens, HALO, CB),
            (from_high, HALO + CB, HALO),
        ):
            scaled, _s = standardize(source[i].astype(F32))
            total = total + jnp.sum(acc[i, start : start + size] * scaled, axis=0, keepdims=True)
    dgain[...] = total
    inner[...] = acc[:, HALO : HALO + CB, :]
    to_low[...] = acc[:, :HALO, :].astype(LOW)
    to_high[...] = acc[:, HALO + CB :, :].astype(LOW)


def input_finish(inner, from_low, from_high, e1, tokens, gain, grad):
    def step(i, _):
        upward = jnp.concatenate(
            [
                inner[i, :HALO] + from_low[i].astype(F32),
                inner[i, HALO:] + from_high[i].astype(F32),
            ],
            axis=0,
        )
        part, _g = norm_pull(upward, tokens[i].astype(F32), gain[0:1])
        grad[i] = (e1[i] + part).astype(LOW)
        return 0

    lax.fori_loop(0, SEQ, step, 0, unroll=True)


def in_vmem(count):
    return [pl.BlockSpec(memory_space=pltpu.VMEM)] * count


def like(*shapes):
    return tuple(jax.ShapeDtypeStruct(shape, dtype) for shape, dtype in shapes)


SEQ_CB = (SEQ, CB, D)
SEQ_EXT = (SEQ, EXT, D)
RIM = (SEQ, HALO, D)
PER_MICRO = 1.15e9
VM = pltpu.VMEM
DMA = pltpu.SemaphoreType.DMA


def pieces(count):
    return (
        *(((count, SPAN, D), LOW),) * 4,
        ((3, count, SPAN, D), LOW),
        ((count, SPAN, D), LOW),
    )


def run_kernel(body, scalars, args, weights, outs, raw_out, scratch, micros):
    vmem = pl.BlockSpec(memory_space=pltpu.VMEM)
    raw = pl.BlockSpec(memory_space=pltpu.HBM)
    moved = sum(a.size * a.dtype.itemsize for a in args)
    moved += sum(o.size * jnp.dtype(o.dtype).itemsize for o in outs)
    call = body
    sources = ()
    if weights is not None:
        table, groups = weights
        sources = [buffer for group in groups for buffer in group]
        call = partial(body, table, tuple(len(group) for group in groups))
    return pl.pallas_call(
        call,
        name=body.__name__,
        out_shape=outs,
        in_specs=[pl.BlockSpec(memory_space=pltpu.SMEM)] * len(scalars)
        + [vmem] * len(args)
        + [raw] * len(sources),
        out_specs=tuple(raw if i in raw_out else vmem for i in range(len(outs))),
        scratch_shapes=scratch,
        compiler_params=pltpu.CompilerParams(vmem_limit_bytes=(60 if body is feed_forward else 32) << 20),
        cost_estimate=pl.CostEstimate(
            flops=int(micros * PER_MICRO), bytes_accessed=moved, transcendentals=0
        ),
    )(*scalars, *args, *sources)


def held(count):
    return [VM((count, D, D), LOW), DMA((2 * count,))]


def terms(count):
    return [VM((count, D, D), LOW), DMA((2 * count,))]


def corner_terms(keep, got, half_a, half_b):
    total = keep[...].astype(F32) + got[...].astype(F32)
    half_a[...] = total[:, :PART].astype(LOW)
    half_b[...] = total[:, PART:].astype(LOW)


def side_terms(keep_x, got_x, keep_y, got_y, half_a, half_b, *outs):
    count = len(outs) // 2
    for n in range(count):
        over_x, over_y = outs[n], outs[count + n]
        total = keep_x[n].astype(F32) + got_x[0, n].astype(F32)
        over_x[0, :PART] = (total[:PART] + half_a[n].astype(F32)).astype(LOW)
        over_x[0, PART:] = total[PART:].astype(LOW)
        total = keep_y[n].astype(F32) + got_y[0, n].astype(F32)
        over_y[0, :PART] = total[:PART].astype(LOW)
        over_y[0, PART:] = (total[PART:] + half_b[n].astype(F32)).astype(LOW)


def own_terms(keep, got, *refs):
    *sides, total, low = refs
    count = len(sides) // 2
    for n in range(count):
        value = keep[n].astype(F32) + got[0, n].astype(F32)
        value = value + sides[n][0].astype(F32) + sides[count + n][0].astype(F32)
        total[n] = value
        low[n] = value.astype(LOW)


SPLIT = 2


def call_small(body, args, picks, shapes):
    count = args[0].shape[0]
    width = D // SPLIT
    specs = []
    for arg, pick in zip(args, picks):
        if pick is None:
            specs.append(pl.BlockSpec((*arg.shape[:-1], width), lambda j: (0, 0, j)))
        elif isinstance(pick, int):
            specs.append(
                pl.BlockSpec((1, count, SPAN, width), lambda j, k=pick: (k, 0, 0, j))
            )
    moved = sum(s.block_shape[-2] * D * count * 2 for s in specs)
    return pl.pallas_call(
        body,
        name=body.__name__,
        grid=(SPLIT,),
        out_shape=tuple(
            jax.ShapeDtypeStruct((*shape, D), dtype) for shape, dtype in shapes
        ),
        in_specs=specs,
        out_specs=tuple(
            pl.BlockSpec((*shape, width), lambda j: (0, 0, j)) for shape, _d in shapes
        ),
        compiler_params=pltpu.CompilerParams(vmem_limit_bytes=24 << 20),
        cost_estimate=pl.CostEstimate(
            flops=int(8 * PER_MICRO), bytes_accessed=moved, transcendentals=0
        ),
    )(*args)


def swap_pairs(count, bit):
    return [(i, i ^ bit) for i in range(count)]


def after(value, *before):
    return lax.optimization_barrier((value, *before))[0]


def add(*parts):
    total = parts[0].astype(F32)
    for part in parts[1:]:
        total = total + part.astype(F32)
    return total


def together(*values):
    return lax.optimization_barrier(values)


class Staged:
    planes = 4
    tables = ((0, 1, 2, 2), (1, 0, 1, 3), (2, 2, 0, 1), (3, 3, 3, 0))

    def __init__(self):
        self.count = NMAT
        self.step = NMAT // self.planes
        cols = lax.axis_index("cols")
        self.z = cols // self.step
        self.place = jnp.stack(
            [lax.axis_index("fsdp"), (cols // 2) % 2, cols % 2, self.z]
        ).astype(jnp.int32)

    def over_x(self, value):
        return lax.ppermute(value, "fsdp", [(0, 1), (1, 0)])

    def over_y(self, value):
        return lax.ppermute(value, "cols", swap_pairs(self.count, 2))

    def over_core(self, value):
        return lax.ppermute(value, "cols", swap_pairs(self.count, 1))

    def over_z(self, value, pairs):
        step = self.step
        full = [(a * step + i, b * step + i) for a, b in pairs for i in range(step)]
        return lax.ppermute(value, "cols", full)

    def by_plane(self, options):
        result = options[-1]
        for index in range(len(options) - 2, -1, -1):
            result = jnp.where(self.z == index, options[index], result)
        return result

    def own_place(self, gains):
        index = lax.axis_index("cols") * 2 + lax.axis_index("fsdp")
        spread = jnp.zeros((EXTRA * D,), LOW)
        spread = lax.dynamic_update_slice(spread, gains, (index * gains.shape[0],))
        return spread.reshape(EXTRA, D)

    def sum_step(self, value, index):
        swaps = (
            lambda v: self.over_z(v, [(0, 1), (1, 0), (2, 3), (3, 2)]),
            lambda v: self.over_z(v, [(0, 2), (2, 0), (1, 3), (3, 1)]),
            self.over_core,
            self.over_x,
            self.over_y,
        )
        return value + swaps[index](value)

    def own_gains(self, value, size):
        value = value.reshape(3 * D)
        index = lax.axis_index("cols") * 2 + lax.axis_index("fsdp")
        return lax.dynamic_slice(value, (index * size,), (size,))

    def halves(self, from_x, from_y):
        return self.over_y(from_x[:PART]), self.over_x(from_y[PART:])

    def gather(self, shard, gains, tokens):
        core = self.over_core
        own1 = jnp.concatenate([shard, self.own_place(gains)], axis=0)
        up1 = self.over_z(own1, [(0, 1), (1, 2), (2, 3)])
        down1 = self.over_z(own1, [(3, 2), (2, 1), (1, 0)])
        x1, y1 = self.over_x(own1), self.over_y(own1)
        up1, down1, x1, y1 = together(up1, down1, x1, y1)
        own2 = jnp.where(self.z == 0, down1, up1)
        x2, y2 = self.over_x(own2), self.over_y(own2)
        a1, b1 = self.halves(x1, y1)
        up2 = self.over_z(up1, [(1, 2), (2, 3)])
        down2 = self.over_z(down1, [(2, 1), (1, 0)])
        rims = neighbours(*after((tokens[:, CB - HALO :], tokens[:, :HALO]), x1))
        c1 = [core(own1)]
        up2, down2, a1, b1, x2, y2, *rims = together(up2, down2, a1, b1, x2, y2, *rims)
        up3 = self.over_z(up2, [(2, 3)])
        down3 = self.over_z(down2, [(1, 0)])
        a2, b2 = self.halves(x2, y2)
        c1 += [core(x1), core(y1), core(a1), core(b1)]
        up3, down3, a2, b2, *c1 = together(up3, down3, a2, b2, *c1)
        own3 = self.by_plane([down2, down1, up2, up3])
        placed = [v[SPAN:] for v in (own1, up1, up2, up3, down1, down2, down3)]
        own3 = jnp.concatenate([own3[:SPAN], add(*placed).astype(LOW)], axis=0)
        x3, y3 = self.over_x(own3), self.over_y(own3)
        c2 = [core(v) for v in (own2, x2, y2, a2, b2)]
        x3, y3, *c2 = together(x3, y3, *c2)
        a3, b3 = self.halves(x3, y3)
        c3 = [core(own3), core(x3), core(y3)]
        own4 = self.by_plane([down3, down2, down1, up2])
        a3, b3, own4, *c3 = together(a3, b3, own4, *c3)
        x4, y4 = self.over_x(own4), self.over_y(own4)
        c3 += [core(a3), core(b3)]
        self.row_gate = (own4,)
        self.fourth = own4, x4, y4
        self.first = ((own1, x1, y1, a1, b1), tuple(c1), (own2, x2, y2, a2, b2), tuple(c2))
        self.first += ((own3, x3, y3, a3, b3), tuple(c3))
        return (self.tables[0], self.first), 2, rims

    def gather_more(self, seen):
        own4, x4, y4 = self.fourth
        x4, y4, seen = together(x4, y4, seen)
        xa, yb = x4[:PART], y4[PART:]
        self.attend_gate = (xa, yb)
        core = self.over_core
        self.fourth = own4, x4, y4, self.over_y(xa), self.over_x(yb)
        self.fourth_core = [core(own4), core(x4), core(y4)]

    def gather_last(self, seen):
        own4, x4, y4, a4, b4 = self.fourth
        a4, b4, _ = together(a4, b4, seen)
        core = self.over_core
        c4 = (*self.fourth_core, core(a4), core(b4))
        every = (*self.first, (own4, x4, y4, a4, b4), c4)
        return (self.tables[1], every), (self.tables[2:], every)

    def corner_swap(self, keep, got):
        shapes = (((keep[3].shape[0], PART), LOW),) * 2
        return call_small(corner_terms, (keep[3], got), (None, None), shapes)

    def side_blocks(self, keep, got, corner_a, corner_b):
        picks = (None, 1, None, 2, None, None)
        args = (keep[1], got, keep[2], got, corner_a, corner_b)
        count = keep[0].shape[0]
        sides = call_small(side_terms, args, picks, (((1, SPAN), LOW),) * (2 * count))
        return sides[:count], sides[count:]

    def own_sum(self, keep, got, from_x, from_y):
        count = keep[0].shape[0]
        picks = (None, 0, *(None,) * (2 * count))
        shapes = (((count, SPAN), F32), ((count, SPAN), LOW))
        return call_small(own_terms, (keep[0], got, *from_x, *from_y), picks, shapes)

    def reduce_forward(self, *terms):
        *keep, rest, corner = terms
        corner = self.over_core(corner)
        a, b = self.corner_swap(keep, corner)
        self.fwd = keep, self.over_core(after(rest, a, b))
        self.fwd_corner = self.over_y(a), self.over_x(b)
        return a, b

    def reduce_forward_sides(self, seen):
        a, b, _ = together(*self.fwd_corner, seen)
        (x2, x3), (y2, y3) = self.side_blocks(*self.fwd, a, b)
        self.first_sides = self.over_x(x2), self.over_y(y2)
        self.later_sides = x3, y3
        return x2, y2, x3, y3

    def reduce_col(self, *terms):
        *keep, rest, corner = terms
        corner = self.over_core(corner)
        fx, fy = together(*self.first_sides)
        self.first_sides = fx, fy
        a, b = after(self.later_sides, fx, fy)
        self.later_sides = self.over_x(a), self.over_y(b)
        a, b = self.corner_swap(keep, after(corner, a, b))
        self.col = keep, self.over_core(after(rest, a, b))
        self.col_corner = self.over_y(a), self.over_x(b)
        return a, b

    def reduce_row(self, seen, *terms):
        *keep, rest, corner = terms
        corner = self.over_core(corner)
        a, b, fx, fy, _ = together(*self.col_corner, *self.later_sides, seen)
        (cx,), (cy,) = self.side_blocks(*self.col, a, b)
        corner = after(corner, cx, cy)
        cx, cy = self.over_x(cx), self.over_y(cy)
        a, b = self.corner_swap(keep, corner)
        got = self.over_core(after(rest, a, b))
        fx, fy, *_ = together(fx, fy, a, b)
        a, b = self.over_y(a), self.over_x(b)
        sides = (self.first_sides[0], fx), (self.first_sides[1], fy)
        self.forward, low = self.own_sum(*self.fwd, *sides)
        near = self.over_z(low, [(0, 1), (2, 3), (3, 2)])
        a, b, cx, cy, got, _ = together(a, b, cx, cy, got, low)
        (rx,), (ry,) = self.side_blocks(keep, got, a, b)
        cx, cy, *_ = together(cx, cy, rx, ry)
        self.row = keep, got
        self.row_sides = self.over_x(rx), self.over_y(ry)
        self.near_forward = near
        self.col_sum, low = self.own_sum(*self.col, (cx,), (cy,))
        self.near_col = self.over_z(low[0], [(0, 1), (3, 2)])
        return rx, ry, low

    def reduce_last(self, gains):
        gains = self.sum_step(gains.reshape(18, LANES), 0)
        rx, ry, near, gains = together(*self.row_sides, self.near_forward, gains)
        row, low = self.own_sum(*self.row, (rx,), (ry,))
        near_row = self.over_z(low[0], [(1, 0), (3, 2)])
        self.rim_gate = (low,)
        near, near_col, gains, _ = together(near, self.near_col, gains, low)
        forward = [add(self.forward[k], near[k]) for k in range(2)]
        far = [
            self.over_z(value.astype(LOW), [pair]) for value, pair in zip(forward, ((1, 2), (1, 3)))
        ]
        col = add(self.col_sum[0], near_col)
        far_col = self.over_z(col.astype(LOW), [(2, 1)])
        gains = self.sum_step(gains, 1)
        near_row, gains = together(near_row, gains)
        row = add(row[0], near_row)
        low = row.astype(LOW)
        far_row = self.over_z(low, [(2, 0)])
        low, gains = together(low, gains)
        self.last_gate = (low,)
        for index in range(2, 5):
            gains = self.sum_step(gains, index)
        self.totals = row, far_row, col, far_col, forward, far
        return gains

    def total(self, seen):
        row, far_row, col, far_col, forward, far = self.totals
        far_row, far_col, far[0], far[1], seen = together(far_row, far_col, *far, seen)
        options = [add(row, far_row), add(col, far_col)]
        options += [add(forward[0], far[0]), add(forward[1], far[1])]
        return self.by_plane(options), seen


class Native:
    axes = ("cols", "fsdp")
    rim_gate = ()
    last_gate = ()
    row_gate = ()
    attend_gate = ()

    def __init__(self):
        self.place = jnp.zeros((4,), jnp.int32)
        self.parts = []

    def gather(self, shard, gains, tokens):
        full = lax.all_gather(shard, self.axes, axis=0, tiled=True)
        gains = lax.all_gather(gains, self.axes, axis=0, tiled=True)
        rims = neighbours(tokens[:, CB - HALO :], tokens[:, :HALO])
        row, *self.rest = self.arranged(full, gains)
        return row, 0, rims

    def gather_more(self, seen):
        pass

    def gather_last(self, seen):
        return self.rest

    def arranged(self, full, gains):
        blocks = full.reshape(4, 2, 2, 2 * SPAN, D).transpose(0, 2, 1, 3, 4)
        blocks = blocks.reshape(4, 2, 4, SPAN, D)
        extra = jnp.pad(gains.reshape(3, D), ((0, EXTRA - 3), (0, 0)))
        groups = []
        for b in range(4):
            parts = []
            for c in range(2):
                for k in range(3):
                    mine = extra if b == c == k == 0 else jnp.zeros_like(extra)
                    parts.append(jnp.concatenate([blocks[b, c, k], mine], axis=0))
                last = jnp.concatenate([blocks[b, c, 3], jnp.zeros_like(extra)], axis=0)
                parts += [last[:PART], last[PART:]]
            groups.append((tuple(parts[:5]), tuple(parts[5:])))
        row, col, low, high = groups
        flat = (0, 0, 0, 0)
        return (flat, row), (flat, col), ((flat, (1, 1, 1, 1)), (*low, *high))

    def own_gains(self, value, size):
        value = value.reshape(3 * D)
        return lax.psum_scatter(value, self.axes, scatter_dimension=0, tiled=True)

    def stash(self, *terms):
        *keep, rest, corner = terms
        sent = jnp.concatenate([rest, corner[None]], axis=0)
        blocks = jnp.stack([jnp.stack(keep), sent])
        blocks = blocks.reshape(2, 2, 2, *corner.shape)
        self.parts.insert(0, blocks.transpose(3, 1, 0, 2, 4, 5))
        return ()

    def reduce_forward(self, *terms):
        return self.stash(*terms)

    def reduce_forward_sides(self, seen):
        return ()

    def reduce_col(self, *terms):
        return self.stash(*terms)

    def reduce_row(self, seen, *terms):
        return self.stash(*terms)

    def reduce_last(self, gains):
        return gains

    def total(self, seen):
        full = jnp.concatenate([self.parts[0], self.parts[1], self.parts[2]], axis=0)
        full = full.reshape(NMAT * D, D)
        full = lax.psum_scatter(full, self.axes, scatter_dimension=0, tiled=True)
        return full.astype(F32), seen


def neighbours(upward, downward):
    count = lax.axis_size("cols")
    forward = [(i, i + 1) for i in range(count - 1)]
    backward = [(target, source) for source, target in forward]
    return lax.ppermute(upward, "cols", forward), lax.ppermute(downward, "cols", backward)


def adamw(master, moment, square, grad_total, rate, decay, steps_done):
    moment_new = BETA_ONE * moment + (1.0 - BETA_ONE) * grad_total
    square_new = BETA_TWO * square + (1.0 - BETA_TWO) * grad_total * grad_total
    moment_fix = 1.0 - BETA_ONE**steps_done
    square_fix = 1.0 - BETA_TWO**steps_done
    update = moment_new / moment_fix / (jnp.sqrt(square_new / square_fix) + ADAM_EPS)
    return (master - rate * (update + decay * master), moment_new, square_new)


def band_mask(band_reach):
    first_col = lax.axis_index("cols") * CB
    col_total = CB * lax.axis_size("cols")
    query_pos = first_col + jnp.arange(CB, dtype=jnp.int32)
    key_pos = first_col - HALO + jnp.arange(EXT, dtype=jnp.int32)
    lowest = query_pos[None] - band_reach[:, 0]
    highest = query_pos[None] + band_reach[:, 1]
    key = key_pos[None, None]
    allowed = (key >= lowest[..., None]) & (key <= highest[..., None])
    allowed = allowed & (key >= 0) & (key < col_total)
    return allowed.astype(F32)


def layer(tokens, cot, counts, reach, mover, shard, gains):
    row_w, group, rims = mover.gather(shard, gains, tokens)
    from_low, from_high = rims
    present = (jnp.arange(ROWS, dtype=jnp.int32)[None] < counts[:, None]).astype(F32)
    row_scale = DH ** (-0.5) * lax.rsqrt(counts.astype(F32))
    scalars = (jnp.concatenate([row_scale[:, None], present], axis=1), mover.place)
    run = partial(run_kernel, scalars=scalars)
    low, wide = (SEQ_CB, LOW), (SEQ_EXT, LOW)
    row_gain = ((1, D), F32)
    probs = ((MB, PAIRS, 2 * CB, EXT), F32)
    col_probs = ((SEQ, ROWS * CB, LANES), F32)

    a1e, q, ke, ve, gain = run(
        row_project,
        args=(after(tokens, *mover.row_gate), from_low, from_high),
        weights=((row_w[0], group), row_w[1]),
        outs=like(wide, low, wide, wide, ((3, D), F32)),
        raw_out=(),
        scratch=[held(3)[0], VM((8, EXTRA, D), LOW), DMA((6,)), DMA((8,))],
        micros=9.5,
    )
    mover.gather_more(q)
    p1, o1, x1, a2 = run(
        row_attend,
        args=(tokens, after(q, *mover.attend_gate), ke, ve, band_mask(reach), gain),
        weights=row_w,
        outs=like(probs, low, (SEQ_CB, F32), low),
        raw_out=(),
        scratch=held(1),
        micros=12.5,
    )
    col_w, forward_w = mover.gather_last(a2)
    q2, k2, v2, p2, o2, x2, a3 = run(
        col_forward,
        args=(x1, a2, gain),
        weights=col_w,
        outs=like(low, low, low, col_probs, low, (SEQ_CB, F32), low),
        raw_out=(),
        scratch=held(4),
        micros=15.5,
    )
    token = (TOK, D)
    out, e2, dg3, *forward_g = run(
        feed_forward,
        args=(x2, a3, cot, gain),
        weights=forward_w,
        outs=like(low, (SEQ_CB, F32), row_gain, *pieces(2)),
        raw_out=range(3, 9),
        scratch=[VM(token, F32)] * 2 + [VM(token, LOW)] * 3 + [held(8)[0], terms(8)[0]]
        + [DMA((16,))] * 2,
        micros=26,
    )
    gate = mover.reduce_forward(*forward_g)
    dq2, dk2, dv2 = run(
        col_attend_back,
        args=(after(e2, *gate), q2, k2, v2, p2),
        weights=col_w,
        outs=like(low, low, low),
        raw_out=(),
        scratch=[VM(SEQ_CB, LOW)] + [VM(SEQ_CB, F32)] * 2 + held(1),
        micros=10.5,
    )
    gate = mover.reduce_forward_sides(dq2)
    dq2 = after(dq2, *gate)
    e1, dg2, *col_g = run(
        col_project_back,
        args=(e2, o2, dq2, dk2, dv2, a2, x1, gain),
        weights=col_w,
        outs=like((SEQ_CB, F32), row_gain, *pieces(1)),
        raw_out=range(2, 8),
        scratch=[VM(SEQ_CB, F32), held(3)[0], terms(4)[0], DMA((6,)), DMA((8,))],
        micros=11.5,
    )
    gate = mover.reduce_col(*col_g)
    dq, dke, dve, *row_g = run(
        row_backward,
        args=(after(e1, *gate), o1, q, ke, ve, p1, a1e),
        weights=row_w,
        outs=like(low, wide, wide, *pieces(1)),
        raw_out=range(3, 9),
        scratch=[VM(SEQ_CB, LOW)] + [held(1)[0], terms(4)[0], DMA((2,)), DMA((8,))],
        micros=20,
    )
    gate = mover.reduce_row(dq, *row_g)
    inner, to_low, to_high, dg1 = run(
        input_project,
        args=(after(dq, *gate), dke, dve, tokens, from_low, from_high),
        weights=row_w,
        outs=like((SEQ_CB, F32), (RIM, LOW), (RIM, LOW), row_gain),
        raw_out=(),
        scratch=[VM(SEQ_EXT, F32)] + held(3),
        micros=8,
    )
    gains = jnp.concatenate([dg1, dg2, dg3], axis=0)
    gains = mover.reduce_last(gains)
    to_high, to_low, *_ = together(to_high, to_low, *mover.rim_gate)
    from_low, from_high = neighbours(to_high, to_low)
    (grad,) = run_kernel(
        input_finish,
        (),
        (after(inner, *mover.last_gate), from_low, from_high, e1, tokens, gain),
        None,
        like(low),
        (),
        (),
        3,
    )
    weight_grad, grad = mover.total(grad)
    return out, grad, weight_grad, gains


def per_device(
    alignment,
    cotangent,
    row_counts,
    band_reach,
    master_weights,
    weight_moment,
    weight_square,
    norm_gains,
    gain_moment,
    gain_square,
):
    staged = lax.axis_size("cols") == NMAT and lax.axis_size("fsdp") == 2
    mover = Staged() if staged else Native()
    out, grad, weight_total, gain_grad = layer(
        alignment.reshape(SEQ, CB, D),
        cotangent.reshape(SEQ, CB, D),
        row_counts[:, 0],
        band_reach[:, 0],
        mover,
        master_weights.astype(LOW),
        norm_gains.astype(LOW),
    )
    gain_total = mover.own_gains(gain_grad, norm_gains.shape[0])
    new_weights, new_moment, new_square = adamw(
        master_weights,
        weight_moment,
        weight_square,
        weight_total.reshape(master_weights.shape),
        D ** (-0.5),
        DECAY,
        STEP_NUMBER,
    )
    new_gains, new_gain_moment, new_gain_square = adamw(
        norm_gains, gain_moment, gain_square, gain_total, RATE_GAIN, 0.0, STEP_NUMBER
    )
    shape = (MB, 1, ROWS, CB, D)
    return (
        out.reshape(shape),
        grad.reshape(shape),
        new_weights,
        new_moment,
        new_square,
        new_weights.astype(LOW),
        new_gains,
        new_gain_moment,
        new_gain_square,
    )


def solution(mesh):
    tokens = P(None, "fsdp", None, "cols", None)
    rows = P(("cols", "fsdp"), None)
    flat = P(("cols", "fsdp"))
    in_specs = (
        tokens,
        tokens,
        P(None, "fsdp"),
        P(None, "fsdp", None, "cols"),
        rows,
        rows,
        rows,
        flat,
        flat,
        flat,
    )
    out_specs = (tokens, tokens, rows, rows, rows, rows, flat, flat, flat)
    return jax.shard_map(
        per_device, mesh=mesh, in_specs=in_specs, out_specs=out_specs, check_vma=False
    )
```

```python
from functools import partial

import jax
import jax.numpy as jnp
from jax import lax
from jax.experimental import pallas as pl
from jax.experimental.pallas import tpu as pltpu
from jax.sharding import PartitionSpec as P

D = 768
H = 12
DH = 64
FF = 3072
NMAT = 16
ROWS = 4
CB = 64
HALO = 32
MB = 2
EXT = CB + 2 * HALO
SEQ = MB * ROWS
TOK = SEQ * CB
PAIRS = H // 2
LANES = 128
FOLD = FF // D
SPAN = D // 2
PART = SPAN // 2
EXTRA = 16
PER_GROUP = 10

EPS = 1e-05
BETA_ONE = 0.9
BETA_TWO = 0.999
ADAM_EPS = 1e-08
DECAY = 0.01
RATE_GAIN = 0.3
STEP_NUMBER = 10.0
MASKED = -1e30
F32 = jnp.float32
LOW = jnp.bfloat16


def dot_nn(a, b):
    return lax.dot_general(a, b, (((1,), (0,)), ((), ())), preferred_element_type=F32)


def dot_nt(a, b):
    return lax.dot_general(a, b, (((1,), (1,)), ((), ())), preferred_element_type=F32)


def dot_tn(a, b):
    return lax.dot_general(a, b, (((0,), (0,)), ((), ())), preferred_element_type=F32)


def standardize(values):
    center = values - jnp.mean(values, axis=-1, keepdims=True)
    spread = lax.rsqrt(jnp.mean(center * center, axis=-1, keepdims=True) + EPS)
    return center * spread, spread


def norm_pull(upward, values, gain):
    scaled, spread = standardize(values)
    weighted = upward * gain
    result = spread * (
        weighted
        - jnp.mean(weighted, axis=-1, keepdims=True)
        - scaled * jnp.mean(weighted * scaled, axis=-1, keepdims=True)
    )
    return result, jnp.sum(upward * scaled, axis=0, keepdims=True)


def lane_window(pair):
    return pl.ds(pl.multiple_of(pair * LANES, LANES), LANES)


def side_by_side(ref, micro, window):
    return jnp.concatenate([ref[micro * ROWS + r, :, window] for r in range(ROWS)], axis=1)


def head_stack(packed):
    lane = lax.broadcasted_iota(jnp.int32, packed.shape, 1)
    first = (lane % LANES) < DH
    zero = jnp.zeros_like(packed)
    return jnp.concatenate([jnp.where(first, packed, zero), jnp.where(first, zero, packed)], axis=0)


def head_merge(stacked, r):
    block = stacked[:, r * LANES : (r + 1) * LANES]
    lane = lax.broadcasted_iota(jnp.int32, (CB, LANES), 1)
    return jnp.where(lane < DH, block[:CB], block[CB:])


def head_sums():
    feature = lax.broadcasted_iota(jnp.int32, (D, LANES), 0)
    head = lax.broadcasted_iota(jnp.int32, (D, LANES), 1)
    return (feature // DH == head).astype(F32).astype(LOW)


def head_spread():
    head = lax.broadcasted_iota(jnp.int32, (LANES, D), 0)
    feature = lax.broadcasted_iota(jnp.int32, (LANES, D), 1)
    return (feature // DH == head).astype(F32).astype(LOW)


FULL = SPAN + EXTRA
STARTS = (0, FULL, 2 * FULL, 3 * FULL, 3 * FULL + PART)


def spot(buffers, number, row):
    if len(buffers) == 5:
        return buffers[number], row
    start = STARTS[number]
    if len(buffers) == 2 and number >= 3:
        return buffers[1], start - 3 * FULL + row
    return buffers[0], start + row


def regroup(sizes, refs):
    groups, start = [], 0
    for size in sizes:
        groups.append(refs[start : start + size])
        start += size
    return groups


def fetch_matrix(place, sources, table, matrix, target, sems, base):
    y_rel = jnp.where(place[1] == matrix // 2, 0, 1)
    waits = []
    for x in range(2):
        x_rel = jnp.where(place[0] == x, 0, 1)
        block = 2 * y_rel + x_rel
        sem = sems.at[base + x]
        for index in sorted(set(table)):
            here = None
            for plane, chosen in enumerate(table):
                if chosen == index:
                    hit = place[3] == plane
                    here = hit if here is None else jnp.logical_or(here, hit)
            for core_rel in range(2):
                held = jnp.logical_and(here, place[2] == (matrix % 2) ^ core_rel)
                buffers = sources[2 * index + core_rel]
                for number in range(5):
                    source, row = spot(buffers, number, 0)
                    size = SPAN if number < 3 else PART
                    to = x * SPAN + (PART if number == 4 else 0)
                    part = pltpu.make_async_copy(
                        source.at[pl.ds(row, size)], target.at[pl.ds(to, size)], sem
                    )
                    pl.when(jnp.logical_and(held, block == min(number, 3)))(part.start)
                    if number == 0:
                        copy = part
        waits.append(copy)
    return waits


def fetch(place, sources, table, matrices, w, sems, first=0):
    waits = []
    for slot, matrix in enumerate(matrices):
        slot += first
        waits.append(
            fetch_matrix(place, sources, table, matrix, w.at[slot], sems, 2 * slot)
        )
    return waits


def settle(waits):
    for copy in waits:
        copy.wait()


def emit_matrix(place, source, matrix, n, out, sems, base):
    *keep, rest, corner = out
    core_same = place[2] == matrix % 2
    y_rel = jnp.where(place[1] == matrix // 2, 0, 1)
    waits = []
    for x in range(2):
        x_rel = jnp.where(place[0] == x, 0, 1)
        spot_rel = 2 * y_rel + x_rel
        block = source.at[pl.ds(x * SPAN, SPAN)]
        sem = sems.at[base + x]
        sent = jnp.logical_not(core_same)
        for number, target in enumerate(keep):
            kept = pltpu.make_async_copy(block, target.at[n], sem)
            pl.when(jnp.logical_and(core_same, spot_rel == number))(kept.start)
        near = pltpu.make_async_copy(block, rest.at[jnp.minimum(spot_rel, 2), n], sem)
        far = pltpu.make_async_copy(block, corner.at[n], sem)
        pl.when(jnp.logical_and(sent, spot_rel < 3))(near.start)
        pl.when(jnp.logical_and(sent, spot_rel == 3))(far.start)
        waits.append(far)
    return waits


def gain_copies(sources, group, target, sem):
    copies = []
    for core_rel in range(2):
        buffers = sources[2 * group + core_rel]
        for number, row in ((0, SPAN), (1, SPAN), (2, SPAN), (4, PART)):
            source, row = spot(buffers, number, row)
            copy = pltpu.make_async_copy(
                source.at[pl.ds(row, EXTRA)], target.at[len(copies)], sem.at[len(copies)]
            )
            copies.append(copy)
    return copies


def row_project(
    spec, count, scal, place, tokens, from_low, from_high, *refs
):
    table, group = spec
    sources, (a1e, q, ke, ve, gain, w, held, sems, gain_sems) = regroup(count, refs), refs[sum(count) :]
    parts = gain_copies(sources, group, held, gain_sems)
    for copy in parts:
        copy.start()
    copies = fetch(place, sources, table, range(3), w, sems)
    settle(parts)
    total = held[0].astype(F32)
    for k in range(1, 8):
        total = total + held[k].astype(F32)
    gain[...] = total[:3]

    def norm_step(i, _):
        for source, start, size in (
            (from_low, 0, HALO),
            (tokens, HALO, CB),
            (from_high, HALO + CB, HALO),
        ):
            scaled, _s = standardize(source[i].astype(F32))
            a1e[i, start : start + size] = (scaled * gain[0:1]).astype(LOW)
        return 0

    lax.fori_loop(0, SEQ, norm_step, 0, unroll=True)
    wide = a1e[...].reshape(SEQ * EXT, D)
    settle(copies[1])
    ke[...] = dot_nn(wide, w[1]).astype(LOW).reshape(SEQ, EXT, D)
    settle(copies[2])
    ve[...] = dot_nn(wide, w[2]).astype(LOW).reshape(SEQ, EXT, D)
    inner = a1e[:, HALO : HALO + CB, :].reshape(TOK, D)
    settle(copies[0])
    q[...] = dot_nn(inner, w[0]).astype(LOW).reshape(SEQ, CB, D)
    for i in range(SEQ):
        q[i] = (q[i].astype(F32) * scal[i // ROWS, 1 + i % ROWS]).astype(LOW)


def row_attend(
    table, count, scal, place, tokens, q, ke, ve, allowed, gain, *refs
):
    sources, (p1, o1, x1, a2, w, sems) = regroup(count, refs), refs[sum(count) :]
    copies = fetch(place, sources, table, (3,), w, sems)

    def attend(pair, _):
        window = lane_window(pair)
        for m in range(MB):
            query = head_stack(side_by_side(q, m, window))
            scores = dot_nt(query, side_by_side(ke, m, window)) * scal[m, 0]
            mask = allowed[m]
            mask = jnp.concatenate([mask, mask], axis=0)
            scores = jnp.where(mask > 0, scores, MASKED)
            weight = jnp.exp(scores - jnp.max(scores, axis=-1, keepdims=True))
            prob = weight / jnp.sum(weight, axis=-1, keepdims=True)
            p1[m, pair] = prob
            mixed = dot_nn(prob.astype(LOW), side_by_side(ve, m, window))
            for r in range(ROWS):
                o1[m * ROWS + r, :, window] = head_merge(mixed, r).astype(LOW)
        return 0

    lax.fori_loop(0, PAIRS, attend, 0, unroll=True)
    settle(copies[0])
    x1[...] = tokens[...].astype(F32) + dot_nn(o1[...].reshape(TOK, D), w[0]).reshape(SEQ, CB, D)

    def next_norm(i, _):
        scaled, _s = standardize(x1[i])
        a2[i] = (scaled * gain[1:2]).astype(LOW)
        return 0

    lax.fori_loop(0, SEQ, next_norm, 0, unroll=True)


def col_forward(table, count, scal, place, x1, a2, gain, *refs):
    sources, (q2, k2, v2, p2, o2, x2, a3, w, sems) = regroup(count, refs), refs[sum(count) :]
    copies = fetch(place, sources, table, range(4), w, sems)
    for j in range(3):
        settle(copies[j])
    flat = a2[...].reshape(TOK, D)
    q2[...] = dot_nn(flat, w[0]).astype(LOW).reshape(SEQ, CB, D)
    k2[...] = dot_nn(flat, w[1]).astype(LOW).reshape(SEQ, CB, D)
    v2[...] = dot_nn(flat, w[2]).astype(LOW).reshape(SEQ, CB, D)
    sums = head_sums()
    spread = head_spread()

    def attend(i, _):
        micro = i // ROWS
        query = q2[i].astype(F32)
        products = jnp.concatenate(
            [(query * k2[micro * ROWS + s].astype(F32)).astype(LOW) for s in range(ROWS)], axis=0
        )
        scores = dot_nn(products, sums) * (DH ** (-0.5))
        parts = [
            jnp.where(scal[micro, 1 + s] > 0, scores[s * CB : (s + 1) * CB], MASKED)
            for s in range(ROWS)
        ]
        top = jnp.maximum(jnp.maximum(parts[0], parts[1]), jnp.maximum(parts[2], parts[3]))
        parts = [jnp.exp(part - top) for part in parts]
        scale = 1.0 / (parts[0] + parts[1] + parts[2] + parts[3])
        prob = jnp.concatenate([part * scale for part in parts], axis=0)
        p2[i] = prob
        wide = dot_nn(prob.astype(LOW), spread)
        total = wide[:CB] * v2[micro * ROWS].astype(F32)
        for s in range(1, ROWS):
            total = total + wide[s * CB : (s + 1) * CB] * v2[micro * ROWS + s].astype(F32)
        o2[i] = total.astype(LOW)
        return 0

    lax.fori_loop(0, SEQ, attend, 0, unroll=True)
    settle(copies[3])
    x2[...] = x1[...] + dot_nn(o2[...].reshape(TOK, D), w[3]).reshape(SEQ, CB, D)

    def next_norm(i, _):
        scaled, _s = standardize(x2[i])
        a3[i] = (scaled * gain[2:3]).astype(LOW)
        return 0

    lax.fori_loop(0, SEQ, next_norm, 0, unroll=True)


CHUNK = 256


def feed_forward(tables, count, scal, place, x2, a3, cot, gain, *refs):
    sources, refs = regroup(count, refs), refs[sum(count) :]
    out, e2, dgain, *terms_out, up, down, live_cot, gl, dhd, w, dw, in_sems, out_sems = refs
    copies = []
    for n in range(2):
        copies += fetch(place, sources, tables[n], range(4), w, in_sems, 4 * n)
    for i in range(SEQ):
        live_cot[i * CB : (i + 1) * CB] = (
            cot[i].astype(F32) * scal[i // ROWS, 1 + i % ROWS]
        ).astype(LOW)
    normed = a3[...].reshape(TOK, D)
    grad = live_cot[...]
    waits = []
    for step in range(FOLD):
        settle(copies[step])
        settle(copies[FOLD + step])
        win = w[step]
        wout = w[FOLD + step]
        for base in range(0, TOK, CHUNK):
            rows = slice(base, base + CHUNK)
            hidden = dot_nn(normed[rows], win)
            pulled = dot_nt(grad[rows], wout)
            half = 0.5 * lax.erf(hidden * (0.5**0.5)) + 0.5
            gl[rows] = (hidden * half).astype(LOW)
            slope = half + hidden * (jnp.exp(-0.5 * hidden * hidden) * ((2.0 * jnp.pi) ** -0.5))
            dhd[rows] = (pulled * slope).astype(LOW)
        for n, value in enumerate((dot_tn(normed, dhd[...]), dot_tn(gl[...], grad))):
            slot = 4 * n + step
            dw[slot] = value.astype(LOW)
            waits += emit_matrix(place, dw.at[slot], step, n, terms_out, out_sems, 2 * slot)
        forward = dot_nn(gl[...], wout)
        backward = dot_nt(dhd[...], win)
        if step == 0:
            up[...] = forward
            down[...] = backward
        else:
            up[...] += forward
            down[...] += backward
    total = jnp.zeros((1, D), F32)
    for i in range(SEQ):
        rows = slice(i * CB, (i + 1) * CB)
        value = x2[i]
        out[i] = ((value + up[rows]) * scal[i // ROWS, 1 + i % ROWS]).astype(LOW)
        part, gain_part = norm_pull(down[rows], value, gain[2:3])
        e2[i] = live_cot[rows].astype(F32) + part
        total = total + gain_part
    dgain[...] = total
    settle(waits)


def col_attend_back(table, count, scal, place, e2, q2, k2, v2, p2, *refs):
    sources, refs = regroup(count, refs), refs[sum(count) :]
    dq2, dk2, dv2, do2, dka, dva, w, in_sems = refs
    copies = fetch(place, sources, table, (3,), w, in_sems)
    low = e2[...].reshape(TOK, D).astype(LOW)
    settle(copies[0])
    do2[...] = dot_nt(low, w[0]).astype(LOW).reshape(SEQ, CB, D)
    sums = head_sums()
    spread = head_spread()
    dka[...] = jnp.zeros_like(dka)
    dva[...] = jnp.zeros_like(dva)

    def pull(i, _):
        micro = i // ROWS
        upward = do2[i].astype(F32)
        products = jnp.concatenate(
            [(upward * v2[micro * ROWS + s].astype(F32)).astype(LOW) for s in range(ROWS)], axis=0
        )
        dprob = dot_nn(products, sums)
        prob = p2[i]
        mixed = prob * dprob
        inner = mixed[:CB] + mixed[CB : 2 * CB] + mixed[2 * CB : 3 * CB] + mixed[3 * CB :]
        dscore = prob * (dprob - jnp.concatenate([inner] * ROWS, axis=0))
        wide = dot_nn(prob.astype(LOW), spread)
        dwide = dot_nn(dscore.astype(LOW), spread)
        query = q2[i].astype(F32)
        total = jnp.zeros((CB, D), F32)
        for s in range(ROWS):
            rows = slice(s * CB, (s + 1) * CB)
            total = total + dwide[rows] * k2[micro * ROWS + s].astype(F32)
            dka[micro * ROWS + s] += dwide[rows] * query
            dva[micro * ROWS + s] += wide[rows] * upward
        dq2[i] = (total * (DH ** (-0.5))).astype(LOW)
        return 0

    lax.fori_loop(0, SEQ, pull, 0, unroll=True)
    dk2[...] = (dka[...] * (DH ** (-0.5))).astype(LOW)
    dv2[...] = dva[...].astype(LOW)


def col_project_back(table, count, scal, place, e2, o2, dq2, dk2, dv2, a2, x1, gain, *refs):
    sources, refs = regroup(count, refs), refs[sum(count) :]
    e1, dgain, *terms_out, acc, w, dw, in_sems, out_sems = refs
    copies = fetch(place, sources, table, range(3), w, in_sems)
    flat = a2[...].reshape(TOK, D)
    low = e2[...].reshape(TOK, D).astype(LOW)
    dw[3] = dot_tn(o2[...].reshape(TOK, D), low).astype(LOW)
    waits = emit_matrix(place, dw.at[3], 3, 0, terms_out, out_sems, 6)
    for j, ref in enumerate((dq2, dk2, dv2)):
        grads = ref[...].reshape(TOK, D)
        dw[j] = dot_tn(flat, grads).astype(LOW)
        waits += emit_matrix(place, dw.at[j], j, 0, terms_out, out_sems, 2 * j)
        settle(copies[j])
        part = dot_nt(grads, w[j]).reshape(SEQ, CB, D)
        if j == 0:
            acc[...] = part
        else:
            acc[...] += part
    gain_total = jnp.zeros((1, D), F32)
    for i in range(SEQ):
        part, gain_part = norm_pull(acc[i], x1[i], gain[1:2])
        e1[i] = e2[i] + part
        gain_total = gain_total + gain_part
    dgain[...] = gain_total
    settle(waits)


def row_backward(table, count, scal, place, e1, o1, q, ke, ve, p1, a1e, *refs):
    sources, refs = regroup(count, refs), refs[sum(count) :]
    dq, dke, dve, *terms_out, do1, w, dw, in_sems, out_sems = refs
    copies = fetch(place, sources, table, (3,), w, in_sems)
    low = e1[...].reshape(TOK, D).astype(LOW)
    settle(copies[0])
    do1[...] = dot_nt(low, w[0]).astype(LOW).reshape(SEQ, CB, D)

    def pull(pair, _):
        window = lane_window(pair)
        for m in range(MB):
            query = head_stack(side_by_side(q, m, window))
            upward = head_stack(side_by_side(do1, m, window))
            prob = p1[m, pair]
            dprob = dot_nt(upward, side_by_side(ve, m, window))
            dscore = prob * (dprob - jnp.sum(prob * dprob, axis=-1, keepdims=True))
            dscore = dscore.astype(LOW)
            dvalue = dot_tn(prob.astype(LOW), upward)
            dkey = dot_tn(dscore, query) * scal[m, 0]
            dquery = dot_nn(dscore, side_by_side(ke, m, window)) * scal[m, 0]
            for r in range(ROWS):
                lanes = slice(r * LANES, (r + 1) * LANES)
                dve[m * ROWS + r, :, window] = dvalue[:, lanes].astype(LOW)
                dke[m * ROWS + r, :, window] = dkey[:, lanes].astype(LOW)
                dq[m * ROWS + r, :, window] = (head_merge(dquery, r) * scal[m, 1 + r]).astype(LOW)
        return 0

    lax.fori_loop(0, PAIRS, pull, 0, unroll=True)
    wide = a1e[...].reshape(SEQ * EXT, D)
    own = a1e[:, HALO : HALO + CB, :].reshape(TOK, D)
    waits = []
    for j, (left, right) in enumerate(
        (
            (own, dq[...].reshape(TOK, D)),
            (wide, dke[...].reshape(SEQ * EXT, D)),
            (wide, dve[...].reshape(SEQ * EXT, D)),
            (o1[...].reshape(TOK, D), low),
        )
    ):
        dw[j] = dot_tn(left, right).astype(LOW)
        waits += emit_matrix(place, dw.at[j], j, 0, terms_out, out_sems, 2 * j)
    settle(waits)


def input_project(
    table, count, scal, place, dq, dke, dve, tokens, from_low, from_high, *refs
):
    sources, (inner, to_low, to_high, dgain, acc, w, sems) = regroup(count, refs), refs[sum(count) :]
    copies = fetch(place, sources, table, range(3), w, sems)
    settle(copies[1])
    acc[...] = dot_nt(dke[...].reshape(SEQ * EXT, D), w[1]).reshape(SEQ, EXT, D)
    settle(copies[2])
    acc[...] += dot_nt(dve[...].reshape(SEQ * EXT, D), w[2]).reshape(SEQ, EXT, D)
    settle(copies[0])
    acc[:, HALO : HALO + CB, :] += dot_nt(dq[...].reshape(TOK, D), w[0]).reshape(SEQ, CB, D)
    total = jnp.zeros((1, D), F32)
    for i in range(SEQ):
        for source, start, size in (
            (from_low, 0, HALO),
            (tokens, HALO, CB),
            (from_high, HALO + CB, HALO),
        ):
            scaled, _s = standardize(source[i].astype(F32))
            total = total + jnp.sum(acc[i, start : start + size] * scaled, axis=0, keepdims=True)
    dgain[...] = total
    inner[...] = acc[:, HALO : HALO + CB, :]
    to_low[...] = acc[:, :HALO, :].astype(LOW)
    to_high[...] = acc[:, HALO + CB :, :].astype(LOW)


def input_finish(inner, from_low, from_high, e1, tokens, gain, grad):
    def step(i, _):
        upward = jnp.concatenate(
            [
                inner[i, :HALO] + from_low[i].astype(F32),
                inner[i, HALO:] + from_high[i].astype(F32),
            ],
            axis=0,
        )
        part, _g = norm_pull(upward, tokens[i].astype(F32), gain[0:1])
        grad[i] = (e1[i] + part).astype(LOW)
        return 0

    lax.fori_loop(0, SEQ, step, 0, unroll=True)


def in_vmem(count):
    return [pl.BlockSpec(memory_space=pltpu.VMEM)] * count


def like(*shapes):
    return tuple(jax.ShapeDtypeStruct(shape, dtype) for shape, dtype in shapes)


SEQ_CB = (SEQ, CB, D)
SEQ_EXT = (SEQ, EXT, D)
RIM = (SEQ, HALO, D)
PER_MICRO = 1.15e9
VM = pltpu.VMEM
DMA = pltpu.SemaphoreType.DMA


ROOM = {col_attend_back: 40, col_project_back: 40, row_backward: 40, input_project: 40, input_finish: 40}


def pieces(count):
    return (
        *(((count, SPAN, D), LOW),) * 4,
        ((3, count, SPAN, D), LOW),
        ((count, SPAN, D), LOW),
    )


def run_kernel(body, scalars, args, weights, outs, raw_out, scratch, micros):
    vmem = pl.BlockSpec(memory_space=pltpu.VMEM)
    raw = pl.BlockSpec(memory_space=pltpu.HBM)
    moved = sum(a.size * a.dtype.itemsize for a in args)
    moved += sum(o.size * jnp.dtype(o.dtype).itemsize for o in outs)
    call = body
    sources = ()
    if weights is not None:
        table, groups = weights
        sources = [buffer for group in groups for buffer in group]
        call = partial(body, table, tuple(len(group) for group in groups))
    return pl.pallas_call(
        call,
        name=body.__name__,
        out_shape=outs,
        in_specs=[pl.BlockSpec(memory_space=pltpu.SMEM)] * len(scalars)
        + [vmem] * len(args)
        + [raw] * len(sources),
        out_specs=tuple(raw if i in raw_out else vmem for i in range(len(outs))),
        scratch_shapes=scratch,
        compiler_params=pltpu.CompilerParams(vmem_limit_bytes=ROOM.get(body, 60) << 20),
        cost_estimate=pl.CostEstimate(
            flops=int(micros * PER_MICRO), bytes_accessed=moved, transcendentals=0
        ),
    )(*scalars, *args, *sources)


def held(count):
    return [VM((count, D, D), LOW), DMA((2 * count,))]


def terms(count):
    return [VM((count, D, D), LOW), DMA((2 * count,))]


def corner_terms(keep, got, half_a, half_b):
    total = keep[...].astype(F32) + got[...].astype(F32)
    half_a[...] = total[:, :PART].astype(LOW)
    half_b[...] = total[:, PART:].astype(LOW)


def side_terms(keep_x, got_x, keep_y, got_y, half_a, half_b, *outs):
    count = len(outs) // 2
    for n in range(count):
        over_x, over_y = outs[n], outs[count + n]
        total = keep_x[n].astype(F32) + got_x[0, n].astype(F32)
        over_x[0, :PART] = (total[:PART] + half_a[n].astype(F32)).astype(LOW)
        over_x[0, PART:] = total[PART:].astype(LOW)
        total = keep_y[n].astype(F32) + got_y[0, n].astype(F32)
        over_y[0, :PART] = total[:PART].astype(LOW)
        over_y[0, PART:] = (total[PART:] + half_b[n].astype(F32)).astype(LOW)


def own_terms(keep, got, from_x, from_y, total, low):
    value = keep[0].astype(F32) + got[0, 0].astype(F32)
    value = value + from_x[0].astype(F32) + from_y[0].astype(F32)
    total[0] = value
    low[0] = value.astype(LOW)


SPLIT = 2


def call_small(body, args, picks, shapes):
    count = args[0].shape[0]
    width = D // SPLIT
    specs = []
    for arg, pick in zip(args, picks):
        if pick is None:
            specs.append(pl.BlockSpec((*arg.shape[:-1], width), lambda j: (0, 0, j)))
        elif isinstance(pick, tuple) and pick[0] == "keep":
            specs.append(pl.BlockSpec((1, SPAN, width), lambda j, k=pick[1]: (k, 0, j)))
        elif isinstance(pick, tuple):
            specs.append(
                pl.BlockSpec((1, 1, SPAN, width), lambda j, k=pick[1]: (0, k, 0, j))
            )
        elif isinstance(pick, int):
            specs.append(
                pl.BlockSpec((1, count, SPAN, width), lambda j, k=pick: (k, 0, 0, j))
            )
    moved = sum(s.block_shape[-2] * D * count * 2 for s in specs)
    return pl.pallas_call(
        body,
        name=body.__name__,
        grid=(SPLIT,),
        out_shape=tuple(
            jax.ShapeDtypeStruct((*shape, D), dtype) for shape, dtype in shapes
        ),
        in_specs=specs,
        out_specs=tuple(
            pl.BlockSpec((*shape, width), lambda j: (0, 0, j)) for shape, _d in shapes
        ),
        compiler_params=pltpu.CompilerParams(vmem_limit_bytes=24 << 20),
        cost_estimate=pl.CostEstimate(
            flops=int(8 * PER_MICRO), bytes_accessed=moved, transcendentals=0
        ),
    )(*args)


def swap_pairs(count, bit):
    return [(i, i ^ bit) for i in range(count)]


def after(value, *before):
    return lax.optimization_barrier((value, *before))[0]


def add(*parts):
    total = parts[0].astype(F32)
    for part in parts[1:]:
        total = total + part.astype(F32)
    return total


def together(*values):
    return lax.optimization_barrier(values)


class Staged:
    planes = 4
    tables = ((0, 1, 2, 2), (1, 0, 1, 3), (2, 2, 0, 1), (3, 3, 3, 0))

    def __init__(self):
        self.count = NMAT
        self.step = NMAT // self.planes
        cols = lax.axis_index("cols")
        self.z = cols // self.step
        self.place = jnp.stack(
            [lax.axis_index("fsdp"), (cols // 2) % 2, cols % 2, self.z]
        ).astype(jnp.int32)

    def over_x(self, value):
        return lax.ppermute(value, "fsdp", [(0, 1), (1, 0)])

    def over_y(self, value):
        return lax.ppermute(value, "cols", swap_pairs(self.count, 2))

    def over_core(self, value):
        return lax.ppermute(value, "cols", swap_pairs(self.count, 1))

    def over_z(self, value, pairs):
        step = self.step
        full = [(a * step + i, b * step + i) for a, b in pairs for i in range(step)]
        return lax.ppermute(value, "cols", full)

    def by_plane(self, options):
        result = options[-1]
        for index in range(len(options) - 2, -1, -1):
            result = jnp.where(self.z == index, options[index], result)
        return result

    def own_place(self, gains):
        index = lax.axis_index("cols") * 2 + lax.axis_index("fsdp")
        spread = jnp.zeros((EXTRA * D,), LOW)
        spread = lax.dynamic_update_slice(spread, gains, (index * gains.shape[0],))
        return spread.reshape(EXTRA, D)

    def sum_step(self, value, index):
        swaps = (
            self.over_core,
            self.over_x,
            self.over_y,
            lambda v: self.over_z(v, [(0, 1), (1, 0), (2, 3), (3, 2)]),
            lambda v: self.over_z(v, [(0, 2), (2, 0), (1, 3), (3, 1)]),
        )
        return value + swaps[index](value)

    def own_gains(self, value, size):
        value = value.reshape(3 * D)
        index = lax.axis_index("cols") * 2 + lax.axis_index("fsdp")
        return lax.dynamic_slice(value, (index * size,), (size,))

    def halves(self, from_x, from_y):
        return self.over_y(from_x[:PART]), self.over_x(from_y[PART:])

    def gather(self, shard, gains, tokens):
        core = self.over_core
        own1 = jnp.concatenate([shard, self.own_place(gains)], axis=0)
        up1 = self.over_z(own1, [(0, 1), (1, 2), (2, 3)])
        down1 = self.over_z(own1, [(3, 2), (2, 1), (1, 0)])
        x1, y1 = self.over_x(own1), self.over_y(own1)
        up1, down1, x1, y1 = together(up1, down1, x1, y1)
        own2 = jnp.where(self.z == 0, down1, up1)
        x2, y2 = self.over_x(own2), self.over_y(own2)
        a1, b1 = self.halves(x1, y1)
        up2 = self.over_z(up1, [(1, 2), (2, 3)])
        down2 = self.over_z(down1, [(2, 1), (1, 0)])
        rims = neighbours(*after((tokens[:, CB - HALO :], tokens[:, :HALO]), x1))
        c1 = [core(own1)]
        up2, down2, a1, b1, x2, y2, *rims = together(up2, down2, a1, b1, x2, y2, *rims)
        up3 = self.over_z(up2, [(2, 3)])
        down3 = self.over_z(down2, [(1, 0)])
        a2, b2 = self.halves(x2, y2)
        c1 += [core(x1), core(y1), core(a1), core(b1)]
        up3, down3, a2, b2, *c1 = together(up3, down3, a2, b2, *c1)
        own3 = self.by_plane([down2, down1, up2, up3])
        placed = [v[SPAN:] for v in (own1, up1, up2, up3, down1, down2, down3)]
        own3 = jnp.concatenate([own3[:SPAN], add(*placed).astype(LOW)], axis=0)
        x3, y3 = self.over_x(own3), self.over_y(own3)
        c2 = [core(v) for v in (own2, x2, y2, a2, b2)]
        x3, y3, *c2 = together(x3, y3, *c2)
        a3, b3 = self.halves(x3, y3)
        c3 = [core(own3), core(x3), core(y3)]
        own4 = self.by_plane([down3, down2, down1, up2])
        a3, b3, own4, *c3 = together(a3, b3, own4, *c3)
        x4, y4 = self.over_x(own4), self.over_y(own4)
        c3 += [core(a3), core(b3)]
        self.row_gate = (own4,)
        self.fourth = own4, x4, y4
        self.first = ((own1, x1, y1, a1, b1), tuple(c1), (own2, x2, y2, a2, b2), tuple(c2))
        self.first += ((own3, x3, y3, a3, b3), tuple(c3))
        return (self.tables[0], self.first), 2, rims

    def gather_more(self, seen):
        own4, x4, y4 = self.fourth
        x4, y4, seen = together(x4, y4, seen)
        xa, yb = x4[:PART], y4[PART:]
        self.attend_gate = (xa, yb)
        core = self.over_core
        self.fourth = own4, x4, y4, self.over_y(xa), self.over_x(yb)
        self.fourth_core = [core(own4), core(x4), core(y4)]

    def gather_last(self, seen):
        own4, x4, y4, a4, b4 = self.fourth
        a4, b4, _ = together(a4, b4, seen)
        core = self.over_core
        c4 = (*self.fourth_core, core(a4), core(b4))
        every = (*self.first, (own4, x4, y4, a4, b4), c4)
        return (self.tables[1], every), (self.tables[2:], every)

    def corner_swap(self, keep, got):
        shapes = (((keep[3].shape[0], PART), LOW),) * 2
        return call_small(corner_terms, (keep[3], got), (None, None), shapes)

    def side_blocks(self, keep, got, corner_a, corner_b):
        picks = (None, 1, None, 2, None, None)
        args = (keep[1], got, keep[2], got, corner_a, corner_b)
        count = keep[0].shape[0]
        sides = call_small(side_terms, args, picks, (((1, SPAN), LOW),) * (2 * count))
        return sides[:count], sides[count:]

    def own_sum(self, keep, got, from_x, from_y, n=0):
        shapes = (((1, SPAN), F32), ((1, SPAN), LOW))
        picks = (("keep", n), ("got", n), None, None)
        total, low = call_small(own_terms, (keep[0], got, from_x, from_y), picks, shapes)
        return total[0], low[0]

    def reduce_forward(self, *terms):
        *keep, rest, corner = terms
        corner = self.over_core(corner)
        a, b = self.corner_swap(keep, corner)
        self.fwd = keep, self.over_core(after(rest, a, b))
        self.fwd_corner = self.over_y(a), self.over_x(b)
        return a, b

    def reduce_forward_sides(self, seen):
        a, b, _ = together(*self.fwd_corner, seen)
        (x2, x3), (y2, y3) = self.side_blocks(*self.fwd, a, b)
        self.first_sides = self.over_x(x2), self.over_y(y2)
        self.later_sides = x3, y3
        return x2, y2, x3, y3

    def reduce_col(self, *terms):
        *keep, rest, corner = terms
        corner = self.over_core(corner)
        fx, fy = together(*self.first_sides)
        a, b = after(self.later_sides, fx, fy)
        self.later_sides = self.over_x(a), self.over_y(b)
        a, b = self.corner_swap(keep, after(corner, a, b))
        self.col = keep, self.over_core(after(rest, a, b))
        self.col_corner = self.over_y(a), self.over_x(b)
        fx, fy, *_ = together(fx, fy, a, b)
        self.second, low = self.own_sum(*self.fwd, fx, fy, 0)
        self.near_second = self.over_z(low, [(0, 1), (3, 2)])
        return a, b, low

    def reduce_row(self, seen, *terms):
        *keep, rest, corner = terms
        corner = self.over_core(corner)
        a, b, fx, fy, near, _ = together(
            *self.col_corner, *self.later_sides, self.near_second, seen
        )
        (cx,), (cy,) = self.side_blocks(*self.col, a, b)
        corner = after(corner, cx, cy)
        cx, cy = self.over_x(cx), self.over_y(cy)
        a, b = self.corner_swap(keep, corner)
        got = self.over_core(after(rest, a, b))
        fx, fy, near, *_ = together(fx, fy, near, a, b)
        a, b = self.over_y(a), self.over_x(b)
        self.third, low = self.own_sum(*self.fwd, fx, fy, 1)
        self.near_third = self.over_z(low, [(0, 1), (2, 3)])
        self.second = add(self.second, near)
        second_low = self.second.astype(LOW)
        self.far_second = self.over_z(second_low, [(1, 2)])
        a, b, cx, cy, got, *_ = together(a, b, cx, cy, got, low, second_low)
        (rx,), (ry,) = self.side_blocks(keep, got, a, b)
        cx, cy, *_ = together(cx, cy, rx, ry)
        self.row = keep, got
        self.row_sides = self.over_x(rx), self.over_y(ry)
        self.col_sum, low = self.own_sum(*self.col, cx, cy)
        self.near_col = self.over_z(low, [(0, 1), (3, 2)])
        return rx, ry, low

    def reduce_last(self, gains):
        rx, ry, near_col, near, far_second, gains = together(
            *self.row_sides, self.near_col, self.near_third, self.far_second, gains
        )
        row, low = self.own_sum(*self.row, rx, ry)
        near_row = self.over_z(low, [(1, 0), (3, 2)])
        self.rim_gate = (low,)
        near_col, near, gains, _ = together(near_col, near, gains, low)
        col = add(self.col_sum, near_col)
        far_col = self.over_z(col.astype(LOW), [(2, 1)])
        third = add(self.third, near)
        far_third = self.over_z(third.astype(LOW), [(1, 3)])
        gains = gains.reshape(18, LANES)
        for index in range(4):
            gains = self.sum_step(gains, index)
        near_row, far_col, far_third, gains = together(near_row, far_col, far_third, gains)
        row = add(row, near_row)
        low = row.astype(LOW)
        far_row = self.over_z(low, [(2, 0)])
        self.last_gate = (low,)
        self.gains = gains
        forward = jnp.where(
            self.z == 2, add(self.second, far_second), add(third, far_third)
        )
        self.totals = row, far_row, jnp.where(self.z == 1, add(col, far_col), forward)

    def total(self, seen):
        row, far_row, rest = self.totals
        far_row, rest, seen, gains = together(far_row, rest, seen, self.gains)
        result = jnp.where(self.z == 0, add(row, far_row), rest)
        return result, seen, self.sum_step(gains, 4)


class Native:
    axes = ("cols", "fsdp")
    rim_gate = ()
    last_gate = ()
    row_gate = ()
    attend_gate = ()

    def __init__(self):
        self.place = jnp.zeros((4,), jnp.int32)
        self.parts = []

    def gather(self, shard, gains, tokens):
        full = lax.all_gather(shard, self.axes, axis=0, tiled=True)
        gains = lax.all_gather(gains, self.axes, axis=0, tiled=True)
        rims = neighbours(tokens[:, CB - HALO :], tokens[:, :HALO])
        row, *self.rest = self.arranged(full, gains)
        return row, 0, rims

    def gather_more(self, seen):
        pass

    def gather_last(self, seen):
        return self.rest

    def arranged(self, full, gains):
        blocks = full.reshape(4, 2, 2, 2 * SPAN, D).transpose(0, 2, 1, 3, 4)
        blocks = blocks.reshape(4, 2, 4, SPAN, D)
        extra = jnp.pad(gains.reshape(3, D), ((0, EXTRA - 3), (0, 0)))
        groups = []
        for b in range(4):
            parts = []
            for c in range(2):
                for k in range(3):
                    mine = extra if b == c == k == 0 else jnp.zeros_like(extra)
                    parts.append(jnp.concatenate([blocks[b, c, k], mine], axis=0))
                last = jnp.concatenate([blocks[b, c, 3], jnp.zeros_like(extra)], axis=0)
                parts += [last[:PART], last[PART:]]
            groups.append((tuple(parts[:5]), tuple(parts[5:])))
        row, col, low, high = groups
        flat = (0, 0, 0, 0)
        return (flat, row), (flat, col), ((flat, (1, 1, 1, 1)), (*low, *high))

    def own_gains(self, value, size):
        value = value.reshape(3 * D)
        return lax.psum_scatter(value, self.axes, scatter_dimension=0, tiled=True)

    def stash(self, *terms):
        *keep, rest, corner = terms
        sent = jnp.concatenate([rest, corner[None]], axis=0)
        blocks = jnp.stack([jnp.stack(keep), sent])
        blocks = blocks.reshape(2, 2, 2, *corner.shape)
        self.parts.insert(0, blocks.transpose(3, 1, 0, 2, 4, 5))
        return ()

    def reduce_forward(self, *terms):
        return self.stash(*terms)

    def reduce_forward_sides(self, seen):
        return ()

    def reduce_col(self, *terms):
        return self.stash(*terms)

    def reduce_row(self, seen, *terms):
        return self.stash(*terms)

    def reduce_last(self, gains):
        self.gains = gains

    def total(self, seen):
        full = jnp.concatenate([self.parts[0], self.parts[1], self.parts[2]], axis=0)
        full = full.reshape(NMAT * D, D)
        full = lax.psum_scatter(full, self.axes, scatter_dimension=0, tiled=True)
        return full.astype(F32), seen, self.gains


def neighbours(upward, downward):
    count = lax.axis_size("cols")
    forward = [(i, i + 1) for i in range(count - 1)]
    backward = [(target, source) for source, target in forward]
    return lax.ppermute(upward, "cols", forward), lax.ppermute(downward, "cols", backward)


def adamw(master, moment, square, grad_total, rate, decay, steps_done):
    moment_new = BETA_ONE * moment + (1.0 - BETA_ONE) * grad_total
    square_new = BETA_TWO * square + (1.0 - BETA_TWO) * grad_total * grad_total
    moment_fix = 1.0 - BETA_ONE**steps_done
    square_fix = 1.0 - BETA_TWO**steps_done
    update = moment_new / moment_fix / (jnp.sqrt(square_new / square_fix) + ADAM_EPS)
    return (master - rate * (update + decay * master), moment_new, square_new)


def band_mask(band_reach):
    first_col = lax.axis_index("cols") * CB
    col_total = CB * lax.axis_size("cols")
    query_pos = first_col + jnp.arange(CB, dtype=jnp.int32)
    key_pos = first_col - HALO + jnp.arange(EXT, dtype=jnp.int32)
    lowest = query_pos[None] - band_reach[:, 0]
    highest = query_pos[None] + band_reach[:, 1]
    key = key_pos[None, None]
    allowed = (key >= lowest[..., None]) & (key <= highest[..., None])
    allowed = allowed & (key >= 0) & (key < col_total)
    return allowed.astype(F32)


def layer(tokens, cot, counts, reach, mover, shard, gains):
    row_w, group, rims = mover.gather(shard, gains, tokens)
    from_low, from_high = rims
    present = (jnp.arange(ROWS, dtype=jnp.int32)[None] < counts[:, None]).astype(F32)
    row_scale = DH ** (-0.5) * lax.rsqrt(counts.astype(F32))
    scalars = (jnp.concatenate([row_scale[:, None], present], axis=1), mover.place)
    run = partial(run_kernel, scalars=scalars)
    low, wide = (SEQ_CB, LOW), (SEQ_EXT, LOW)
    row_gain = ((1, D), F32)
    probs = ((MB, PAIRS, 2 * CB, EXT), F32)
    col_probs = ((SEQ, ROWS * CB, LANES), F32)

    a1e, q, ke, ve, gain = run(
        row_project,
        args=(after(tokens, *mover.row_gate), from_low, from_high),
        weights=((row_w[0], group), row_w[1]),
        outs=like(wide, low, wide, wide, ((3, D), F32)),
        raw_out=(),
        scratch=[held(3)[0], VM((8, EXTRA, D), LOW), DMA((6,)), DMA((8,))],
        micros=9.5,
    )
    mover.gather_more(q)
    p1, o1, x1, a2 = run(
        row_attend,
        args=(tokens, after(q, *mover.attend_gate), ke, ve, band_mask(reach), gain),
        weights=row_w,
        outs=like(probs, low, (SEQ_CB, F32), low),
        raw_out=(),
        scratch=held(1),
        micros=12.5,
    )
    col_w, forward_w = mover.gather_last(a2)
    q2, k2, v2, p2, o2, x2, a3 = run(
        col_forward,
        args=(x1, a2, gain),
        weights=col_w,
        outs=like(low, low, low, col_probs, low, (SEQ_CB, F32), low),
        raw_out=(),
        scratch=held(4),
        micros=15.5,
    )
    token = (TOK, D)
    out, e2, dg3, *forward_g = run(
        feed_forward,
        args=(x2, a3, cot, gain),
        weights=forward_w,
        outs=like(low, (SEQ_CB, F32), row_gain, *pieces(2)),
        raw_out=range(3, 9),
        scratch=[VM(token, F32)] * 2 + [VM(token, LOW)] * 3 + [held(8)[0], terms(8)[0]]
        + [DMA((16,))] * 2,
        micros=26,
    )
    gate = mover.reduce_forward(*forward_g)
    dq2, dk2, dv2 = run(
        col_attend_back,
        args=(after(e2, *gate), q2, k2, v2, p2),
        weights=col_w,
        outs=like(low, low, low),
        raw_out=(),
        scratch=[VM(SEQ_CB, LOW)] + [VM(SEQ_CB, F32)] * 2 + held(1),
        micros=10.5,
    )
    gate = mover.reduce_forward_sides(dq2)
    dq2 = after(dq2, *gate)
    e1, dg2, *col_g = run(
        col_project_back,
        args=(e2, o2, dq2, dk2, dv2, a2, x1, gain),
        weights=col_w,
        outs=like((SEQ_CB, F32), row_gain, *pieces(1)),
        raw_out=range(2, 8),
        scratch=[VM(SEQ_CB, F32), held(3)[0], terms(4)[0], DMA((6,)), DMA((8,))],
        micros=11.5,
    )
    gate = mover.reduce_col(*col_g)
    dq, dke, dve, *row_g = run(
        row_backward,
        args=(after(e1, *gate), o1, q, ke, ve, p1, a1e),
        weights=row_w,
        outs=like(low, wide, wide, *pieces(1)),
        raw_out=range(3, 9),
        scratch=[VM(SEQ_CB, LOW)] + [held(1)[0], terms(4)[0], DMA((2,)), DMA((8,))],
        micros=20,
    )
    gate = mover.reduce_row(dq, *row_g)
    inner, to_low, to_high, dg1 = run(
        input_project,
        args=(after(dq, *gate), dke, dve, tokens, from_low, from_high),
        weights=row_w,
        outs=like((SEQ_CB, F32), (RIM, LOW), (RIM, LOW), row_gain),
        raw_out=(),
        scratch=[VM(SEQ_EXT, F32)] + held(3),
        micros=8,
    )
    gains = jnp.concatenate([dg1, dg2, dg3], axis=0)
    mover.reduce_last(gains)
    to_high, to_low, *_ = together(to_high, to_low, *mover.rim_gate)
    from_low, from_high = neighbours(to_high, to_low)
    (grad,) = run_kernel(
        input_finish,
        (),
        (after(inner, *mover.last_gate), from_low, from_high, e1, tokens, gain),
        None,
        like(low),
        (),
        (),
        3,
    )
    weight_grad, grad, gains = mover.total(grad)
    return out, grad, weight_grad, gains


def per_device(
    alignment,
    cotangent,
    row_counts,
    band_reach,
    master_weights,
    weight_moment,
    weight_square,
    norm_gains,
    gain_moment,
    gain_square,
):
    staged = lax.axis_size("cols") == NMAT and lax.axis_size("fsdp") == 2
    mover = Staged() if staged else Native()
    out, grad, weight_total, gain_grad = layer(
        alignment.reshape(SEQ, CB, D),
        cotangent.reshape(SEQ, CB, D),
        row_counts[:, 0],
        band_reach[:, 0],
        mover,
        master_weights.astype(LOW),
        norm_gains.astype(LOW),
    )
    gain_total = mover.own_gains(gain_grad, norm_gains.shape[0])
    new_weights, new_moment, new_square = adamw(
        master_weights,
        weight_moment,
        weight_square,
        weight_total.reshape(master_weights.shape),
        D ** (-0.5),
        DECAY,
        STEP_NUMBER,
    )
    new_gains, new_gain_moment, new_gain_square = adamw(
        norm_gains, gain_moment, gain_square, gain_total, RATE_GAIN, 0.0, STEP_NUMBER
    )
    shape = (MB, 1, ROWS, CB, D)
    return (
        out.reshape(shape),
        grad.reshape(shape),
        new_weights,
        new_moment,
        new_square,
        new_weights.astype(LOW),
        new_gains,
        new_gain_moment,
        new_gain_square,
    )


def solution(mesh):
    tokens = P(None, "fsdp", None, "cols", None)
    rows = P(("cols", "fsdp"), None)
    flat = P(("cols", "fsdp"))
    in_specs = (
        tokens,
        tokens,
        P(None, "fsdp"),
        P(None, "fsdp", None, "cols"),
        rows,
        rows,
        rows,
        flat,
        flat,
        flat,
    )
    out_specs = (tokens, tokens, rows, rows, rows, rows, flat, flat, flat)
    return jax.shard_map(
        per_device, mesh=mesh, in_specs=in_specs, out_specs=out_specs, check_vma=False
    )
```

```python
from functools import partial

import jax
import jax.numpy as jnp
from jax import lax
from jax.experimental import pallas as pl
from jax.experimental.pallas import tpu as pltpu
from jax.sharding import PartitionSpec as P

D = 768
H = 12
DH = 64
FF = 3072
NMAT = 16
ROWS = 4
CB = 64
HALO = 32
MB = 2
EXT = CB + 2 * HALO
SEQ = MB * ROWS
TOK = SEQ * CB
PAIRS = H // 2
LANES = 128
FOLD = FF // D
SPAN = D // 2
PART = SPAN // 2
EXTRA = 16
PER_GROUP = 10

EPS = 1e-05
BETA_ONE = 0.9
BETA_TWO = 0.999
ADAM_EPS = 1e-08
DECAY = 0.01
RATE_GAIN = 0.3
STEP_NUMBER = 10.0
MASKED = -1e30
F32 = jnp.float32
LOW = jnp.bfloat16


def dot_nn(a, b):
    return lax.dot_general(a, b, (((1,), (0,)), ((), ())), preferred_element_type=F32)


def dot_nt(a, b):
    return lax.dot_general(a, b, (((1,), (1,)), ((), ())), preferred_element_type=F32)


def dot_tn(a, b):
    return lax.dot_general(a, b, (((0,), (0,)), ((), ())), preferred_element_type=F32)


def standardize(values):
    center = values - jnp.mean(values, axis=-1, keepdims=True)
    spread = lax.rsqrt(jnp.mean(center * center, axis=-1, keepdims=True) + EPS)
    return center * spread, spread


def norm_pull(upward, values, gain):
    scaled, spread = standardize(values)
    weighted = upward * gain
    result = spread * (
        weighted
        - jnp.mean(weighted, axis=-1, keepdims=True)
        - scaled * jnp.mean(weighted * scaled, axis=-1, keepdims=True)
    )
    return result, jnp.sum(upward * scaled, axis=0, keepdims=True)


def lane_window(pair):
    return pl.ds(pl.multiple_of(pair * LANES, LANES), LANES)


def side_by_side(ref, micro, window):
    return jnp.concatenate([ref[micro * ROWS + r, :, window] for r in range(ROWS)], axis=1)


def head_stack(packed):
    lane = lax.broadcasted_iota(jnp.int32, packed.shape, 1)
    first = (lane % LANES) < DH
    zero = jnp.zeros_like(packed)
    return jnp.concatenate([jnp.where(first, packed, zero), jnp.where(first, zero, packed)], axis=0)


def head_merge(stacked, r):
    block = stacked[:, r * LANES : (r + 1) * LANES]
    lane = lax.broadcasted_iota(jnp.int32, (CB, LANES), 1)
    return jnp.where(lane < DH, block[:CB], block[CB:])


def head_sums():
    feature = lax.broadcasted_iota(jnp.int32, (D, LANES), 0)
    head = lax.broadcasted_iota(jnp.int32, (D, LANES), 1)
    return (feature // DH == head).astype(F32).astype(LOW)


def head_spread():
    head = lax.broadcasted_iota(jnp.int32, (LANES, D), 0)
    feature = lax.broadcasted_iota(jnp.int32, (LANES, D), 1)
    return (feature // DH == head).astype(F32).astype(LOW)


FULL = SPAN + EXTRA
STARTS = (0, FULL, 2 * FULL, 3 * FULL, 3 * FULL + PART)


def spot(buffers, number, row):
    if len(buffers) == 5:
        return buffers[number], row
    start = STARTS[number]
    if len(buffers) == 2 and number >= 3:
        return buffers[1], start - 3 * FULL + row
    return buffers[0], start + row


def regroup(sizes, refs):
    groups, start = [], 0
    for size in sizes:
        groups.append(refs[start : start + size])
        start += size
    return groups


def fetch_matrix(place, sources, table, matrix, target, sems, base):
    y_rel = jnp.where(place[1] == matrix // 2, 0, 1)
    waits = []
    for x in range(2):
        x_rel = jnp.where(place[0] == x, 0, 1)
        block = 2 * y_rel + x_rel
        sem = sems.at[base + x]
        for index in sorted(set(table)):
            here = None
            for plane, chosen in enumerate(table):
                if chosen == index:
                    hit = place[3] == plane
                    here = hit if here is None else jnp.logical_or(here, hit)
            for core_rel in range(2):
                held = jnp.logical_and(here, place[2] == (matrix % 2) ^ core_rel)
                buffers = sources[2 * index + core_rel]
                for number in range(5):
                    source, row = spot(buffers, number, 0)
                    size = SPAN if number < 3 else PART
                    to = x * SPAN + (PART if number == 4 else 0)
                    part = pltpu.make_async_copy(
                        source.at[pl.ds(row, size)], target.at[pl.ds(to, size)], sem
                    )
                    pl.when(jnp.logical_and(held, block == min(number, 3)))(part.start)
                    if number == 0:
                        copy = part
        waits.append(copy)
    return waits


def fetch(place, sources, table, matrices, w, sems, first=0):
    waits = []
    for slot, matrix in enumerate(matrices):
        slot += first
        waits.append(
            fetch_matrix(place, sources, table, matrix, w.at[slot], sems, 2 * slot)
        )
    return waits


def settle(waits):
    for copy in waits:
        copy.wait()


def emit_matrix(place, source, matrix, n, out, sems, base):
    *keep, rest, corner = out
    core_same = place[2] == matrix % 2
    y_rel = jnp.where(place[1] == matrix // 2, 0, 1)
    waits = []
    for x in range(2):
        x_rel = jnp.where(place[0] == x, 0, 1)
        spot_rel = 2 * y_rel + x_rel
        block = source.at[pl.ds(x * SPAN, SPAN)]
        sem = sems.at[base + x]
        sent = jnp.logical_not(core_same)
        for number, target in enumerate(keep):
            kept = pltpu.make_async_copy(block, target.at[n], sem)
            pl.when(jnp.logical_and(core_same, spot_rel == number))(kept.start)
        near = pltpu.make_async_copy(block, rest.at[jnp.minimum(spot_rel, 2), n], sem)
        far = pltpu.make_async_copy(block, corner.at[n], sem)
        pl.when(jnp.logical_and(sent, spot_rel < 3))(near.start)
        pl.when(jnp.logical_and(sent, spot_rel == 3))(far.start)
        waits.append(far)
    return waits


def gain_copies(sources, group, target, sem):
    copies = []
    for core_rel in range(2):
        buffers = sources[2 * group + core_rel]
        for number, row in ((0, SPAN), (1, SPAN), (2, SPAN), (4, PART)):
            source, row = spot(buffers, number, row)
            copy = pltpu.make_async_copy(
                source.at[pl.ds(row, EXTRA)], target.at[len(copies)], sem.at[len(copies)]
            )
            copies.append(copy)
    return copies


def row_project(
    spec, count, scal, place, tokens, from_low, from_high, *refs
):
    table, group = spec
    sources, (a1e, q, ke, ve, gain, w, held, sems, gain_sems) = regroup(count, refs), refs[sum(count) :]
    parts = gain_copies(sources, group, held, gain_sems)
    for copy in parts:
        copy.start()
    copies = fetch(place, sources, table, range(3), w, sems)
    settle(parts)
    total = held[0].astype(F32)
    for k in range(1, 8):
        total = total + held[k].astype(F32)
    gain[...] = total[:3]

    def norm_step(i, _):
        for source, start, size in (
            (from_low, 0, HALO),
            (tokens, HALO, CB),
            (from_high, HALO + CB, HALO),
        ):
            scaled, _s = standardize(source[i].astype(F32))
            a1e[i, start : start + size] = (scaled * gain[0:1]).astype(LOW)
        return 0

    lax.fori_loop(0, SEQ, norm_step, 0, unroll=True)
    wide = a1e[...].reshape(SEQ * EXT, D)
    settle(copies[1])
    ke[...] = dot_nn(wide, w[1]).astype(LOW).reshape(SEQ, EXT, D)
    settle(copies[2])
    ve[...] = dot_nn(wide, w[2]).astype(LOW).reshape(SEQ, EXT, D)
    inner = a1e[:, HALO : HALO + CB, :].reshape(TOK, D)
    settle(copies[0])
    q[...] = dot_nn(inner, w[0]).astype(LOW).reshape(SEQ, CB, D)
    for i in range(SEQ):
        q[i] = (q[i].astype(F32) * scal[i // ROWS, 1 + i % ROWS]).astype(LOW)


def row_attend(
    table, count, scal, place, tokens, q, ke, ve, allowed, gain, *refs
):
    sources, (p1, o1, x1, a2, w, sems) = regroup(count, refs), refs[sum(count) :]
    copies = fetch(place, sources, table, (3,), w, sems)

    def attend(pair, _):
        window = lane_window(pair)
        for m in range(MB):
            query = head_stack(side_by_side(q, m, window))
            scores = dot_nt(query, side_by_side(ke, m, window)) * scal[m, 0]
            mask = allowed[m]
            mask = jnp.concatenate([mask, mask], axis=0)
            scores = jnp.where(mask > 0, scores, MASKED)
            weight = jnp.exp(scores - jnp.max(scores, axis=-1, keepdims=True))
            prob = weight / jnp.sum(weight, axis=-1, keepdims=True)
            p1[m, pair] = prob
            mixed = dot_nn(prob.astype(LOW), side_by_side(ve, m, window))
            for r in range(ROWS):
                o1[m * ROWS + r, :, window] = head_merge(mixed, r).astype(LOW)
        return 0

    lax.fori_loop(0, PAIRS, attend, 0, unroll=True)
    settle(copies[0])
    x1[...] = tokens[...].astype(F32) + dot_nn(o1[...].reshape(TOK, D), w[0]).reshape(SEQ, CB, D)

    def next_norm(i, _):
        scaled, _s = standardize(x1[i])
        a2[i] = (scaled * gain[1:2]).astype(LOW)
        return 0

    lax.fori_loop(0, SEQ, next_norm, 0, unroll=True)


def col_forward(table, count, scal, place, x1, a2, gain, *refs):
    sources, (q2, k2, v2, p2, o2, x2, a3, w, sems) = regroup(count, refs), refs[sum(count) :]
    copies = fetch(place, sources, table, range(4), w, sems)
    for j in range(3):
        settle(copies[j])
    flat = a2[...].reshape(TOK, D)
    q2[...] = dot_nn(flat, w[0]).astype(LOW).reshape(SEQ, CB, D)
    k2[...] = dot_nn(flat, w[1]).astype(LOW).reshape(SEQ, CB, D)
    v2[...] = dot_nn(flat, w[2]).astype(LOW).reshape(SEQ, CB, D)
    sums = head_sums()
    spread = head_spread()

    def attend(i, _):
        micro = i // ROWS
        query = q2[i].astype(F32)
        products = jnp.concatenate(
            [(query * k2[micro * ROWS + s].astype(F32)).astype(LOW) for s in range(ROWS)], axis=0
        )
        scores = dot_nn(products, sums) * (DH ** (-0.5))
        parts = [
            jnp.where(scal[micro, 1 + s] > 0, scores[s * CB : (s + 1) * CB], MASKED)
            for s in range(ROWS)
        ]
        top = jnp.maximum(jnp.maximum(parts[0], parts[1]), jnp.maximum(parts[2], parts[3]))
        parts = [jnp.exp(part - top) for part in parts]
        scale = 1.0 / (parts[0] + parts[1] + parts[2] + parts[3])
        prob = jnp.concatenate([part * scale for part in parts], axis=0)
        p2[i] = prob
        wide = dot_nn(prob.astype(LOW), spread)
        total = wide[:CB] * v2[micro * ROWS].astype(F32)
        for s in range(1, ROWS):
            total = total + wide[s * CB : (s + 1) * CB] * v2[micro * ROWS + s].astype(F32)
        o2[i] = total.astype(LOW)
        return 0

    lax.fori_loop(0, SEQ, attend, 0, unroll=True)
    settle(copies[3])
    x2[...] = x1[...] + dot_nn(o2[...].reshape(TOK, D), w[3]).reshape(SEQ, CB, D)

    def next_norm(i, _):
        scaled, _s = standardize(x2[i])
        a3[i] = (scaled * gain[2:3]).astype(LOW)
        return 0

    lax.fori_loop(0, SEQ, next_norm, 0, unroll=True)


CHUNK = 256


def feed_forward(tables, count, scal, place, x2, a3, cot, gain, *refs):
    sources, refs = regroup(count, refs), refs[sum(count) :]
    out, e2, dgain, *terms_out, up, down, live_cot, gl, dhd, w, dw, in_sems, out_sems = refs
    copies = []
    for n in range(2):
        copies += fetch(place, sources, tables[n], range(4), w, in_sems, 4 * n)
    for i in range(SEQ):
        live_cot[i * CB : (i + 1) * CB] = (
            cot[i].astype(F32) * scal[i // ROWS, 1 + i % ROWS]
        ).astype(LOW)
    normed = a3[...].reshape(TOK, D)
    grad = live_cot[...]
    waits = []
    for step in range(FOLD):
        settle(copies[step])
        settle(copies[FOLD + step])
        win = w[step]
        wout = w[FOLD + step]
        for base in range(0, TOK, CHUNK):
            rows = slice(base, base + CHUNK)
            hidden = dot_nn(normed[rows], win)
            pulled = dot_nt(grad[rows], wout)
            half = 0.5 * lax.erf(hidden * (0.5**0.5)) + 0.5
            gl[rows] = (hidden * half).astype(LOW)
            slope = half + hidden * (jnp.exp(-0.5 * hidden * hidden) * ((2.0 * jnp.pi) ** -0.5))
            dhd[rows] = (pulled * slope).astype(LOW)
        for n, value in enumerate((dot_tn(normed, dhd[...]), dot_tn(gl[...], grad))):
            slot = 4 * n + step
            dw[slot] = value.astype(LOW)
            waits += emit_matrix(place, dw.at[slot], step, n, terms_out, out_sems, 2 * slot)
        forward = dot_nn(gl[...], wout)
        backward = dot_nt(dhd[...], win)
        if step == 0:
            up[...] = forward
            down[...] = backward
        else:
            up[...] += forward
            down[...] += backward
    total = jnp.zeros((1, D), F32)
    for i in range(SEQ):
        rows = slice(i * CB, (i + 1) * CB)
        value = x2[i]
        out[i] = ((value + up[rows]) * scal[i // ROWS, 1 + i % ROWS]).astype(LOW)
        part, gain_part = norm_pull(down[rows], value, gain[2:3])
        e2[i] = live_cot[rows].astype(F32) + part
        total = total + gain_part
    dgain[...] = total
    settle(waits)


def col_attend_back(table, count, scal, place, e2, q2, k2, v2, p2, *refs):
    sources, refs = regroup(count, refs), refs[sum(count) :]
    dq2, dk2, dv2, do2, dka, dva, w, in_sems = refs
    copies = fetch(place, sources, table, (3,), w, in_sems)
    low = e2[...].reshape(TOK, D).astype(LOW)
    settle(copies[0])
    do2[...] = dot_nt(low, w[0]).astype(LOW).reshape(SEQ, CB, D)
    sums = head_sums()
    spread = head_spread()
    dka[...] = jnp.zeros_like(dka)
    dva[...] = jnp.zeros_like(dva)

    def pull(i, _):
        micro = i // ROWS
        upward = do2[i].astype(F32)
        products = jnp.concatenate(
            [(upward * v2[micro * ROWS + s].astype(F32)).astype(LOW) for s in range(ROWS)], axis=0
        )
        dprob = dot_nn(products, sums)
        prob = p2[i]
        mixed = prob * dprob
        inner = mixed[:CB] + mixed[CB : 2 * CB] + mixed[2 * CB : 3 * CB] + mixed[3 * CB :]
        dscore = prob * (dprob - jnp.concatenate([inner] * ROWS, axis=0))
        wide = dot_nn(prob.astype(LOW), spread)
        dwide = dot_nn(dscore.astype(LOW), spread)
        query = q2[i].astype(F32)
        total = jnp.zeros((CB, D), F32)
        for s in range(ROWS):
            rows = slice(s * CB, (s + 1) * CB)
            total = total + dwide[rows] * k2[micro * ROWS + s].astype(F32)
            dka[micro * ROWS + s] += dwide[rows] * query
            dva[micro * ROWS + s] += wide[rows] * upward
        dq2[i] = (total * (DH ** (-0.5))).astype(LOW)
        return 0

    lax.fori_loop(0, SEQ, pull, 0, unroll=True)
    dk2[...] = (dka[...] * (DH ** (-0.5))).astype(LOW)
    dv2[...] = dva[...].astype(LOW)


def col_project_back(table, count, scal, place, e2, o2, dq2, dk2, dv2, a2, x1, gain, *refs):
    sources, refs = regroup(count, refs), refs[sum(count) :]
    e1, dgain, *terms_out, acc, w, dw, in_sems, out_sems = refs
    copies = fetch(place, sources, table, range(3), w, in_sems)
    flat = a2[...].reshape(TOK, D)
    low = e2[...].reshape(TOK, D).astype(LOW)
    dw[3] = dot_tn(o2[...].reshape(TOK, D), low).astype(LOW)
    waits = emit_matrix(place, dw.at[3], 3, 0, terms_out, out_sems, 6)
    for j, ref in enumerate((dq2, dk2, dv2)):
        grads = ref[...].reshape(TOK, D)
        dw[j] = dot_tn(flat, grads).astype(LOW)
        waits += emit_matrix(place, dw.at[j], j, 0, terms_out, out_sems, 2 * j)
        settle(copies[j])
        part = dot_nt(grads, w[j]).reshape(SEQ, CB, D)
        if j == 0:
            acc[...] = part
        else:
            acc[...] += part
    gain_total = jnp.zeros((1, D), F32)
    for i in range(SEQ):
        part, gain_part = norm_pull(acc[i], x1[i], gain[1:2])
        e1[i] = e2[i] + part
        gain_total = gain_total + gain_part
    dgain[...] = gain_total
    settle(waits)


def row_backward(table, count, scal, place, e1, o1, q, ke, ve, p1, a1e, *refs):
    sources, refs = regroup(count, refs), refs[sum(count) :]
    dq, dke, dve, *terms_out, do1, w, dw, in_sems, out_sems = refs
    copies = fetch(place, sources, table, (3,), w, in_sems)
    low = e1[...].reshape(TOK, D).astype(LOW)
    settle(copies[0])
    do1[...] = dot_nt(low, w[0]).astype(LOW).reshape(SEQ, CB, D)

    def pull(pair, _):
        window = lane_window(pair)
        for m in range(MB):
            query = head_stack(side_by_side(q, m, window))
            upward = head_stack(side_by_side(do1, m, window))
            prob = p1[m, pair]
            dprob = dot_nt(upward, side_by_side(ve, m, window))
            dscore = prob * (dprob - jnp.sum(prob * dprob, axis=-1, keepdims=True))
            dscore = dscore.astype(LOW)
            dvalue = dot_tn(prob.astype(LOW), upward)
            dkey = dot_tn(dscore, query) * scal[m, 0]
            dquery = dot_nn(dscore, side_by_side(ke, m, window)) * scal[m, 0]
            for r in range(ROWS):
                lanes = slice(r * LANES, (r + 1) * LANES)
                dve[m * ROWS + r, :, window] = dvalue[:, lanes].astype(LOW)
                dke[m * ROWS + r, :, window] = dkey[:, lanes].astype(LOW)
                dq[m * ROWS + r, :, window] = (head_merge(dquery, r) * scal[m, 1 + r]).astype(LOW)
        return 0

    lax.fori_loop(0, PAIRS, pull, 0, unroll=True)
    wide = a1e[...].reshape(SEQ * EXT, D)
    own = a1e[:, HALO : HALO + CB, :].reshape(TOK, D)
    waits = []
    for j, (left, right) in enumerate(
        (
            (own, dq[...].reshape(TOK, D)),
            (wide, dke[...].reshape(SEQ * EXT, D)),
            (wide, dve[...].reshape(SEQ * EXT, D)),
            (o1[...].reshape(TOK, D), low),
        )
    ):
        dw[j] = dot_tn(left, right).astype(LOW)
        waits += emit_matrix(place, dw.at[j], j, 0, terms_out, out_sems, 2 * j)
    settle(waits)


def input_project(
    table, count, scal, place, dq, dke, dve, tokens, from_low, from_high, *refs
):
    sources, (inner, to_low, to_high, dgain, acc, w, sems) = regroup(count, refs), refs[sum(count) :]
    copies = fetch(place, sources, table, range(3), w, sems)
    settle(copies[1])
    acc[...] = dot_nt(dke[...].reshape(SEQ * EXT, D), w[1]).reshape(SEQ, EXT, D)
    settle(copies[2])
    acc[...] += dot_nt(dve[...].reshape(SEQ * EXT, D), w[2]).reshape(SEQ, EXT, D)
    settle(copies[0])
    acc[:, HALO : HALO + CB, :] += dot_nt(dq[...].reshape(TOK, D), w[0]).reshape(SEQ, CB, D)
    total = jnp.zeros((1, D), F32)
    for i in range(SEQ):
        for source, start, size in (
            (from_low, 0, HALO),
            (tokens, HALO, CB),
            (from_high, HALO + CB, HALO),
        ):
            scaled, _s = standardize(source[i].astype(F32))
            total = total + jnp.sum(acc[i, start : start + size] * scaled, axis=0, keepdims=True)
    dgain[...] = total
    inner[...] = acc[:, HALO : HALO + CB, :]
    to_low[...] = acc[:, :HALO, :].astype(LOW)
    to_high[...] = acc[:, HALO + CB :, :].astype(LOW)


def input_finish(inner, from_low, from_high, e1, tokens, gain, grad):
    def step(i, _):
        upward = jnp.concatenate(
            [
                inner[i, :HALO] + from_low[i].astype(F32),
                inner[i, HALO:] + from_high[i].astype(F32),
            ],
            axis=0,
        )
        part, _g = norm_pull(upward, tokens[i].astype(F32), gain[0:1])
        grad[i] = (e1[i] + part).astype(LOW)
        return 0

    lax.fori_loop(0, SEQ, step, 0, unroll=True)


def in_vmem(count):
    return [pl.BlockSpec(memory_space=pltpu.VMEM)] * count


def like(*shapes):
    return tuple(jax.ShapeDtypeStruct(shape, dtype) for shape, dtype in shapes)


SEQ_CB = (SEQ, CB, D)
SEQ_EXT = (SEQ, EXT, D)
RIM = (SEQ, HALO, D)
PER_MICRO = 1.15e9
VM = pltpu.VMEM
DMA = pltpu.SemaphoreType.DMA


ROOM = {col_attend_back: 40, col_project_back: 40, row_backward: 40, input_project: 40, input_finish: 40}


def pieces(count):
    return (
        *(((count, SPAN, D), LOW),) * 4,
        ((3, count, SPAN, D), LOW),
        ((count, SPAN, D), LOW),
    )


def run_kernel(body, scalars, args, weights, outs, raw_out, scratch, micros):
    vmem = pl.BlockSpec(memory_space=pltpu.VMEM)
    raw = pl.BlockSpec(memory_space=pltpu.HBM)
    moved = sum(a.size * a.dtype.itemsize for a in args)
    moved += sum(o.size * jnp.dtype(o.dtype).itemsize for o in outs)
    call = body
    sources = ()
    if weights is not None:
        table, groups = weights
        sources = [buffer for group in groups for buffer in group]
        call = partial(body, table, tuple(len(group) for group in groups))
    return pl.pallas_call(
        call,
        name=body.__name__,
        out_shape=outs,
        in_specs=[pl.BlockSpec(memory_space=pltpu.SMEM)] * len(scalars)
        + [vmem] * len(args)
        + [raw] * len(sources),
        out_specs=tuple(raw if i in raw_out else vmem for i in range(len(outs))),
        scratch_shapes=scratch,
        compiler_params=pltpu.CompilerParams(vmem_limit_bytes=ROOM.get(body, 60) << 20),
        cost_estimate=pl.CostEstimate(
            flops=int(micros * PER_MICRO), bytes_accessed=moved, transcendentals=0
        ),
    )(*scalars, *args, *sources)


def held(count):
    return [VM((count, D, D), LOW), DMA((2 * count,))]


def terms(count):
    return [VM((count, D, D), LOW), DMA((2 * count,))]


def corner_terms(keep, got, half_a, half_b):
    total = keep[...].astype(F32) + got[...].astype(F32)
    half_a[...] = total[:, :PART].astype(LOW)
    half_b[...] = total[:, PART:].astype(LOW)


def side_terms(keep_x, got_x, keep_y, got_y, half_a, half_b, *outs):
    count = len(outs) // 2
    for n in range(count):
        over_x, over_y = outs[n], outs[count + n]
        total = keep_x[n].astype(F32) + got_x[0, n].astype(F32)
        over_x[0, :PART] = (total[:PART] + half_a[n].astype(F32)).astype(LOW)
        over_x[0, PART:] = total[PART:].astype(LOW)
        total = keep_y[n].astype(F32) + got_y[0, n].astype(F32)
        over_y[0, :PART] = total[:PART].astype(LOW)
        over_y[0, PART:] = (total[PART:] + half_b[n].astype(F32)).astype(LOW)


def own_terms(keep, got, from_x, from_y, total, low):
    value = keep[0].astype(F32) + got[0, 0].astype(F32)
    value = value + from_x[0].astype(F32) + from_y[0].astype(F32)
    total[0] = value
    low[0] = value.astype(LOW)


SPLIT = 2


def call_small(body, args, picks, shapes):
    count = args[0].shape[0]
    width = D // SPLIT
    specs = []
    for arg, pick in zip(args, picks):
        if pick is None:
            specs.append(pl.BlockSpec((*arg.shape[:-1], width), lambda j: (0, 0, j)))
        elif isinstance(pick, tuple) and pick[0] == "keep":
            specs.append(pl.BlockSpec((1, SPAN, width), lambda j, k=pick[1]: (k, 0, j)))
        elif isinstance(pick, tuple):
            specs.append(
                pl.BlockSpec((1, 1, SPAN, width), lambda j, k=pick[1]: (0, k, 0, j))
            )
        elif isinstance(pick, int):
            specs.append(
                pl.BlockSpec((1, count, SPAN, width), lambda j, k=pick: (k, 0, 0, j))
            )
    moved = sum(s.block_shape[-2] * D * count * 2 for s in specs)
    return pl.pallas_call(
        body,
        name=body.__name__,
        grid=(SPLIT,),
        out_shape=tuple(
            jax.ShapeDtypeStruct((*shape, D), dtype) for shape, dtype in shapes
        ),
        in_specs=specs,
        out_specs=tuple(
            pl.BlockSpec((*shape, width), lambda j: (0, 0, j)) for shape, _d in shapes
        ),
        compiler_params=pltpu.CompilerParams(vmem_limit_bytes=16 << 20),
        cost_estimate=pl.CostEstimate(
            flops=int(8 * PER_MICRO), bytes_accessed=moved, transcendentals=0
        ),
    )(*args)


def swap_pairs(count, bit):
    return [(i, i ^ bit) for i in range(count)]


def after(value, *before):
    return lax.optimization_barrier((value, *before))[0]


def add(*parts):
    total = parts[0].astype(F32)
    for part in parts[1:]:
        total = total + part.astype(F32)
    return total


def together(*values):
    return lax.optimization_barrier(values)


class Staged:
    planes = 4
    tables = ((0, 1, 2, 2), (1, 0, 1, 3), (2, 2, 0, 1), (3, 3, 3, 0))

    def __init__(self):
        self.count = NMAT
        self.step = NMAT // self.planes
        cols = lax.axis_index("cols")
        self.z = cols // self.step
        self.place = jnp.stack(
            [lax.axis_index("fsdp"), (cols // 2) % 2, cols % 2, self.z]
        ).astype(jnp.int32)

    def over_x(self, value):
        return lax.ppermute(value, "fsdp", [(0, 1), (1, 0)])

    def over_y(self, value):
        return lax.ppermute(value, "cols", swap_pairs(self.count, 2))

    def over_core(self, value):
        return lax.ppermute(value, "cols", swap_pairs(self.count, 1))

    def over_z(self, value, pairs):
        step = self.step
        full = [(a * step + i, b * step + i) for a, b in pairs for i in range(step)]
        return lax.ppermute(value, "cols", full)

    def by_plane(self, options):
        result = options[-1]
        for index in range(len(options) - 2, -1, -1):
            result = jnp.where(self.z == index, options[index], result)
        return result

    def own_place(self, gains):
        index = lax.axis_index("cols") * 2 + lax.axis_index("fsdp")
        spread = jnp.zeros((EXTRA * D,), LOW)
        spread = lax.dynamic_update_slice(spread, gains, (index * gains.shape[0],))
        return spread.reshape(EXTRA, D)

    def sum_step(self, value, index):
        swaps = (
            self.over_core,
            self.over_x,
            self.over_y,
            lambda v: self.over_z(v, [(0, 1), (1, 0), (2, 3), (3, 2)]),
            lambda v: self.over_z(v, [(0, 2), (2, 0), (1, 3), (3, 1)]),
        )
        return value + swaps[index](value)

    def own_gains(self, value, size):
        value = value.reshape(3 * D)
        index = lax.axis_index("cols") * 2 + lax.axis_index("fsdp")
        return lax.dynamic_slice(value, (index * size,), (size,))

    def halves(self, from_x, from_y):
        return self.over_y(from_x[:PART]), self.over_x(from_y[PART:])

    def gather(self, shard, gains, tokens):
        core = self.over_core
        own1 = jnp.concatenate([shard, self.own_place(gains)], axis=0)
        up1 = self.over_z(own1, [(0, 1), (1, 2), (2, 3)])
        down1 = self.over_z(own1, [(3, 2), (2, 1), (1, 0)])
        x1, y1 = self.over_x(own1), self.over_y(own1)
        up1, down1, x1, y1 = together(up1, down1, x1, y1)
        own2 = jnp.where(self.z == 0, down1, up1)
        x2, y2 = self.over_x(own2), self.over_y(own2)
        a1, b1 = self.halves(x1, y1)
        up2 = self.over_z(up1, [(1, 2), (2, 3)])
        down2 = self.over_z(down1, [(2, 1), (1, 0)])
        rims = neighbours(*after((tokens[:, CB - HALO :], tokens[:, :HALO]), x1))
        c1 = [core(own1)]
        up2, down2, a1, b1, x2, y2, *rims = together(up2, down2, a1, b1, x2, y2, *rims)
        up3 = self.over_z(up2, [(2, 3)])
        down3 = self.over_z(down2, [(1, 0)])
        a2, b2 = self.halves(x2, y2)
        c1 += [core(x1), core(y1), core(a1), core(b1)]
        up3, down3, a2, b2, *c1 = together(up3, down3, a2, b2, *c1)
        own3 = self.by_plane([down2, down1, up2, up3])
        placed = [v[SPAN:] for v in (own1, up1, up2, up3, down1, down2, down3)]
        own3 = jnp.concatenate([own3[:SPAN], add(*placed).astype(LOW)], axis=0)
        x3, y3 = self.over_x(own3), self.over_y(own3)
        c2 = [core(v) for v in (own2, x2, y2, a2, b2)]
        x3, y3, *c2 = together(x3, y3, *c2)
        a3, b3 = self.halves(x3, y3)
        c3 = [core(own3), core(x3), core(y3)]
        own4 = self.by_plane([down3, down2, down1, up2])
        a3, b3, own4, *c3 = together(a3, b3, own4, *c3)
        x4, y4 = self.over_x(own4), self.over_y(own4)
        c3 += [core(a3), core(b3)]
        self.row_gate = (own4,)
        self.fourth = own4, x4, y4
        self.first = ((own1, x1, y1, a1, b1), tuple(c1), (own2, x2, y2, a2, b2), tuple(c2))
        self.first += ((own3, x3, y3, a3, b3), tuple(c3))
        return (self.tables[0], self.first), 2, rims

    def gather_more(self, seen):
        own4, x4, y4 = self.fourth
        x4, y4, seen = together(x4, y4, seen)
        xa, yb = x4[:PART], y4[PART:]
        self.attend_gate = (xa, yb)
        core = self.over_core
        self.fourth = own4, x4, y4, self.over_y(xa), self.over_x(yb)
        self.fourth_core = [core(own4), core(x4), core(y4)]

    def gather_last(self, seen):
        own4, x4, y4, a4, b4 = self.fourth
        a4, b4, _ = together(a4, b4, seen)
        core = self.over_core
        c4 = (*self.fourth_core, core(a4), core(b4))
        every = (*self.first, (own4, x4, y4, a4, b4), c4)
        return (self.tables[1], every), (self.tables[2:], every)

    def corner_swap(self, keep, got):
        shapes = (((keep[3].shape[0], PART), LOW),) * 2
        return call_small(corner_terms, (keep[3], got), (None, None), shapes)

    def side_blocks(self, keep, got, corner_a, corner_b):
        picks = (None, 1, None, 2, None, None)
        args = (keep[1], got, keep[2], got, corner_a, corner_b)
        count = keep[0].shape[0]
        sides = call_small(side_terms, args, picks, (((1, SPAN), LOW),) * (2 * count))
        return sides[:count], sides[count:]

    def own_sum(self, keep, got, from_x, from_y, n=0):
        shapes = (((1, SPAN), F32), ((1, SPAN), LOW))
        picks = (("keep", n), ("got", n), None, None)
        total, low = call_small(own_terms, (keep[0], got, from_x, from_y), picks, shapes)
        return total[0], low[0]

    def reduce_forward(self, *terms):
        *keep, rest, corner = terms
        corner = self.over_core(corner)
        a, b = self.corner_swap(keep, corner)
        self.fwd = keep, self.over_core(after(rest, a, b))
        self.fwd_corner = self.over_y(a), self.over_x(b)
        return a, b

    def reduce_forward_sides(self, seen):
        a, b, _ = together(*self.fwd_corner, seen)
        (x2, x3), (y2, y3) = self.side_blocks(*self.fwd, a, b)
        self.first_sides = self.over_x(x2), self.over_y(y2)
        self.later_sides = x3, y3
        return x2, y2, x3, y3

    def reduce_col(self, *terms):
        *keep, rest, corner = terms
        corner = self.over_core(corner)
        fx, fy = together(*self.first_sides)
        a, b = after(self.later_sides, fx, fy)
        self.later_sides = self.over_x(a), self.over_y(b)
        a, b = self.corner_swap(keep, after(corner, a, b))
        self.col = keep, self.over_core(after(rest, a, b))
        self.col_corner = self.over_y(a), self.over_x(b)
        fx, fy, *_ = together(fx, fy, a, b)
        self.second, low = self.own_sum(*self.fwd, fx, fy, 0)
        self.near_second = self.over_z(low, [(0, 1), (3, 2)])
        return a, b, low

    def reduce_row(self, seen, *terms):
        *keep, rest, corner = terms
        corner = self.over_core(corner)
        a, b, fx, fy, near, _ = together(
            *self.col_corner, *self.later_sides, self.near_second, seen
        )
        (cx,), (cy,) = self.side_blocks(*self.col, a, b)
        corner = after(corner, cx, cy)
        cx, cy = self.over_x(cx), self.over_y(cy)
        a, b = self.corner_swap(keep, corner)
        got = self.over_core(after(rest, a, b))
        fx, fy, near, *_ = together(fx, fy, near, a, b)
        a, b = self.over_y(a), self.over_x(b)
        self.third, low = self.own_sum(*self.fwd, fx, fy, 1)
        self.near_third = self.over_z(low, [(0, 1), (2, 3)])
        self.second = add(self.second, near)
        second_low = self.second.astype(LOW)
        self.far_second = self.over_z(second_low, [(1, 2)])
        a, b, cx, cy, got, *_ = together(a, b, cx, cy, got, low, second_low)
        (rx,), (ry,) = self.side_blocks(keep, got, a, b)
        cx, cy, *_ = together(cx, cy, rx, ry)
        self.row = keep, got
        self.row_sides = self.over_x(rx), self.over_y(ry)
        self.col_sum, low = self.own_sum(*self.col, cx, cy)
        self.near_col = self.over_z(low, [(0, 1), (3, 2)])
        return rx, ry, low

    def reduce_last(self, gains):
        rx, ry, near_col, near, far_second, gains = together(
            *self.row_sides, self.near_col, self.near_third, self.far_second, gains
        )
        row, low = self.own_sum(*self.row, rx, ry)
        near_row = self.over_z(low, [(1, 0), (3, 2)])
        self.rim_gate = (low,)
        near_col, near, gains, _ = together(near_col, near, gains, low)
        col = add(self.col_sum, near_col)
        far_col = self.over_z(col.astype(LOW), [(2, 1)])
        third = add(self.third, near)
        far_third = self.over_z(third.astype(LOW), [(1, 3)])
        gains = gains.reshape(18, LANES)
        for index in range(4):
            gains = self.sum_step(gains, index)
        near_row, far_col, far_third, gains = together(near_row, far_col, far_third, gains)
        row = add(row, near_row)
        low = row.astype(LOW)
        far_row = self.over_z(low, [(2, 0)])
        self.last_gate = (low,)
        self.gains = gains
        forward = jnp.where(
            self.z == 2, add(self.second, far_second), add(third, far_third)
        )
        self.totals = row, far_row, jnp.where(self.z == 1, add(col, far_col), forward)

    def total(self, seen):
        row, far_row, rest = self.totals
        far_row, rest, seen, gains = together(far_row, rest, seen, self.gains)
        result = jnp.where(self.z == 0, add(row, far_row), rest)
        return result, seen, self.sum_step(gains, 4)


class Native:
    axes = ("cols", "fsdp")
    rim_gate = ()
    last_gate = ()
    row_gate = ()
    attend_gate = ()

    def __init__(self):
        self.place = jnp.zeros((4,), jnp.int32)
        self.parts = []

    def gather(self, shard, gains, tokens):
        full = lax.all_gather(shard, self.axes, axis=0, tiled=True)
        gains = lax.all_gather(gains, self.axes, axis=0, tiled=True)
        rims = neighbours(tokens[:, CB - HALO :], tokens[:, :HALO])
        row, *self.rest = self.arranged(full, gains)
        return row, 0, rims

    def gather_more(self, seen):
        pass

    def gather_last(self, seen):
        return self.rest

    def arranged(self, full, gains):
        blocks = full.reshape(4, 2, 2, 2 * SPAN, D).transpose(0, 2, 1, 3, 4)
        blocks = blocks.reshape(4, 2, 4, SPAN, D)
        extra = jnp.pad(gains.reshape(3, D), ((0, EXTRA - 3), (0, 0)))
        groups = []
        for b in range(4):
            parts = []
            for c in range(2):
                for k in range(3):
                    mine = extra if b == c == k == 0 else jnp.zeros_like(extra)
                    parts.append(jnp.concatenate([blocks[b, c, k], mine], axis=0))
                last = jnp.concatenate([blocks[b, c, 3], jnp.zeros_like(extra)], axis=0)
                parts += [last[:PART], last[PART:]]
            groups.append((tuple(parts[:5]), tuple(parts[5:])))
        row, col, low, high = groups
        flat = (0, 0, 0, 0)
        return (flat, row), (flat, col), ((flat, (1, 1, 1, 1)), (*low, *high))

    def own_gains(self, value, size):
        value = value.reshape(3 * D)
        return lax.psum_scatter(value, self.axes, scatter_dimension=0, tiled=True)

    def stash(self, *terms):
        *keep, rest, corner = terms
        sent = jnp.concatenate([rest, corner[None]], axis=0)
        blocks = jnp.stack([jnp.stack(keep), sent])
        blocks = blocks.reshape(2, 2, 2, *corner.shape)
        self.parts.insert(0, blocks.transpose(3, 1, 0, 2, 4, 5))
        return ()

    def reduce_forward(self, *terms):
        return self.stash(*terms)

    def reduce_forward_sides(self, seen):
        return ()

    def reduce_col(self, *terms):
        return self.stash(*terms)

    def reduce_row(self, seen, *terms):
        return self.stash(*terms)

    def reduce_last(self, gains):
        self.gains = gains

    def total(self, seen):
        full = jnp.concatenate([self.parts[0], self.parts[1], self.parts[2]], axis=0)
        full = full.reshape(NMAT * D, D)
        full = lax.psum_scatter(full, self.axes, scatter_dimension=0, tiled=True)
        return full.astype(F32), seen, self.gains


def neighbours(upward, downward):
    count = lax.axis_size("cols")
    forward = [(i, i + 1) for i in range(count - 1)]
    backward = [(target, source) for source, target in forward]
    return lax.ppermute(upward, "cols", forward), lax.ppermute(downward, "cols", backward)


def adamw(master, moment, square, grad_total, rate, decay, steps_done):
    moment_new = BETA_ONE * moment + (1.0 - BETA_ONE) * grad_total
    square_new = BETA_TWO * square + (1.0 - BETA_TWO) * grad_total * grad_total
    moment_fix = 1.0 - BETA_ONE**steps_done
    square_fix = 1.0 - BETA_TWO**steps_done
    update = moment_new / moment_fix / (jnp.sqrt(square_new / square_fix) + ADAM_EPS)
    return (master - rate * (update + decay * master), moment_new, square_new)


def band_mask(band_reach):
    first_col = lax.axis_index("cols") * CB
    col_total = CB * lax.axis_size("cols")
    query_pos = first_col + jnp.arange(CB, dtype=jnp.int32)
    key_pos = first_col - HALO + jnp.arange(EXT, dtype=jnp.int32)
    lowest = query_pos[None] - band_reach[:, 0]
    highest = query_pos[None] + band_reach[:, 1]
    key = key_pos[None, None]
    allowed = (key >= lowest[..., None]) & (key <= highest[..., None])
    allowed = allowed & (key >= 0) & (key < col_total)
    return allowed.astype(F32)


def layer(tokens, cot, counts, reach, mover, shard, gains):
    row_w, group, rims = mover.gather(shard, gains, tokens)
    from_low, from_high = rims
    present = (jnp.arange(ROWS, dtype=jnp.int32)[None] < counts[:, None]).astype(F32)
    row_scale = DH ** (-0.5) * lax.rsqrt(counts.astype(F32))
    scalars = (jnp.concatenate([row_scale[:, None], present], axis=1), mover.place)
    run = partial(run_kernel, scalars=scalars)
    low, wide = (SEQ_CB, LOW), (SEQ_EXT, LOW)
    row_gain = ((1, D), F32)
    probs = ((MB, PAIRS, 2 * CB, EXT), F32)
    col_probs = ((SEQ, ROWS * CB, LANES), F32)

    a1e, q, ke, ve, gain = run(
        row_project,
        args=(after(tokens, *mover.row_gate), from_low, from_high),
        weights=((row_w[0], group), row_w[1]),
        outs=like(wide, low, wide, wide, ((3, D), F32)),
        raw_out=(),
        scratch=[held(3)[0], VM((8, EXTRA, D), LOW), DMA((6,)), DMA((8,))],
        micros=9.5,
    )
    mover.gather_more(q)
    p1, o1, x1, a2 = run(
        row_attend,
        args=(tokens, after(q, *mover.attend_gate), ke, ve, band_mask(reach), gain),
        weights=row_w,
        outs=like(probs, low, (SEQ_CB, F32), low),
        raw_out=(),
        scratch=held(1),
        micros=12.5,
    )
    col_w, forward_w = mover.gather_last(a2)
    q2, k2, v2, p2, o2, x2, a3 = run(
        col_forward,
        args=(x1, a2, gain),
        weights=col_w,
        outs=like(low, low, low, col_probs, low, (SEQ_CB, F32), low),
        raw_out=(),
        scratch=held(4),
        micros=15.5,
    )
    token = (TOK, D)
    out, e2, dg3, *forward_g = run(
        feed_forward,
        args=(x2, a3, cot, gain),
        weights=forward_w,
        outs=like(low, (SEQ_CB, F32), row_gain, *pieces(2)),
        raw_out=range(3, 9),
        scratch=[VM(token, F32)] * 2 + [VM(token, LOW)] * 3 + [held(8)[0], terms(8)[0]]
        + [DMA((16,))] * 2,
        micros=26,
    )
    gate = mover.reduce_forward(*forward_g)
    dq2, dk2, dv2 = run(
        col_attend_back,
        args=(after(e2, *gate), q2, k2, v2, p2),
        weights=col_w,
        outs=like(low, low, low),
        raw_out=(),
        scratch=[VM(SEQ_CB, LOW)] + [VM(SEQ_CB, F32)] * 2 + held(1),
        micros=10.5,
    )
    gate = mover.reduce_forward_sides(dq2)
    dq2 = after(dq2, *gate)
    e1, dg2, *col_g = run(
        col_project_back,
        args=(e2, o2, dq2, dk2, dv2, a2, x1, gain),
        weights=col_w,
        outs=like((SEQ_CB, F32), row_gain, *pieces(1)),
        raw_out=range(2, 8),
        scratch=[VM(SEQ_CB, F32), held(3)[0], terms(4)[0], DMA((6,)), DMA((8,))],
        micros=11.5,
    )
    gate = mover.reduce_col(*col_g)
    dq, dke, dve, *row_g = run(
        row_backward,
        args=(after(e1, *gate), o1, q, ke, ve, p1, a1e),
        weights=row_w,
        outs=like(low, wide, wide, *pieces(1)),
        raw_out=range(3, 9),
        scratch=[VM(SEQ_CB, LOW)] + [held(1)[0], terms(4)[0], DMA((2,)), DMA((8,))],
        micros=20,
    )
    gate = mover.reduce_row(dq, *row_g)
    inner, to_low, to_high, dg1 = run(
        input_project,
        args=(after(dq, *gate), dke, dve, tokens, from_low, from_high),
        weights=row_w,
        outs=like((SEQ_CB, F32), (RIM, LOW), (RIM, LOW), row_gain),
        raw_out=(),
        scratch=[VM(SEQ_EXT, F32)] + held(3),
        micros=8,
    )
    gains = jnp.concatenate([dg1, dg2, dg3], axis=0)
    mover.reduce_last(gains)
    to_high, to_low, *_ = together(to_high, to_low, *mover.rim_gate)
    from_low, from_high = neighbours(to_high, to_low)
    (grad,) = run_kernel(
        input_finish,
        (),
        (after(inner, *mover.last_gate), from_low, from_high, e1, tokens, gain),
        None,
        like(low),
        (),
        (),
        3,
    )
    weight_grad, grad, gains = mover.total(grad)
    return out, grad, weight_grad, gains


def per_device(
    alignment,
    cotangent,
    row_counts,
    band_reach,
    master_weights,
    weight_moment,
    weight_square,
    norm_gains,
    gain_moment,
    gain_square,
):
    staged = lax.axis_size("cols") == NMAT and lax.axis_size("fsdp") == 2
    mover = Staged() if staged else Native()
    out, grad, weight_total, gain_grad = layer(
        alignment.reshape(SEQ, CB, D),
        cotangent.reshape(SEQ, CB, D),
        row_counts[:, 0],
        band_reach[:, 0],
        mover,
        master_weights.astype(LOW),
        norm_gains.astype(LOW),
    )
    gain_total = mover.own_gains(gain_grad, norm_gains.shape[0])
    new_weights, new_moment, new_square = adamw(
        master_weights,
        weight_moment,
        weight_square,
        weight_total.reshape(master_weights.shape),
        D ** (-0.5),
        DECAY,
        STEP_NUMBER,
    )
    new_gains, new_gain_moment, new_gain_square = adamw(
        norm_gains, gain_moment, gain_square, gain_total, RATE_GAIN, 0.0, STEP_NUMBER
    )
    shape = (MB, 1, ROWS, CB, D)
    return (
        out.reshape(shape),
        grad.reshape(shape),
        new_weights,
        new_moment,
        new_square,
        new_weights.astype(LOW),
        new_gains,
        new_gain_moment,
        new_gain_square,
    )


def solution(mesh):
    tokens = P(None, "fsdp", None, "cols", None)
    rows = P(("cols", "fsdp"), None)
    flat = P(("cols", "fsdp"))
    in_specs = (
        tokens,
        tokens,
        P(None, "fsdp"),
        P(None, "fsdp", None, "cols"),
        rows,
        rows,
        rows,
        flat,
        flat,
        flat,
    )
    out_specs = (tokens, tokens, rows, rows, rows, rows, flat, flat, flat)
    return jax.shard_map(
        per_device, mesh=mesh, in_specs=in_specs, out_specs=out_specs, check_vma=False
    )
```
